32 devices in a mesh: var: 2 (over y), gx: 4 (over z), gy: 2 (over x), nd: 2 (over core).
Axes of the slice: x: 2, y: 2, z: 4, core: 2. Of those that a mesh axis runs over, the one named last changes fastest.
Arguments:
- right_side: float32 [8192, 256], P(('var', 'gx', 'gy', 'nd')), parts along dimension 0, may hold values from -8 to 8
- node_diag: float32 [8192], P(('var', 'gx', 'gy', 'nd')), parts along dimension 0, may hold values from 1 to 10
- local_coup: float32 [64, 7, 128, 128], P(('var', 'gx', 'gy', 'nd')), parts along dimension 0, may hold values from -0.01 to 0.01
- block_cols: int32 [32, 7], P(('gx', 'gy', 'nd')), may hold values from 0 to 3
- border_coup: float32 [32, 8, 128, 128], P(('var', 'gx', 'gy', 'nd')), parts along dimension 0, may hold values from -0.01 to 0.01
- border_send: int32 [16, 8], P(('gx', 'gy', 'nd')), may hold values from 0 to 1
- border_rows: int32 [16, 8], P(('gx', 'gy', 'nd')), may hold values from 0 to 1
Outputs:
- solution_field: float32 [8192, 256], P(('var', 'gx', 'gy', 'nd')), parts along dimension 0
The draws below stay inside these ranges and needn't reach their ends.
There are 2 independent parts, one for each index of `var`. The reference program is written for one: setup_inputs(seed, part) draws one part's arguments, and reference() takes and returns one part's arrays. A program takes and returns all parts, laid end to end along the dimension named above; an argument that names none is the same for every part. Nothing has to cross between parts.
Inputs may be any that keep to these rules, and one draw needn't show every extreme that they name: `block_cols`: block numbers within a patch. `border_send`: block numbers within the sending device. `border_rows`: block numbers within the receiving device.
All inputs are finite; a program needn't handle non-finite values.
Results may differ from the reference program's by a relative error of at most 0.0003.
Values sent between devices are 32-bit elements; how exact they have to be, the bound alone decides.
No kernel may reach another device: no remote copies, remote signals or barrier semaphores. Data moves between devices by JAX's collectives and lax.ppermute only.
A program may use at most 64 MiB of HBM per device.

```python
import math
import jax
import jax.numpy as jnp
from jax import lax

BS = 128
COLS = 256
NB = 2
NNZ = 7
BB = 2
ITERS = 2
DEVS = 16
PATCH = 4
NBLK = 32
NODES = 4096
N_GX = 4
N_GY = 2
N_ND = 2


def set_ends(drawn, stream_key, low, high):
    longest = drawn.shape.index(max(drawn.shape))
    spots = []
    for shift in (0, 1):
        where = [jax.random.randint(jax.random.fold_in(stream_key, axis), (), 0, length) for axis, length in enumerate(drawn.shape)]
        where[longest] = (where[longest] + shift) % drawn.shape[longest]
        spots.append(tuple(where))
    return drawn.at[spots[0]].set(low).at[spots[1]].set(high)


def block_levels(stream_key, shape, split, low, high):
    def one(axis_at, blocks):
        draws = jax.random.uniform(jax.random.fold_in(jax.random.fold_in(stream_key, 6), axis_at), (blocks,), jnp.float32, low / len(split), high / len(split))
        return jnp.repeat(jnp.exp(draws), shape[axis_at] // blocks).reshape((-1,) + (1,) * (len(shape) - axis_at - 1))

    level = one(*split[0])
    for cut in split[1:]:
        level = level * one(*cut)
    return level


def centred(rng, dims, spread, limit, shards=(), kind=jnp.bfloat16):
    drawn = jax.random.normal(rng, dims, jnp.float32) * spread
    if len(shards) > 0:
        drawn = block_levels(rng, dims, shards, -0.22, 0.18) * drawn
    return jnp.clip(drawn, min=-limit, max=limit).astype(kind)


def setup_inputs(seed: int = 0, part: int = 0) -> dict:
    splits = jax.random.split(jax.random.key(seed), 8)
    part_keys = jax.random.split(jax.random.fold_in(splits[7], part), 8)
    return {
        "right_side": centred(part_keys[0], (NODES, COLS), 1.0, 8.0, ((0, 16),), jnp.float32),
        "node_diag": jnp.clip(jnp.exp(math.log(10.0) - 2.3025851 * jax.random.uniform(part_keys[1], (NODES,), jnp.float32) ** block_levels(part_keys[1], (NODES,), ((0, 16),), -0.2, 0.2)), 1.0, 10.0),
        "local_coup": jnp.clip(jax.random.uniform(part_keys[2], (NBLK, NNZ, BS, BS), jnp.float32, -0.01, 0.01) * block_levels(part_keys[2], (NBLK, NNZ, BS, BS), ((0, 16),), -0.4, 0.0), -0.01, 0.01),
        "block_cols": set_ends(jax.random.randint(splits[3], (NBLK, NNZ), 0, PATCH), jax.random.fold_in(splits[3], 1), 0, PATCH - 1).astype(jnp.int32),
        "border_coup": jnp.clip(jax.random.uniform(part_keys[4], (DEVS, 4 * BB, BS, BS), jnp.float32, -0.01, 0.01) * block_levels(part_keys[4], (DEVS, 4 * BB, BS, BS), ((0, 16),), -0.4, 0.0), -0.01, 0.01),
        "border_send": set_ends(jax.random.randint(splits[5], (DEVS, 4 * BB), 0, NB), jax.random.fold_in(splits[5], 1), 0, NB - 1).astype(jnp.int32),
        "border_rows": set_ends(jax.random.randint(splits[6], (DEVS, 4 * BB), 0, NB), jax.random.fold_in(splits[6], 1), 0, NB - 1).astype(jnp.int32),
    }


def apply_prec(field, node_diag, local_coup, block_cols, border_coup, border_send, border_rows):
    blocks = field.reshape(NBLK, BS, COLS)
    diag_blocks = node_diag.reshape(NBLK, BS)
    hp = lax.Precision.HIGHEST

    def one_device(dev):
        gxi = dev // (N_GY * N_ND)
        gyi = (dev // N_ND) % N_GY
        ndi = dev % N_ND
        pstart = (dev // N_ND) * PATCH
        patch = lax.dynamic_slice_in_dim(blocks, pstart, PATCH, 0)
        picks = lax.dynamic_slice_in_dim(block_cols, dev * NB, NB, 0)
        coup = lax.dynamic_slice_in_dim(local_coup, dev * NB, NB, 0)
        own = lax.dynamic_slice_in_dim(blocks, dev * NB, NB, 0)
        diag = lax.dynamic_slice_in_dim(diag_blocks, dev * NB, NB, 0)
        picked = jnp.take(patch, picks, axis=0)
        result = diag[:, :, None] * own + jnp.einsum("bkij,bkjc->bic", coup, picked, precision=hp)
        pcoup = lax.dynamic_slice_in_dim(local_coup, pstart, PATCH, 0)
        pcols = lax.dynamic_slice_in_dim(block_cols, pstart, PATCH, 0)
        tterms = jnp.einsum("pkji,pjc->pkic", pcoup, patch, precision=hp).reshape(PATCH * NNZ, BS, COLS)
        mine = ndi * NB + jnp.arange(NB, dtype=jnp.int32)
        tonehot = (pcols.reshape(PATCH * NNZ)[None, :] == mine[:, None]).astype(field.dtype)
        result = result + jnp.einsum("nq,qic->nic", tonehot, tterms, precision=hp)
        left = (((gxi - 1) % N_GX) * N_GY + gyi) * N_ND + ndi
        right = (((gxi + 1) % N_GX) * N_GY + gyi) * N_ND + ndi
        down = (gxi * N_GY + jnp.maximum(gyi - 1, 0)) * N_ND + ndi
        upper = (gxi * N_GY + jnp.minimum(gyi + 1, N_GY - 1)) * N_ND + ndi
        lowok = (gyi > 0).astype(field.dtype)
        highok = (gyi < N_GY - 1).astype(field.dtype)
        valids = [1.0, 1.0, lowok, highok]
        parts = []
        for turn, sender in enumerate([left, right, down, upper]):
            slots = jnp.take(border_send, sender, axis=0)[turn * BB:(turn + 1) * BB]
            index = sender * NB + slots
            parts.append(jnp.take(blocks, index, axis=0) * valids[turn])
        received = jnp.concatenate(parts, axis=0)
        bcoup = jnp.take(border_coup, dev, axis=0)
        contrib = jnp.einsum("mij,mjc->mic", bcoup, received, precision=hp)
        targets = jnp.take(border_rows, dev, axis=0)
        onehot = (targets[None, :] == jnp.arange(NB, dtype=jnp.int32)[:, None]).astype(field.dtype)
        result = result + jnp.einsum("nm,mic->nic", onehot, contrib, precision=hp)
        backs = []
        back_valids = [1.0, 1.0, highok, lowok]
        for turn, source in enumerate([right, left, upper, down]):
            qcoup = jnp.take(border_coup, source, axis=0)[turn * BB:(turn + 1) * BB]
            qrows = jnp.take(border_rows, source, axis=0)[turn * BB:(turn + 1) * BB]
            qblocks = jnp.take(blocks, source * NB + qrows, axis=0)
            backs.append(jnp.einsum("mji,mjc->mic", qcoup, qblocks, precision=hp) * back_valids[turn])
        returned = jnp.concatenate(backs, axis=0)
        sendto = jnp.take(border_send, dev, axis=0)
        sonehot = (sendto[None, :] == jnp.arange(NB, dtype=jnp.int32)[:, None]).astype(field.dtype)
        return result + jnp.einsum("nm,mic->nic", sonehot, returned, precision=hp)

    out = lax.map(one_device, jnp.arange(DEVS, dtype=jnp.int32))
    return out.reshape(NODES, COLS)


def reference(right_side, node_diag, local_coup, block_cols, border_coup, border_send, border_rows):
    solution_field = jnp.zeros_like(right_side)
    residual = right_side
    direction = right_side
    norm_now = jnp.sum(residual * residual, axis=0)
    for step in range(ITERS):
        image = apply_prec(direction, node_diag, local_coup, block_cols, border_coup, border_send, border_rows)
        alpha = norm_now / jnp.sum(direction * image, axis=0)
        solution_field = solution_field + alpha * direction
        residual = residual - alpha * image
        norm_next = jnp.sum(residual * residual, axis=0)
        direction = residual + (norm_next / norm_now) * direction
        norm_now = norm_next
    return solution_field
```

```python
import jax
import jax.numpy as jnp
from jax import lax
from jax.experimental import pallas as pl
from jax.experimental.pallas import tpu as pltpu
from jax.sharding import PartitionSpec as P

F32 = jnp.float32
HP = lax.Precision.HIGHEST
AXES = ("gx", "gy", "nd")
SIDE = 2
TAIL = 8


def vmem():
    return pl.BlockSpec(memory_space=pltpu.VMEM)


def smem():
    return pl.BlockSpec(memory_space=pltpu.SMEM)


def axis_sum(part):
    for axis in ("nd", "gy", "gx"):
        count = lax.axis_size(axis)
        if count & (count - 1):
            part = lax.psum(part, axis)
            continue
        step = 1
        while step < count:
            part = part + lax.ppermute(part, axis, [(i, i ^ step) for i in range(count)])
            step *= 2
    return part


def prep_kernel(cols, send, rows, sides, field, diag, local, border, own, pair, *pays):
    nblocks, nonzeros, bs, _ = local.shape
    width = nblocks * bs
    patch_len = 2 * nblocks
    base = sides[0] * nblocks
    own[...] = jnp.zeros(own.shape, F32)
    pair[...] = jnp.zeros(pair.shape, F32)
    pair[pl.ds(0, width), :] = field[...]
    for b in range(nblocks):
        for k in range(nonzeros):
            spot = lax.rem(cols[b, k] - base + patch_len, patch_len)
            block = local[b, k]
            for c in range(nblocks):

                @pl.when(spot == c)
                def _():
                    own[pl.ds(b * bs, bs), pl.ds(c * bs, bs)] += block

                @pl.when(spot == c + nblocks)
                def _():
                    pair[pl.ds(width + b * bs, bs), pl.ds(c * bs, bs)] += block

    lower = own[...]
    here = lax.broadcasted_iota(jnp.int32, (width, width), 0)
    there = lax.broadcasted_iota(jnp.int32, (width, width), 1)
    own[...] = lower + lower.T + jnp.where(here == there, diag[...], 0.0)
    lane = lax.broadcasted_iota(jnp.int32, (TAIL, bs), 1)
    for n, pay in enumerate(pays):
        give = sides[1 + n]
        tail = jnp.zeros((TAIL, bs), F32)
        for s in range(SIDE):
            pay[pl.ds(s * bs, bs), :] = border[give * SIDE + s]
            tail = jnp.where(lane == s, rows[0, give * SIDE + s].astype(F32), tail)
            back = (give ^ 1) * SIDE + s
            tail = jnp.where(lane == SIDE + s, send[0, back].astype(F32), tail)
        pay[pl.ds(SIDE * bs, TAIL), :] = tail


def apply_kernel(nslots, send, rows, sides, field, own, pair, mate, border, *refs):
    fields = refs[:nslots]
    pays = refs[nslots : 2 * nslots]
    image, coup, sums = refs[2 * nslots :]
    width = field.shape[0]
    bs = border.shape[1]
    coup[0] = pair[pl.ds(width, width), :] + mate[pl.ds(width, width), :].T
    for n in range(nslots):
        take = sides[1 + n]
        other = take ^ 1
        coup[1 + n] = jnp.zeros((width, width), F32)
        pay = pays[n]
        tail = pay[pl.ds(SIDE * bs, TAIL), :]
        for s in range(SIDE):
            from_row = tail[0:1, s : s + 1]
            from_send = tail[0:1, SIDE + s : SIDE + s + 1]
            block = border[take * SIDE + s]
            turned = pay[pl.ds(s * bs, bs), :].T
            at = pl.multiple_of(rows[0, take * SIDE + s] * bs, bs)
            bt = pl.multiple_of(send[0, other * SIDE + s] * bs, bs)
            for c in range(width // bs):
                coup[1 + n, pl.ds(at, bs), pl.ds(c * bs, bs)] += jnp.where(from_send == c, block, 0.0)
                coup[1 + n, pl.ds(bt, bs), pl.ds(c * bs, bs)] += jnp.where(from_row == c, turned, 0.0)
    acc = jnp.dot(own[...], field[...], precision=HP, preferred_element_type=F32)
    acc += jnp.dot(coup[0], mate[pl.ds(0, width), :], precision=HP, preferred_element_type=F32)
    for n in range(nslots):
        acc += jnp.dot(coup[1 + n], fields[n][...], precision=HP, preferred_element_type=F32)
    image[...] = acc
    sums[0:1, :] = jnp.sum(field[...] * field[...], axis=0, keepdims=True)
    sums[1:2, :] = jnp.sum(field[...] * acc, axis=0, keepdims=True)


def form_kernel(weights, step, field, image, mate_b, mate_w, own, coup, *refs):
    nused = len(weights)
    fields = refs[:nused]
    images = refs[nused : 2 * nused]
    sums = refs[2 * nused]
    width = field.shape[0]
    a = step[...]
    res = field[...] - a * image[...]
    acc = jnp.dot(own[...], res, precision=HP, preferred_element_type=F32)
    far = mate_b[pl.ds(0, width), :] - a * mate_w[...]
    acc += jnp.dot(coup[0], far, precision=HP, preferred_element_type=F32)
    for n, (slot, weight) in enumerate(weights):
        far = weight * (fields[n][...] - a * images[n][...])
        acc += jnp.dot(coup[1 + slot], far, precision=HP, preferred_element_type=F32)
    sums[0:1, :] = jnp.sum(res * res, axis=0, keepdims=True)
    sums[1:2, :] = jnp.sum(res * acc, axis=0, keepdims=True)


def shards(right_side, node_diag, local_coup, block_cols, border_coup, border_send, border_rows):
    width, ncols = right_side.shape
    nblocks, _, bs, _ = local_coup.shape
    n_gx, n_gy, n_nd = (lax.axis_size(a) for a in AXES)
    assert n_nd == 2 and border_coup.shape[1] == 4 * SIDE
    gyi = lax.axis_index("gy")
    swap = [(0, 1), (1, 0)]
    right = [(i, (i + 1) % n_gx) for i in range(n_gx)]
    left = [(j, i) for i, j in right]
    up = [(i, i + 1) for i in range(n_gy - 1)]
    down = [(j, i) for i, j in up]
    slots = [("gx", right, 0), ("gx", left, 1)]
    if n_gy == 2:
        slots.insert(1, ("gy", swap, jnp.where(gyi == 0, 3, 2)))
        weights = [(0, 2.0), (1, 1.0)]
    elif n_gy > 2:
        slots.insert(1, ("gy", up, 2))
        slots.append(("gy", down, 3))
        weights = [(0, 2.0), (1, 2.0)]
    else:
        weights = [(0, 2.0)]
    nslots = len(slots)
    take = [jnp.asarray(t, jnp.int32) for _, _, t in slots]
    ndi = lax.axis_index("nd").astype(jnp.int32)
    give = [jnp.where(gyi == 0, 3, 2).astype(jnp.int32) if n_gy == 2 and a == "gy" else t ^ 1 for (a, _, _), t in zip(slots, take)]
    sides_out = jnp.stack([ndi] + give)
    sides_in = jnp.stack([ndi] + take)

    fields = [lax.ppermute(right_side, axis, perm) for axis, perm, _ in slots]
    pay_shape = jax.ShapeDtypeStruct((SIDE * bs + TAIL, bs), F32)
    border = border_coup[0]
    own, pair, *pays = pl.pallas_call(
        prep_kernel,
        name="prep",
        in_specs=[smem()] * 4 + [vmem()] * 4,
        out_specs=[vmem()] * (2 + nslots),
        out_shape=[jax.ShapeDtypeStruct((width, width), F32), jax.ShapeDtypeStruct((2 * width, ncols), F32)]
        + [pay_shape] * nslots,
    )(block_cols, border_send, border_rows, sides_out, right_side, node_diag.reshape(1, width), local_coup, border)
    mate = lax.ppermute(pair, "nd", swap)
    pays = [lax.ppermute(pay, axis, perm) for pay, (axis, perm, _) in zip(pays, slots)]

    image, coup, sums = pl.pallas_call(
        lambda *refs: apply_kernel(nslots, *refs),
        name="apply",
        in_specs=[smem()] * 3 + [vmem()] * (5 + 2 * nslots),
        out_specs=[vmem()] * 3,
        out_shape=[
            jax.ShapeDtypeStruct((width, ncols), F32),
            jax.ShapeDtypeStruct((1 + nslots, width, width), F32),
            jax.ShapeDtypeStruct((2, ncols), F32),
        ],
    )(border_send, border_rows, sides_in, right_side, own, pair, mate, border, *fields, *pays)

    images = [lax.ppermute(image, slots[n][0], slots[n][1]) for n, _ in weights]
    mate_w = lax.ppermute(image, "nd", swap)
    sums = axis_sum(sums)
    norm, curve = sums[0:1], sums[1:2]
    step = norm / curve

    sums = pl.pallas_call(
        lambda *refs: form_kernel(weights, *refs),
        name="form",
        in_specs=[vmem()] * (7 + 2 * len(weights)),
        out_specs=vmem(),
        out_shape=jax.ShapeDtypeStruct((2, ncols), F32),
    )(step, right_side, image, mate, mate_w, own, coup, *[fields[n] for n, _ in weights], *images)
    sums = axis_sum(sums)
    ratio = sums[0:1] / norm
    last = sums[0:1] / (sums[1:2] - ratio * ratio * curve)
    residual = right_side - step * image
    return step * right_side + last * (residual + ratio * right_side)


def solution(mesh):
    blocks = P(("var", "gx", "gy", "nd"))
    tables = P(AXES)
    in_specs = (blocks, blocks, blocks, tables, blocks, tables, tables)
    return jax.shard_map(shards, mesh=mesh, in_specs=in_specs, out_specs=blocks, check_vma=False)
```

```python
import jax
import jax.numpy as jnp
from jax import lax
from jax.experimental import pallas as pl
from jax.experimental.pallas import tpu as pltpu
from jax.sharding import PartitionSpec as P

F32 = jnp.float32
HP = lax.Precision.HIGHEST
AXES = ("gx", "gy", "nd")
SIDE = 2
TAIL = 8


def vmem():
    return pl.BlockSpec(memory_space=pltpu.VMEM)


def smem():
    return pl.BlockSpec(memory_space=pltpu.SMEM)


def call(kernel, name, tables, shapes, flops=None):
    def run(*args):
        args = list(args[:tables]) + [pltpu.with_memory_space_constraint(a, pltpu.VMEM) for a in args[tables:]]
        return pl.pallas_call(
            kernel,
            name=name,
            in_specs=[smem()] * tables + [vmem()] * (len(args) - tables),
            out_specs=[vmem()] * len(shapes),
            out_shape=[pltpu.VMEM(shape, F32) for shape in shapes],
            compiler_params=pltpu.CompilerParams(vmem_limit_bytes=16 << 20),
            cost_estimate=flops and pl.CostEstimate(flops=flops, bytes_accessed=1 << 20, transcendentals=0),
        )(*args)

    return run


def axis_sum(part, axes):
    count = lax.axis_size(axes)
    if count & (count - 1):
        return lax.psum(part, axes)
    step = 1
    while step < count:
        masks = [m * step for m in (1, 2, 3) if m * step < count]
        part = part + sum(lax.ppermute(part, axes, [(i, i ^ m) for i in range(count)]) for m in masks)
        step *= 4
    return part


def prep_kernel(cols, sides, packed, diag, local, own, pair):
    nblocks, nonzeros, bs, _ = local.shape
    width = nblocks * bs
    patch_len = 2 * nblocks
    base = sides[0] * nblocks
    own[...] = jnp.zeros(own.shape, F32)
    pair[...] = jnp.zeros((width, width), F32)
    for b in range(nblocks):
        for k in range(nonzeros):
            spot = lax.rem(cols[b, k] - base + patch_len, patch_len)
            block = local[b, k]
            for c in range(nblocks):

                @pl.when(spot == c)
                def _():
                    own[pl.ds(b * bs, bs), pl.ds(c * bs, bs)] += block

                @pl.when(spot == c + nblocks)
                def _():
                    pair[pl.ds(b * bs, bs), pl.ds(c * bs, bs)] += block

    lower = own[...]
    here = lax.broadcasted_iota(jnp.int32, (width, width), 0)
    there = lax.broadcasted_iota(jnp.int32, (width, width), 1)
    own[...] = lower + lower.T + jnp.where(here == there, diag[...], 0.0)


def pack_kernel(send, rows, gives, field, border, *pays):
    width = field.shape[0]
    bs = border.shape[1]
    lane = lax.broadcasted_iota(jnp.int32, (TAIL, SIDE * bs), 1)
    for n, pay in enumerate(pays):
        give = gives[n]
        pay[pl.ds(0, width), :] = field[...]
        tail = jnp.zeros(lane.shape, F32)
        for s in range(SIDE):
            pay[pl.ds(width, bs), pl.ds(s * bs, bs)] = border[give * SIDE + s]
            tail = jnp.where(lane == s, rows[0, give * SIDE + s].astype(F32), tail)
            sent = send[0, (give ^ 1) * SIDE + s].astype(F32)
            tail = jnp.where(lane == SIDE + s, sent, tail)
        pay[pl.ds(width + bs, TAIL), :] = tail


def apply_kernel(send, rows, takes, field, own, pair, mate, mate_pair, border, *refs):
    *pays, image, coup = refs
    width = field.shape[0]
    bs = border.shape[1]
    coup[0] = pair[...] + mate_pair[...].T
    for n, pay in enumerate(pays):
        take = takes[n]
        other = take ^ 1
        coup[1 + n] = jnp.zeros((width, width), F32)
        tail = pay[pl.ds(width + bs, TAIL), :]
        for s in range(SIDE):
            from_row = tail[0:1, s : s + 1]
            from_send = tail[0:1, SIDE + s : SIDE + s + 1]
            block = border[take * SIDE + s]
            turned = pay[pl.ds(width, bs), pl.ds(s * bs, bs)].T
            at = pl.multiple_of(rows[0, take * SIDE + s] * bs, bs)
            bt = pl.multiple_of(send[0, other * SIDE + s] * bs, bs)
            for c in range(width // bs):
                coup[1 + n, pl.ds(at, bs), pl.ds(c * bs, bs)] += jnp.where(from_send == c, block, 0.0)
                coup[1 + n, pl.ds(bt, bs), pl.ds(c * bs, bs)] += jnp.where(from_row == c, turned, 0.0)
    acc = jnp.dot(own[...], field[...], precision=HP, preferred_element_type=F32)
    acc += jnp.dot(coup[0], mate[...], precision=HP, preferred_element_type=F32)
    for n, pay in enumerate(pays):
        acc += jnp.dot(coup[1 + n], pay[pl.ds(0, width), :], precision=HP, preferred_element_type=F32)
    image[pl.ds(0, width), :] = acc
    norm = jnp.sum(field[...] * field[...], axis=0, keepdims=True)
    curve = jnp.sum(field[...] * acc, axis=0, keepdims=True)
    line = lax.broadcasted_iota(jnp.int32, (TAIL, acc.shape[1]), 0)
    image[pl.ds(width, TAIL), :] = jnp.where(line == 0, norm, jnp.where(line == 1, curve, 0.0))


def form_kernel(weights, sums_in, field, image, mate, mate_w, own, coup, *refs):
    nused = len(weights)
    pays = refs[:nused]
    images = refs[nused : 2 * nused]
    sums = refs[2 * nused]
    width = field.shape[0]
    a = sums_in[0:1, :] / sums_in[1:2, :]
    res = field[...] - a * image[pl.ds(0, width), :]
    acc = jnp.dot(own[...], res, precision=HP, preferred_element_type=F32)
    far = mate[...] - a * mate_w[pl.ds(0, width), :]
    acc += jnp.dot(coup[0], far, precision=HP, preferred_element_type=F32)
    for n, (slot, weight) in enumerate(weights):
        far = weight * (pays[n][pl.ds(0, width), :] - a * images[n][pl.ds(0, width), :])
        acc += jnp.dot(coup[1 + slot], far, precision=HP, preferred_element_type=F32)
    sums[0:1, :] = jnp.sum(res * res, axis=0, keepdims=True)
    sums[1:2, :] = jnp.sum(res * acc, axis=0, keepdims=True)


def last_kernel(first, second, field, image, out):
    norm, curve = first[0:1, :], first[1:2, :]
    a = norm / curve
    ratio = second[0:1, :] / norm
    b = second[0:1, :] / (second[1:2, :] - ratio * ratio * curve)
    out[...] = (a + b * (1.0 + ratio)) * field[...] - (b * a) * image[pl.ds(0, field.shape[0]), :]


def shards(right_side, node_diag, local_coup, block_cols, border_coup, border_send, border_rows):
    width, ncols = right_side.shape
    nblocks, _, bs, _ = local_coup.shape
    n_gx, n_gy, n_nd = (lax.axis_size(a) for a in AXES)
    assert n_nd == 2 and border_coup.shape[1] == 4 * SIDE
    gyi = lax.axis_index("gy")
    swap = [(0, 1), (1, 0)]
    right = [(i, (i + 1) % n_gx) for i in range(n_gx)]
    left = [(j, i) for i, j in right]
    up = [(i, i + 1) for i in range(n_gy - 1)]
    down = [(j, i) for i, j in up]
    slots = [("gx", right, 0), ("gx", left, 1)]
    if n_gy == 2:
        slots.insert(1, ("gy", swap, jnp.where(gyi == 0, 3, 2)))
        weights = [(0, 2.0), (1, 1.0)]
    elif n_gy > 2:
        slots.insert(1, ("gy", up, 2))
        slots.append(("gy", down, 3))
        weights = [(0, 2.0), (1, 2.0)]
    else:
        weights = [(0, 2.0)]
    nslots = len(slots)
    take = [jnp.asarray(t, jnp.int32) for _, _, t in slots]
    ndi = lax.axis_index("nd").astype(jnp.int32)
    give = [jnp.where(gyi == 0, 3, 2).astype(jnp.int32) if n_gy == 2 and a == "gy" else t ^ 1 for (a, _, _), t in zip(slots, take)]
    gives = jnp.stack(give)
    takes = jnp.stack(take)
    border = border_coup[0]

    packed = call(pack_kernel, "pack", 3, [(width + bs + TAIL, ncols)] * nslots)(border_send, border_rows, gives, right_side, border)
    pays = [lax.ppermute(pay, axis, perm) for pay, (axis, perm, _) in zip(packed, slots)]
    own, pair = call(prep_kernel, "prep", 2, [(width, width)] * 2, 1 << 24)(
        block_cols, ndi[None], packed[0], node_diag.reshape(1, width), local_coup
    )
    mate = lax.ppermute(right_side, "nd", swap)
    mate_pair = lax.ppermute(pair, "nd", swap)

    image, coup = call(apply_kernel, "apply", 3, [(width + TAIL, ncols), (1 + nslots, width, width)])(
        border_send, border_rows, takes, right_side, own, pair, mate, mate_pair, border, *pays
    )
    images = [lax.ppermute(image, slots[n][0], slots[n][1]) for n, _ in weights]
    mate_w = lax.ppermute(image, "nd", swap)
    first = axis_sum(image[width:] + mate_w[width:], ("gx", "gy"))

    (second,) = call(lambda *refs: form_kernel(weights, *refs), "form", 0, [(2, ncols)])(
        first, right_side, image, mate, mate_w, own, coup, *[pays[n] for n, _ in weights], *images
    )
    second = axis_sum(second, AXES)
    return pl.pallas_call(
        last_kernel,
        name="last",
        in_specs=[vmem()] * 4,
        out_specs=vmem(),
        out_shape=jax.ShapeDtypeStruct((width, ncols), F32),
        compiler_params=pltpu.CompilerParams(vmem_limit_bytes=16 << 20),
    )(first, second, right_side, image)


def solution(mesh):
    blocks = P(("var", "gx", "gy", "nd"))
    tables = P(AXES)
    in_specs = (blocks, blocks, blocks, tables, blocks, tables, tables)
    return jax.shard_map(shards, mesh=mesh, in_specs=in_specs, out_specs=blocks, check_vma=False)
```

```python
from functools import partial

import jax
import jax.numpy as jnp
from jax import lax
from jax.experimental import pallas as pl
from jax.experimental.pallas import tpu as pltpu
from jax.sharding import PartitionSpec as P

F32 = jnp.float32
HP = lax.Precision.HIGHEST
AXES = ("gx", "gy", "nd")
SIDE = 2
LIMIT = 8 << 20
TAIL = 8


def vmem():
    return pl.BlockSpec(memory_space=pltpu.VMEM)


def smem():
    return pl.BlockSpec(memory_space=pltpu.SMEM)


def call(kernel, name, tables, shapes, flops=None, scratch=()):
    def run(*args):
        args = list(args[:tables]) + [pltpu.with_memory_space_constraint(a, pltpu.VMEM) for a in args[tables:]]
        return pl.pallas_call(
            kernel,
            name=name,
            in_specs=[smem()] * tables + [vmem()] * (len(args) - tables),
            out_specs=[vmem()] * len(shapes),
            out_shape=[pltpu.VMEM(shape, F32) for shape in shapes],
            scratch_shapes=scratch,
            compiler_params=pltpu.CompilerParams(vmem_limit_bytes=LIMIT),
            cost_estimate=flops and pl.CostEstimate(flops=flops, bytes_accessed=1 << 20, transcendentals=0),
        )(*args)

    return run


def axis_sum(part, axes):
    count = lax.axis_size(axes)
    if count & (count - 1):
        return lax.psum(part, axes)
    step = 1
    while step < count:
        masks = [m * step for m in (1, 2, 3) if m * step < count]
        part = part + sum(lax.ppermute(part, axes, [(i, i ^ m) for i in range(count)]) for m in masks)
        step *= 4
    return part


def prep_kernel(cols, sides, packed, diag, local, own, pair):
    nblocks, nonzeros, bs, _ = local.shape
    width = nblocks * bs
    patch_len = 2 * nblocks
    base = sides[0] * nblocks
    own[...] = jnp.zeros(own.shape, F32)
    pair[...] = jnp.zeros((width, width), F32)
    for b in range(nblocks):
        for k in range(nonzeros):
            spot = lax.rem(cols[b, k] - base + patch_len, patch_len)
            block = local[b, k]
            for c in range(nblocks):

                @pl.when(spot == c)
                def _():
                    own[pl.ds(b * bs, bs), pl.ds(c * bs, bs)] += block

                @pl.when(spot == c + nblocks)
                def _():
                    pair[pl.ds(b * bs, bs), pl.ds(c * bs, bs)] += block

    lower = own[...]
    here = lax.broadcasted_iota(jnp.int32, (width, width), 0)
    there = lax.broadcasted_iota(jnp.int32, (width, width), 1)
    own[...] = lower + lower.T + jnp.where(here == there, diag[...], 0.0)


def pack_kernel(send, rows, gives, field, border, *refs):
    *pays, sems = refs
    width = field.shape[0]
    bs = border.shape[1]
    copies = []
    for n, pay in enumerate(pays):
        copies.append(pltpu.make_async_copy(field, pay.at[pl.ds(0, width), :], sems.at[n, SIDE]))
        for s in range(SIDE):
            block = pay.at[pl.ds(width, bs), pl.ds(s * bs, bs)]
            copies.append(pltpu.make_async_copy(border.at[gives[n] * SIDE + s], block, sems.at[n, s]))
    for copy in copies:
        copy.start()
    lane = lax.broadcasted_iota(jnp.int32, (TAIL, SIDE * bs), 1)
    for n, pay in enumerate(pays):
        give = gives[n]
        tail = jnp.zeros(lane.shape, F32)
        for s in range(SIDE):
            tail = jnp.where(lane == s, rows[0, give * SIDE + s].astype(F32), tail)
            sent = send[0, (give ^ 1) * SIDE + s].astype(F32)
            tail = jnp.where(lane == SIDE + s, sent, tail)
        pay[pl.ds(width + bs, TAIL), :] = tail
    for copy in copies:
        copy.wait()


def build_edge(coup, take, send, rows, border, pay):
    bs = border.shape[1]
    width = coup.shape[0]
    other = take ^ 1
    coup[...] = jnp.zeros((width, width), F32)
    tail = pay[pl.ds(width + bs, TAIL), :]
    for s in range(SIDE):
        from_row = tail[0:1, s : s + 1]
        from_send = tail[0:1, SIDE + s : SIDE + s + 1]
        block = border[take * SIDE + s]
        turned = pay[pl.ds(width, bs), pl.ds(s * bs, bs)].T
        at = pl.multiple_of(rows[0, take * SIDE + s] * bs, bs)
        bt = pl.multiple_of(send[0, other * SIDE + s] * bs, bs)
        for c in range(width // bs):
            coup[pl.ds(at, bs), pl.ds(c * bs, bs)] += jnp.where(from_send == c, block, 0.0)
            coup[pl.ds(bt, bs), pl.ds(c * bs, bs)] += jnp.where(from_row == c, turned, 0.0)


def dot(a, b):
    return jnp.dot(a, b, precision=HP, preferred_element_type=F32)


def two_rows(first, second):
    line = lax.broadcasted_iota(jnp.int32, (TAIL, first.shape[1]), 0)
    return jnp.where(line == 0, first, jnp.where(line == 1, second, 0.0))


def half_kernel(weights, send, rows, takes, field, own, pair, mate, mate_pair, border, *refs):
    *pays, image, coup, sums = refs
    width = field.shape[0]
    here = field[...]
    coup[0] = pair[...] + mate_pair[...].T
    acc = dot(own[...], here) + dot(coup[0], mate[...])
    half = acc
    for n, pay in enumerate(pays):
        build_edge(coup.at[1 + n], takes[n], send, rows, border, pay)
        edge = dot(coup[1 + n], pay[pl.ds(0, width), :])
        acc += edge
        half += weights[n] * edge
    image[...] = acc
    norm = jnp.sum(here * here, axis=0, keepdims=True)
    sums[...] = two_rows(norm, jnp.sum(here * half, axis=0, keepdims=True))


def rest_kernel(first, send, rows, takes, part, border, *refs):
    *pays, image, coup = refs
    width = part.shape[0]
    acc = part[...]
    for n, pay in enumerate(pays):
        build_edge(coup, takes[first + n], send, rows, border, pay)
        acc += dot(coup[...], pay[pl.ds(0, width), :])
    image[...] = acc


def near_kernel(first, field, image, mate, mate_w, own, coup, sums):
    a = first[0:1, :] / first[1:2, :]
    res = field[...] - a * image[...]
    acc = dot(own[...], res) + dot(coup[0], mate[...] - a * mate_w[...])
    sums[...] = two_rows(jnp.sum(res * res, axis=0, keepdims=True), jnp.sum(res * acc, axis=0, keepdims=True))


def far_kernel(weights, first, near, field, image, coup, *refs):
    count = len(weights)
    pays, images, sums = refs[:count], refs[count : 2 * count], refs[2 * count]
    width = field.shape[0]
    a = first[0:1, :] / first[1:2, :]
    res = field[...] - a * image[...]
    acc = jnp.zeros(res.shape, F32)
    for n, weight in enumerate(weights):
        acc += dot(coup[1 + n], weight * (pays[n][pl.ds(0, width), :] - a * images[n][...]))
    sums[...] = near[...] + two_rows(jnp.zeros(a.shape, F32), jnp.sum(res * acc, axis=0, keepdims=True))


def shards(right_side, node_diag, local_coup, block_cols, border_coup, border_send, border_rows):
    width, ncols = right_side.shape
    nblocks, _, bs, _ = local_coup.shape
    n_gx, n_gy, n_nd = (lax.axis_size(a) for a in AXES)
    assert n_nd == 2 and border_coup.shape[1] == 4 * SIDE
    gyi = lax.axis_index("gy")
    swap = [(0, 1), (1, 0)]
    right = [(i, (i + 1) % n_gx) for i in range(n_gx)]
    left = [(j, i) for i, j in right]
    up = [(i, i + 1) for i in range(n_gy - 1)]
    down = [(j, i) for i, j in up]
    facing = jnp.where(gyi == 0, 3, 2)
    slots = [("gx", right, 0), ("gx", left, 1)]
    weights = [2.0]
    if n_gy == 2:
        slots.insert(0, ("gy", swap, facing))
        weights.insert(0, 1.0)
    elif n_gy > 2:
        slots.insert(0, ("gy", up, 2))
        slots.append(("gy", down, 3))
        weights.insert(0, 2.0)
    early = len(weights)
    takes = jnp.stack([jnp.asarray(t, jnp.int32) for _, _, t in slots])
    gives = jnp.stack([jnp.asarray(facing if t is facing else t ^ 1, jnp.int32) for _, _, t in slots])
    ndi = lax.axis_index("nd").astype(jnp.int32)
    border = border_coup[0]

    packed = pl.pallas_call(
        pack_kernel,
        name="pack",
        in_specs=[smem()] * 3 + [pl.BlockSpec(memory_space=pl.ANY)] * 2,
        out_specs=[vmem()] * len(slots),
        out_shape=[pltpu.VMEM((width + bs + TAIL, ncols), F32)] * len(slots),
        scratch_shapes=[pltpu.SemaphoreType.DMA((len(slots), SIDE + 1))],
        compiler_params=pltpu.CompilerParams(vmem_limit_bytes=LIMIT),
    )(border_send, border_rows, gives, *[pltpu.with_memory_space_constraint(a, pltpu.HBM) for a in (right_side, border)])
    pays = [lax.ppermute(pay, axis, perm) for pay, (axis, perm, _) in zip(packed, slots)]
    mate = lax.ppermute(right_side, "nd", swap)
    own, pair = call(prep_kernel, "prep", 2, [(width, width)] * 2, flops=1 << 24)(
        block_cols, ndi[None], packed[0], node_diag.reshape(1, width), local_coup
    )
    mate_pair = lax.ppermute(pair, "nd", swap)

    part, coup, first = call(partial(half_kernel, weights), "half", 3, [(width, ncols), (1 + early, width, width), (TAIL, ncols)])(
        border_send, border_rows, takes, right_side, own, pair, mate, mate_pair, border, *pays[:early]
    )
    first = axis_sum(first, AXES)
    (image,) = call(partial(rest_kernel, early), "rest", 3, [(width, ncols)], scratch=[pltpu.VMEM((width, width), F32)])(
        border_send, border_rows, takes, part, border, *pays[early:]
    )
    images = [lax.ppermute(image, axis, perm) for axis, perm, _ in slots[:early]]
    mate_w = lax.ppermute(image, "nd", swap)
    (near,) = call(near_kernel, "near", 0, [(TAIL, ncols)])(first, right_side, image, mate, mate_w, own, coup)
    (second,) = call(partial(far_kernel, weights), "far", 0, [(TAIL, ncols)])(
        first, near, right_side, image, coup, *pays[:early], *images
    )
    second = axis_sum(second, AXES)
    norm, curve = first[0:1], first[1:2]
    step = norm / curve
    ratio = second[0:1] / norm
    last = second[0:1] / (second[1:2] - ratio * ratio * curve)
    return (step + last * (1.0 + ratio)) * right_side - (last * step) * image


def solution(mesh):
    blocks = P(("var", "gx", "gy", "nd"))
    tables = P(AXES)
    in_specs = (blocks, blocks, blocks, tables, blocks, tables, tables)
    return jax.shard_map(shards, mesh=mesh, in_specs=in_specs, out_specs=blocks, check_vma=False)
```

```python
from functools import partial

import jax
import jax.numpy as jnp
from jax import lax
from jax.experimental import pallas as pl
from jax.experimental.pallas import tpu as pltpu
from jax.sharding import PartitionSpec as P

F32 = jnp.float32
HP = lax.Precision.HIGHEST
AXES = ("gx", "gy", "nd")
SIDE = 2
LIMIT = 8 << 20
TAIL = 8


def vmem():
    return pl.BlockSpec(memory_space=pltpu.VMEM)


def smem():
    return pl.BlockSpec(memory_space=pltpu.SMEM)


def call(kernel, name, tables, shapes, flops=None, scratch=()):
    def run(*args):
        args = list(args[:tables]) + [pltpu.with_memory_space_constraint(a, pltpu.VMEM) for a in args[tables:]]
        return pl.pallas_call(
            kernel,
            name=name,
            in_specs=[smem()] * tables + [vmem()] * (len(args) - tables),
            out_specs=[vmem()] * len(shapes),
            out_shape=[pltpu.VMEM(shape, F32) for shape in shapes],
            scratch_shapes=scratch,
            compiler_params=pltpu.CompilerParams(vmem_limit_bytes=LIMIT),
            cost_estimate=flops and pl.CostEstimate(flops=flops, bytes_accessed=1 << 20, transcendentals=0),
        )(*args)

    return run


def axis_sum(part, axes):
    count = lax.axis_size(axes)
    if count & (count - 1):
        return lax.psum(part, axes)
    step = 1
    while step < count:
        masks = [m * step for m in (1, 2, 3) if m * step < count]
        part = part + sum(lax.ppermute(part, axes, [(i, i ^ m) for i in range(count)]) for m in masks)
        step *= 4
    return part


def write_tail(pay, give, send, rows, width, bs):
    lane = lax.broadcasted_iota(jnp.int32, (TAIL, SIDE * bs), 1)
    tail = jnp.zeros(lane.shape, F32)
    for s in range(SIDE):
        tail = jnp.where(lane == s, rows[0, give * SIDE + s].astype(F32), tail)
        sent = send[0, (give ^ 1) * SIDE + s].astype(F32)
        tail = jnp.where(lane == SIDE + s, sent, tail)
    pay[pl.ds(width + bs, TAIL), :] = tail


def pack_kernel(send, rows, gives, field, border, *refs):
    *pays, sems = refs
    width = field.shape[0]
    bs = border.shape[1]
    copies = []
    for n, pay in enumerate(pays):
        copies.append(pltpu.make_async_copy(field, pay.at[pl.ds(0, width), :], sems.at[n, SIDE]))
        for s in range(SIDE):
            block = pay.at[pl.ds(width, bs), pl.ds(s * bs, bs)]
            copies.append(pltpu.make_async_copy(border.at[gives[n] * SIDE + s], block, sems.at[n, s]))
    for copy in copies:
        copy.start()
    for n, pay in enumerate(pays):
        write_tail(pay, gives[n], send, rows, width, bs)
    for copy in copies:
        copy.wait()


def prep_kernel(first, cols, sides, send, rows, gives, packed, diag, local, border, own, pair, *pays):
    nblocks, nonzeros, bs, _ = local.shape
    width = nblocks * bs
    patch_len = 2 * nblocks
    base = sides[0] * nblocks
    own[...] = jnp.zeros(own.shape, F32)
    pair[...] = jnp.zeros((width, width), F32)
    for b in range(nblocks):
        for k in range(nonzeros):
            spot = lax.rem(cols[b, k] - base + patch_len, patch_len)
            block = local[b, k]
            for c in range(nblocks):

                @pl.when(spot == c)
                def _():
                    own[pl.ds(b * bs, bs), pl.ds(c * bs, bs)] += block

                @pl.when(spot == c + nblocks)
                def _():
                    pair[pl.ds(b * bs, bs), pl.ds(c * bs, bs)] += block

    lower = own[...]
    here = lax.broadcasted_iota(jnp.int32, (width, width), 0)
    there = lax.broadcasted_iota(jnp.int32, (width, width), 1)
    own[...] = lower + lower.T + jnp.where(here == there, diag[...], 0.0)
    for n, pay in enumerate(pays):
        give = gives[first + n]
        pay[pl.ds(0, width), :] = packed[pl.ds(0, width), :]
        for s in range(SIDE):
            pay[pl.ds(width, bs), pl.ds(s * bs, bs)] = border[give * SIDE + s]
        write_tail(pay, give, send, rows, width, bs)


def build_edge(coup, take, send, rows, border, pay):
    bs = border.shape[1]
    width = coup.shape[0]
    other = take ^ 1
    coup[...] = jnp.zeros((width, width), F32)
    tail = pay[pl.ds(width + bs, TAIL), :]
    for s in range(SIDE):
        from_row = tail[0:1, s : s + 1]
        from_send = tail[0:1, SIDE + s : SIDE + s + 1]
        block = border[take * SIDE + s]
        turned = pay[pl.ds(width, bs), pl.ds(s * bs, bs)].T
        at = pl.multiple_of(rows[0, take * SIDE + s] * bs, bs)
        bt = pl.multiple_of(send[0, other * SIDE + s] * bs, bs)
        for c in range(width // bs):
            coup[pl.ds(at, bs), pl.ds(c * bs, bs)] += jnp.where(from_send == c, block, 0.0)
            coup[pl.ds(bt, bs), pl.ds(c * bs, bs)] += jnp.where(from_row == c, turned, 0.0)


def dot(a, b):
    return jnp.dot(a, b, precision=HP, preferred_element_type=F32)


def two_rows(first, second):
    line = lax.broadcasted_iota(jnp.int32, (TAIL, first.shape[1]), 0)
    return jnp.where(line == 0, first, jnp.where(line == 1, second, 0.0))


def half_kernel(weights, send, rows, takes, field, own, pair, mate, mate_pair, border, *refs):
    *pays, image, coup, sums = refs
    width = field.shape[0]
    here = field[...]
    coup[0] = pair[...] + mate_pair[...].T
    acc = dot(own[...], here) + dot(coup[0], mate[...])
    half = acc
    for n, pay in enumerate(pays):
        build_edge(coup.at[1 + n], takes[n], send, rows, border, pay)
        edge = dot(coup[1 + n], pay[pl.ds(0, width), :])
        acc += edge
        half += weights[n] * edge
    image[...] = acc
    norm = jnp.sum(here * here, axis=0, keepdims=True)
    sums[...] = two_rows(norm, jnp.sum(here * half, axis=0, keepdims=True))


def rest_kernel(skip, send, rows, takes, part, border, *refs):
    *pays, image, coup = refs
    width = part.shape[0]
    acc = part[...]
    for n, pay in enumerate(pays):
        build_edge(coup, takes[skip + n], send, rows, border, pay)
        acc += dot(coup[...], pay[pl.ds(0, width), :])
    image[...] = acc


def step_kernel(first, field, image, res):
    res[...] = field[...] - first[0:1, :] / first[1:2, :] * image[...]


def near_kernel(res, mate_r, own, coup, sums):
    here = res[...]
    acc = dot(own[...], here) + dot(coup[0], mate_r[...])
    sums[...] = two_rows(jnp.sum(here * here, axis=0, keepdims=True), jnp.sum(here * acc, axis=0, keepdims=True))


def far_kernel(weights, near, res, coup, *refs):
    *far, sums = refs
    acc = jnp.zeros(res.shape, F32)
    for n, weight in enumerate(weights):
        acc += weight * dot(coup[1 + n], far[n][...])
    edges = jnp.sum(res[...] * acc, axis=0, keepdims=True)
    sums[...] = near[...] + two_rows(jnp.zeros(edges.shape, F32), edges)


def shards(right_side, node_diag, local_coup, block_cols, border_coup, border_send, border_rows):
    width, ncols = right_side.shape
    nblocks, _, bs, _ = local_coup.shape
    n_gx, n_gy, n_nd = (lax.axis_size(a) for a in AXES)
    assert n_nd == 2 and border_coup.shape[1] == 4 * SIDE
    gyi = lax.axis_index("gy")
    swap = [(0, 1), (1, 0)]
    right = [(i, (i + 1) % n_gx) for i in range(n_gx)]
    left = [(j, i) for i, j in right]
    up = [(i, i + 1) for i in range(n_gy - 1)]
    down = [(j, i) for i, j in up]
    facing = jnp.where(gyi == 0, 3, 2)
    slots = [("gx", right, 0), ("gx", left, 1)]
    weights = [2.0]
    if n_gy == 2:
        slots.insert(0, ("gy", swap, facing))
        weights.insert(0, 1.0)
    elif n_gy > 2:
        slots.insert(0, ("gy", up, 2))
        slots.append(("gy", down, 3))
        weights.insert(0, 2.0)
    early = len(weights)
    takes = jnp.stack([jnp.asarray(t, jnp.int32) for _, _, t in slots])
    gives = jnp.stack([jnp.asarray(facing if t is facing else t ^ 1, jnp.int32) for _, _, t in slots])
    ndi = lax.axis_index("nd").astype(jnp.int32)
    border = border_coup[0]

    pay_shape = (width + bs + TAIL, ncols)
    packed = pl.pallas_call(
        pack_kernel,
        name="pack",
        in_specs=[smem()] * 3 + [pl.BlockSpec(memory_space=pl.ANY)] * 2,
        out_specs=[vmem()] * early,
        out_shape=[pltpu.VMEM(pay_shape, F32)] * early,
        scratch_shapes=[pltpu.SemaphoreType.DMA((early, SIDE + 1))],
        compiler_params=pltpu.CompilerParams(vmem_limit_bytes=LIMIT),
    )(border_send, border_rows, gives, *[pltpu.with_memory_space_constraint(a, pltpu.HBM) for a in (right_side, border)])
    mate = lax.ppermute(right_side, "nd", swap)
    late = len(slots) - early
    own, pair, *rest = call(partial(prep_kernel, early), "prep", 5, [(width, width)] * 2 + [pay_shape] * late, flops=1 << 24)(
        block_cols, ndi[None], border_send, border_rows, gives, packed[0], node_diag.reshape(1, width), local_coup, border
    )
    pays = [lax.ppermute(pay, axis, perm) for pay, (axis, perm, _) in zip([*packed, *rest], slots)]
    mate_pair = lax.ppermute(pair, "nd", swap)

    part, coup, first = call(partial(half_kernel, weights), "half", 3, [(width, ncols), (1 + early, width, width), (TAIL, ncols)])(
        border_send, border_rows, takes, right_side, own, pair, mate, mate_pair, border, *pays[:early]
    )
    first = axis_sum(first, AXES)
    (image,) = call(partial(rest_kernel, early), "rest", 3, [(width, ncols)], scratch=[pltpu.VMEM((width, width), F32)])(
        border_send, border_rows, takes, part, border, *pays[early:]
    )
    (res,) = call(step_kernel, "step", 0, [(width, ncols)])(first, right_side, image)
    far = [lax.ppermute(res, axis, perm) for axis, perm, _ in slots[:early]]
    mate_r = lax.ppermute(res, "nd", swap)
    (near,) = call(near_kernel, "near", 0, [(TAIL, ncols)])(res, mate_r, own, coup)
    (second,) = call(partial(far_kernel, weights), "far", 0, [(TAIL, ncols)])(near, res, coup, *far)
    second = axis_sum(second, AXES)
    norm, curve = first[0:1], first[1:2]
    ratio = second[0:1] / norm
    last = second[0:1] / (second[1:2] - ratio * ratio * curve)
    return (norm / curve + last * ratio) * right_side + last * res


def solution(mesh):
    blocks = P(("var", "gx", "gy", "nd"))
    tables = P(AXES)
    in_specs = (blocks, blocks, blocks, tables, blocks, tables, tables)
    return jax.shard_map(shards, mesh=mesh, in_specs=in_specs, out_specs=blocks, check_vma=False)
```

```python
from functools import partial

import jax
import jax.numpy as jnp
from jax import lax
from jax.experimental import pallas as pl
from jax.experimental.pallas import tpu as pltpu
from jax.sharding import PartitionSpec as P

F32 = jnp.float32
HP = lax.Precision.HIGHEST
AXES = ("gx", "gy", "nd")
SIDE = 2
LIMIT = 8 << 20
TAIL = 8


def vmem():
    return pl.BlockSpec(memory_space=pltpu.VMEM)


def smem():
    return pl.BlockSpec(memory_space=pltpu.SMEM)


def call(kernel, name, tables, shapes, flops=None, scratch=()):
    def run(*args):
        args = list(args[:tables]) + [pltpu.with_memory_space_constraint(a, pltpu.VMEM) for a in args[tables:]]
        return pl.pallas_call(
            kernel,
            name=name,
            in_specs=[smem()] * tables + [vmem()] * (len(args) - tables),
            out_specs=[vmem()] * len(shapes),
            out_shape=[pltpu.VMEM(shape, F32) for shape in shapes],
            scratch_shapes=scratch,
            compiler_params=pltpu.CompilerParams(vmem_limit_bytes=LIMIT),
            cost_estimate=flops and pl.CostEstimate(flops=flops, bytes_accessed=1 << 20, transcendentals=0),
        )(*args)

    return run


def join(state):
    count = lax.axis_size(AXES)
    assert count & (count - 1) == 0
    step = 1
    while step < count:
        masks = [m * step for m in (1, 2, 3) if m * step < count]
        others = [lax.ppermute(state, AXES, [(i, i ^ m) for i in range(count)]) for m in masks]
        (state,) = call(merge_kernel, "merge", 0, [state.shape])(state, *others)
        step *= 4
    return state


def prep_kernel(cols, sides, packed, diag, local, own, pair):
    nblocks, nonzeros, bs, _ = local.shape
    width = nblocks * bs
    patch_len = 2 * nblocks
    base = sides[0] * nblocks
    own[...] = jnp.zeros(own.shape, F32)
    pair[...] = jnp.zeros((width, width), F32)
    for b in range(nblocks):
        for k in range(nonzeros):
            spot = lax.rem(cols[b, k] - base + patch_len, patch_len)
            block = local[b, k]
            for c in range(nblocks):

                @pl.when(spot == c)
                def _():
                    own[pl.ds(b * bs, bs), pl.ds(c * bs, bs)] += block

                @pl.when(spot == c + nblocks)
                def _():
                    pair[pl.ds(b * bs, bs), pl.ds(c * bs, bs)] += block

    lower = own[...]
    here = lax.broadcasted_iota(jnp.int32, (width, width), 0)
    there = lax.broadcasted_iota(jnp.int32, (width, width), 1)
    own[...] = lower + lower.T + jnp.where(here == there, diag[...], 0.0)


def pack_kernel(send, rows, gives, field, border, *refs):
    *pays, sems = refs
    width = field.shape[0]
    bs = border.shape[1]
    copies = []
    for n, pay in enumerate(pays):
        copies.append(pltpu.make_async_copy(field, pay.at[pl.ds(0, width), :], sems.at[n, SIDE]))
        for s in range(SIDE):
            block = pay.at[pl.ds(width, bs), pl.ds(s * bs, bs)]
            copies.append(pltpu.make_async_copy(border.at[gives[n] * SIDE + s], block, sems.at[n, s]))
    for copy in copies:
        copy.start()
    lane = lax.broadcasted_iota(jnp.int32, (TAIL, SIDE * bs), 1)
    for n, pay in enumerate(pays):
        give = gives[n]
        tail = jnp.zeros(lane.shape, F32)
        for s in range(SIDE):
            tail = jnp.where(lane == s, rows[0, give * SIDE + s].astype(F32), tail)
            sent = send[0, (give ^ 1) * SIDE + s].astype(F32)
            tail = jnp.where(lane == SIDE + s, sent, tail)
        pay[pl.ds(width + bs, TAIL), :] = tail
    for copy in copies:
        copy.wait()


def build_edge(coup, take, send, rows, border, pay):
    bs = border.shape[1]
    width = coup.shape[0]
    other = take ^ 1
    coup[...] = jnp.zeros((width, width), F32)
    tail = pay[pl.ds(width + bs, TAIL), :]
    for s in range(SIDE):
        from_row = tail[0:1, s : s + 1]
        from_send = tail[0:1, SIDE + s : SIDE + s + 1]
        block = border[take * SIDE + s]
        turned = pay[pl.ds(width, bs), pl.ds(s * bs, bs)].T
        at = pl.multiple_of(rows[0, take * SIDE + s] * bs, bs)
        bt = pl.multiple_of(send[0, other * SIDE + s] * bs, bs)
        for c in range(width // bs):
            coup[pl.ds(at, bs), pl.ds(c * bs, bs)] += jnp.where(from_send == c, block, 0.0)
            coup[pl.ds(bt, bs), pl.ds(c * bs, bs)] += jnp.where(from_row == c, turned, 0.0)


def dot(a, b):
    return jnp.dot(a, b, precision=HP, preferred_element_type=F32)


def half_kernel(weights, send, rows, takes, field, own, pair, mate, mate_pair, border, *refs):
    *pays, image, once, coup = refs
    width = field.shape[0]
    coup[0] = pair[...] + mate_pair[...].T
    acc = dot(own[...], field[...]) + dot(coup[0], mate[...])
    single = acc
    for n, pay in enumerate(pays):
        build_edge(coup.at[1 + n], takes[n], send, rows, border, pay)
        edge = dot(coup[1 + n], pay[pl.ds(0, width), :])
        acc += edge
        single += weights[n] * edge
    image[...] = acc
    once[...] = single


def rest_kernel(skip, send, rows, takes, part, border, *refs):
    *pays, image, coup = refs
    width = part.shape[0]
    acc = part[...]
    for n, pay in enumerate(pays):
        build_edge(coup, takes[skip + n], send, rows, border, pay)
        acc += dot(coup[...], pay[pl.ds(0, width), :])
    image[...] = acc


def col_sum(a, b):
    return jnp.sum(a * b, axis=0, keepdims=True)


def near_kernel(field, image, once, mate, mate_w, own, coup, part, state):
    b = field[...]
    norm = col_sum(b, b)
    c = jnp.where(norm > 0.0, col_sum(b, image[...]) / jnp.where(norm > 0.0, norm, 1.0), 0.0)
    g = image[...] - c * b
    part[...] = dot(own[...], g) + dot(coup[0], mate_w[...] - c * mate[...])
    rows = [norm, c, col_sum(g, g), jnp.zeros_like(c), -col_sum(g, once[...]), col_sum(b, once[...])]
    line = lax.broadcasted_iota(jnp.int32, state.shape, 0)
    state[...] = sum(jnp.where(line == n, row, 0.0) for n, row in enumerate(rows))


def far_kernel(weights, field, image, part, near, coup, *refs):
    count = len(weights)
    pays, images, state = refs[:count], refs[count : 2 * count], refs[2 * count]
    width = field.shape[0]
    b = field[...]
    c = near[1:2, :]
    acc = part[...]
    for n, weight in enumerate(weights):
        acc += weight * dot(coup[1 + n], images[n][...] - c * pays[n][pl.ds(0, width), :])
    line = lax.broadcasted_iota(jnp.int32, state.shape, 0)
    flat = col_sum(image[...] - c * b, acc)
    slope = -col_sum(b, acc)
    state[...] = near[...] + jnp.where(line == 3, flat, jnp.where(line == 4, slope, 0.0))


def merge_kernel(*refs):
    *states, out = refs
    norm = sum(s[0:1, :] for s in states)
    base = states[0][1:2, :]
    shift = sum(s[0:1, :] * (s[1:2, :] - base) for s in states)
    c = base + jnp.where(norm > 0.0, shift / jnp.where(norm > 0.0, norm, 1.0), 0.0)
    rows = [norm, c] + [jnp.zeros_like(c)] * 4
    for s in states:
        d = c - s[1:2, :]
        flat, slope, bend = s[3:4, :], s[4:5, :], s[5:6, :]
        rows[2] += s[2:3, :] + s[0:1, :] * d * d
        rows[3] += flat + (slope + bend * d) * d
        rows[4] += slope + 2.0 * bend * d
        rows[5] += bend
    line = lax.broadcasted_iota(jnp.int32, out.shape, 0)
    out[...] = sum(jnp.where(line == n, row, 0.0) for n, row in enumerate(rows))


def shards(right_side, node_diag, local_coup, block_cols, border_coup, border_send, border_rows):
    width, ncols = right_side.shape
    nblocks, _, bs, _ = local_coup.shape
    n_gx, n_gy, n_nd = (lax.axis_size(a) for a in AXES)
    assert n_nd == 2 and border_coup.shape[1] == 4 * SIDE
    gyi = lax.axis_index("gy")
    swap = [(0, 1), (1, 0)]
    right = [(i, (i + 1) % n_gx) for i in range(n_gx)]
    left = [(j, i) for i, j in right]
    up = [(i, i + 1) for i in range(n_gy - 1)]
    down = [(j, i) for i, j in up]
    facing = jnp.where(gyi == 0, 3, 2)
    slots = [("gx", right, 0), ("gx", left, 1)]
    weights = [2.0]
    if n_gy == 2:
        slots.insert(1, ("gy", swap, facing))
        weights.append(1.0)
    elif n_gy > 2:
        slots.insert(1, ("gy", up, 2))
        slots.append(("gy", down, 3))
        weights.append(2.0)
    early = len(weights)
    takes = jnp.stack([jnp.asarray(t, jnp.int32) for _, _, t in slots])
    gives = jnp.stack([jnp.asarray(facing if t is facing else t ^ 1, jnp.int32) for _, _, t in slots])
    ndi = lax.axis_index("nd").astype(jnp.int32)
    border = border_coup[0]

    packed = pl.pallas_call(
        pack_kernel,
        name="pack",
        in_specs=[smem()] * 3 + [pl.BlockSpec(memory_space=pl.ANY)] * 2,
        out_specs=[vmem()] * len(slots),
        out_shape=[pltpu.VMEM((width + bs + TAIL, ncols), F32)] * len(slots),
        scratch_shapes=[pltpu.SemaphoreType.DMA((len(slots), SIDE + 1))],
        compiler_params=pltpu.CompilerParams(vmem_limit_bytes=LIMIT),
    )(border_send, border_rows, gives, *[pltpu.with_memory_space_constraint(a, pltpu.HBM) for a in (right_side, border)])
    pays = [lax.ppermute(pay, axis, perm) for pay, (axis, perm, _) in zip(packed, slots)]
    mate = lax.ppermute(right_side, "nd", swap)
    own, pair = call(prep_kernel, "prep", 2, [(width, width)] * 2, flops=1 << 24)(
        block_cols, ndi[None], packed[0], node_diag.reshape(1, width), local_coup
    )
    mate_pair = lax.ppermute(pair, "nd", swap)

    part, once, coup = call(partial(half_kernel, weights), "half", 3, [(width, ncols)] * 2 + [(1 + early, width, width)])(
        border_send, border_rows, takes, right_side, own, pair, mate, mate_pair, border, *pays[:early]
    )
    (image,) = call(partial(rest_kernel, early), "rest", 3, [(width, ncols)], scratch=[pltpu.VMEM((width, width), F32)])(
        border_send, border_rows, takes, part, border, *pays[early:]
    )
    images = [lax.ppermute(image, axis, perm) for axis, perm, _ in slots[:early]]
    mate_w = lax.ppermute(image, "nd", swap)
    part, state = call(near_kernel, "near", 0, [(width, ncols), (TAIL, ncols)])(
        right_side, image, once, mate, mate_w, own, coup
    )
    (state,) = call(partial(far_kernel, weights), "far", 0, [(TAIL, ncols)])(
        right_side, image, part, state, coup, *pays[:early], *images
    )
    norm, c, size, form = (row[None] for row in join(state)[:4])
    ratio = size / (c * c * norm)
    last = size / (form - ratio * ratio * c * c * c * norm)
    return ((1.0 + last * c * (1.0 + ratio)) / c) * right_side - (last / c) * image


def solution(mesh):
    blocks = P(("var", "gx", "gy", "nd"))
    tables = P(AXES)
    in_specs = (blocks, blocks, blocks, tables, blocks, tables, tables)
    return jax.shard_map(shards, mesh=mesh, in_specs=in_specs, out_specs=blocks, check_vma=False)
```

```python
from functools import partial

import jax
import jax.numpy as jnp
from jax import lax
from jax.experimental import pallas as pl
from jax.experimental.pallas import tpu as pltpu
from jax.sharding import PartitionSpec as P

F32 = jnp.float32
BF16 = jnp.bfloat16
AXES = ("gx", "gy", "nd")
SIDE = 2
LIMIT = 8 << 20
TAIL = 8


def vmem():
    return pl.BlockSpec(memory_space=pltpu.VMEM)


def call(kernel, name, shapes, scratch=(), flops=None):
    def run(*args):
        args = [pltpu.with_memory_space_constraint(a, pltpu.VMEM) for a in args]
        return pl.pallas_call(
            kernel,
            name=name,
            in_specs=[vmem()] * len(args),
            out_specs=[vmem()] * len(shapes),
            out_shape=[pltpu.VMEM(shape, F32) for shape in shapes],
            scratch_shapes=scratch,
            compiler_params=pltpu.CompilerParams(vmem_limit_bytes=LIMIT),
            cost_estimate=flops and pl.CostEstimate(flops=flops, bytes_accessed=1 << 20, transcendentals=0),
        )(*args)

    return run


def join(state):
    count = lax.axis_size(AXES)
    assert count & (count - 1) == 0
    step = 1
    while step < count:
        masks = [m * step for m in (1, 2, 3) if m * step < count]
        others = [lax.ppermute(state, AXES, [(i, i ^ m) for i in range(count)]) for m in masks]
        (state,) = call(merge_kernel, "merge", [state.shape])(state, *others)
        step *= 4
    return state


def split(a):
    high = a.astype(BF16)
    return high, (a - high.astype(F32)).astype(BF16)


def dot(a, b):
    (ah, al), (bh, bl) = split(a), split(b)
    mul = partial(jnp.dot, preferred_element_type=F32)
    return mul(ah, bh) + (mul(ah, bl) + mul(al, bh))


def col_sum(a, b):
    return jnp.sum(a * b, axis=0, keepdims=True)


def stack_rows(rows, shape):
    line = lax.broadcasted_iota(jnp.int32, shape, 0)
    return sum(jnp.where(line == n, row, 0.0) for n, row in rows)


def pack_kernel(gives, marks, field, border, send, rows, *refs):
    *pays, sems, table, table_sems = refs
    width = field.shape[0]
    bs = border.shape[1]
    tables = [pltpu.make_async_copy(ref, table.at[n], table_sems.at[n]) for n, ref in enumerate((rows, send))]
    copies = []
    for n, pay in enumerate(pays):
        give = marks[0] if gives[n] is None else gives[n]
        copies.append(pltpu.make_async_copy(field, pay.at[pl.ds(0, width), :], sems.at[n, SIDE]))
        for s in range(SIDE):
            block = pay.at[pl.ds(width, bs), pl.ds(s * bs, bs)]
            copies.append(pltpu.make_async_copy(border.at[give * SIDE + s], block, sems.at[n, s]))
    for copy in tables + copies:
        copy.start()
    for copy in tables:
        copy.wait()
    count = table.shape[2]
    for pay in pays:
        for n in range(2):
            pay[pl.ds(width + bs + n, 1), pl.ds(0, count)] = table[n].astype(F32)
    for copy in copies:
        copy.wait()


def prep_kernel(cols, marks, diag, local, packed, own, pair):
    nblocks, nonzeros, bs, _ = local.shape
    width = nblocks * bs
    patch_len = 2 * nblocks
    base = marks[1] * nblocks
    own[...] = jnp.zeros((width, width), F32)
    pair[...] = jnp.zeros((width, width), F32)
    for b in range(nblocks):
        for k in range(nonzeros):
            spot = lax.rem(cols[b, k] - base + patch_len, patch_len)
            block = local[b, k]
            for c in range(nblocks):

                @pl.when(spot == c)
                def _():
                    own[pl.ds(b * bs, bs), pl.ds(c * bs, bs)] += block

                @pl.when(spot == c + nblocks)
                def _():
                    pair[pl.ds(b * bs, bs), pl.ds(c * bs, bs)] += block

    lower = own[...]
    here = lax.broadcasted_iota(jnp.int32, (width, width), 0)
    there = lax.broadcasted_iota(jnp.int32, (width, width), 1)
    own[...] = lower + lower.T + jnp.where(here == there, diag[...], 0.0)


def edge(take, mine, pay, border):
    bs = border.shape[1]
    width = pay.shape[0] - bs - TAIL
    options = [take] if isinstance(take, int) else [2, 3]

    def number(ref, line, flip, s):
        at = [(t ^ flip) * SIDE + s for t in options]
        found = [ref[pl.ds(width + bs + line, 1), pl.ds(i, 1)] for i in at]
        return found[0] if len(found) == 1 else jnp.where(take == options[0], found[0], found[1])

    blocks = [[0.0] * (width // bs) for _ in range(width // bs)]
    for s in range(SIDE):
        pairs = [
            (border[take * SIDE + s], number(mine, 0, 0, s), number(pay, 1, 0, s)),
            (pay[pl.ds(width, bs), pl.ds(s * bs, bs)].T, number(mine, 1, 1, s), number(pay, 0, 1, s)),
        ]
        for block, to, at in pairs:
            for i, line in enumerate(blocks):
                for j in range(len(line)):
                    line[j] = line[j] + jnp.where((to == i) & (at == j), block, 0.0)
    return jnp.concatenate([jnp.concatenate(line, axis=1) for line in blocks], axis=0)


def base_kernel(mine, own, pair, mate, mate_pair, image, coup):
    width = mate.shape[0]
    coup[...] = pair[...] + mate_pair[...].T
    image[...] = dot(own[...], mine[pl.ds(0, width), :]) + dot(coup[...], mate[...])


def left_kernel(mine, part, border, pay, image, once, coup):
    width = part.shape[0]
    coup[...] = edge(0, mine, pay, border)
    term = dot(coup[...], pay[pl.ds(0, width), :])
    image[...] = part[...] + term
    once[...] = part[...] + 2.0 * term


def gy_kernel(take, weight, marks, mine, part, single, border, pay, image, once, coup):
    width = part.shape[0]
    coup[...] = edge(marks[0] if take is None else take, mine, pay, border)
    term = dot(coup[...], pay[pl.ds(0, width), :])
    image[...] = part[...] + term
    once[...] = single[...] + weight * term


def right_kernel(mine, part, border, pay, image):
    width = part.shape[0]
    image[...] = part[...] + dot(edge(1, mine, pay, border), pay[pl.ds(0, width), :])


def near_kernel(field, image, once, mate, mate_w, own, coup, part, state):
    b = field[...]
    norm = col_sum(b, b)
    c = jnp.where(norm > 0.0, col_sum(b, image[...]) / jnp.where(norm > 0.0, norm, 1.0), 0.0)
    g = image[...] - c * b
    part[...] = dot(own[...], g) + dot(coup[...], mate_w[...] - c * mate[...])
    rows = [(0, norm), (1, c), (2, col_sum(g, g)), (4, -col_sum(g, once[...])), (5, col_sum(b, once[...]))]
    state[...] = stack_rows(rows, state.shape)


def far_kernel(weights, field, image, part, near, *refs):
    count = len(weights)
    coups, pays, fars, state = refs[:count], refs[count : 2 * count], refs[2 * count : -1], refs[-1]
    width = field.shape[0]
    b = field[...]
    c = near[1:2, :]
    acc = part[...]
    for weight, coup, pay, far in zip(weights, coups, pays, fars):
        acc += weight * dot(coup[...], far[...] - c * pay[pl.ds(0, width), :])
    state[...] = near[...] + stack_rows([(3, col_sum(image[...] - c * b, acc)), (4, -col_sum(b, acc))], state.shape)


def merge_kernel(*refs):
    *states, out = refs
    norm = sum(s[0:1, :] for s in states)
    base = states[0][1:2, :]
    shift = sum(s[0:1, :] * (s[1:2, :] - base) for s in states)
    c = base + jnp.where(norm > 0.0, shift / jnp.where(norm > 0.0, norm, 1.0), 0.0)
    size, flat, slope, bend = (jnp.zeros_like(c) for _ in range(4))
    for s in states:
        d = c - s[1:2, :]
        size += s[2:3, :] + s[0:1, :] * d * d
        flat += s[3:4, :] + (s[4:5, :] + s[5:6, :] * d) * d
        slope += s[4:5, :] + 2.0 * s[5:6, :] * d
        bend += s[5:6, :]
    out[...] = stack_rows(list(enumerate([norm, c, size, flat, slope, bend])), out.shape)


def shards(right_side, node_diag, local_coup, block_cols, border_coup, border_send, border_rows):
    width, ncols = right_side.shape
    nblocks, _, bs, _ = local_coup.shape
    n_gx, n_gy, n_nd = (lax.axis_size(a) for a in AXES)
    assert n_nd == 2 and border_coup.shape[1] == 4 * SIDE
    swap = [(0, 1), (1, 0)]
    right = [(i, (i + 1) % n_gx) for i in range(n_gx)]
    left = [(j, i) for i, j in right]
    up = [(i, i + 1) for i in range(n_gy - 1)]
    down = [(j, i) for i, j in up]
    facing = jnp.where(lax.axis_index("gy") == 0, 3, 2).astype(jnp.int32)
    if n_gy == 2:
        sides = [(swap, None, 1.0)]
    elif n_gy > 2:
        sides = [(up, 2, 2.0), (down, 3, 0.0)]
    else:
        sides = []
    sends = [("gx", right), ("gx", left)] + [("gy", perm) for perm, _, _ in sides]
    gives = [1, 0] + [None if t is None else t ^ 1 for _, t, _ in sides]
    marks = jnp.stack([facing, lax.axis_index("nd").astype(jnp.int32)])
    border = border_coup[0]

    def smem(n):
        return [pl.BlockSpec(memory_space=pltpu.SMEM)] * n

    pay_shape = (width + bs + TAIL, ncols)
    nsends = len(sends)
    packed = pl.pallas_call(
        partial(pack_kernel, gives),
        name="pack",
        in_specs=smem(1) + [pl.BlockSpec(memory_space=pl.ANY)] * 4,
        out_specs=[vmem()] * nsends,
        out_shape=[pltpu.VMEM(pay_shape, F32)] * nsends,
        scratch_shapes=[
            pltpu.SemaphoreType.DMA((nsends, SIDE + 1)),
            pltpu.VMEM((2, 1, 4 * SIDE), jnp.int32),
            pltpu.SemaphoreType.DMA((2,)),
        ],
        compiler_params=pltpu.CompilerParams(vmem_limit_bytes=LIMIT),
    )(marks, *[pltpu.with_memory_space_constraint(a, pltpu.HBM) for a in (right_side, border, border_send, border_rows)])
    pays = [lax.ppermute(pay, axis, perm) for pay, (axis, perm) in zip(packed, sends)]
    mine = packed[0]
    mate = lax.ppermute(right_side, "nd", swap)

    def tabled(kernel, name, tables, shapes, flops=None):
        def run(*args):
            args = list(args[:tables]) + [pltpu.with_memory_space_constraint(a, pltpu.VMEM) for a in args[tables:]]
            return pl.pallas_call(
                kernel,
                name=name,
                in_specs=smem(tables) + [vmem()] * (len(args) - tables),
                out_specs=[vmem()] * len(shapes),
                out_shape=[pltpu.VMEM(shape, F32) for shape in shapes],
                compiler_params=pltpu.CompilerParams(vmem_limit_bytes=LIMIT),
                cost_estimate=flops and pl.CostEstimate(flops=flops, bytes_accessed=1 << 20, transcendentals=0),
            )(*args)

        return run

    field, square = (width, ncols), (width, width)
    own, pair = tabled(prep_kernel, "prep", 2, [square] * 2, 1 << 24)(
        block_cols, marks, node_diag.reshape(1, width), local_coup, mine
    )
    mate_pair = lax.ppermute(pair, "nd", swap)

    part, coup = call(base_kernel, "base", [field, square])(mine, own, pair, mate, mate_pair)
    part, once, left_coup = call(left_kernel, "left", [field, field, square])(mine, part, border, pays[0])
    side_coup = []
    for (_, take, weight), pay in zip(sides, pays[2:]):
        part, once, block = tabled(partial(gy_kernel, take, weight), "gy", 1, [field, field, square])(
            marks, mine, part, once, border, pay
        )
        side_coup.append(block)
    (image,) = call(right_kernel, "right", [field])(mine, part, border, pays[1])

    used = [(2.0, left_coup, pays[0], ("gx", right))]
    if sides:
        used.append((sides[0][2], side_coup[0], pays[2], ("gy", sides[0][0])))
    weights, coups, near_b, perms = zip(*used)
    fars = [lax.ppermute(image, axis, perm) for axis, perm in perms]
    mate_w = lax.ppermute(image, "nd", swap)
    part, state = call(near_kernel, "near", [field, (TAIL, ncols)])(right_side, image, once, mate, mate_w, own, coup)
    (state,) = call(partial(far_kernel, weights), "far", [(TAIL, ncols)])(
        right_side, image, part, state, *coups, *near_b, *fars
    )
    norm, c, size, form = (row[None] for row in join(state)[:4])
    ratio = size / (c * c * norm)
    last = size / (form - ratio * ratio * c * c * c * norm)
    return ((1.0 + last * c * (1.0 + ratio)) / c) * right_side - (last / c) * image


def solution(mesh):
    blocks = P(("var", "gx", "gy", "nd"))
    tables = P(AXES)
    in_specs = (blocks, blocks, blocks, tables, blocks, tables, tables)
    return jax.shard_map(shards, mesh=mesh, in_specs=in_specs, out_specs=blocks, check_vma=False)
```

```python
from functools import partial

import jax
import jax.numpy as jnp
from jax import lax
from jax.experimental import pallas as pl
from jax.experimental.pallas import tpu as pltpu
from jax.sharding import PartitionSpec as P

F32 = jnp.float32
BF16 = jnp.bfloat16
AXES = ("gx", "gy", "nd")
SIDE = 2
LIMIT = 8 << 20
TAIL = 8


def vmem():
    return pl.BlockSpec(memory_space=pltpu.VMEM)


def call(kernel, name, shapes, scratch=(), flops=None):
    def run(*args):
        args = [pltpu.with_memory_space_constraint(a, pltpu.VMEM) for a in args]
        return pl.pallas_call(
            kernel,
            name=name,
            in_specs=[vmem()] * len(args),
            out_specs=[vmem()] * len(shapes),
            out_shape=[pltpu.VMEM(shape, F32) for shape in shapes],
            scratch_shapes=scratch,
            compiler_params=pltpu.CompilerParams(vmem_limit_bytes=LIMIT),
            cost_estimate=flops and pl.CostEstimate(flops=flops, bytes_accessed=1 << 20, transcendentals=0),
        )(*args)

    return run


def join(state):
    count = lax.axis_size(AXES)
    assert count & (count - 1) == 0
    step = 1
    while step < count:
        masks = [m * step for m in (1, 2, 3) if m * step < count]
        others = [lax.ppermute(state, AXES, [(i, i ^ m) for i in range(count)]) for m in masks]
        (state,) = call(merge_kernel, "merge", [state.shape])(state, *others)
        step *= 4
    return state


def split(a):
    high = a.astype(BF16)
    return high, (a - high.astype(F32)).astype(BF16)


def dot(a, b):
    (ah, al), (bh, bl) = split(a), split(b)
    mul = partial(jnp.dot, preferred_element_type=F32)
    return mul(ah, bh) + (mul(ah, bl) + mul(al, bh))


def col_sum(a, b):
    return jnp.sum(a * b, axis=0, keepdims=True)


def stack_rows(rows, shape):
    line = lax.broadcasted_iota(jnp.int32, shape, 0)
    return sum(jnp.where(line == n, row, 0.0) for n, row in rows)


def pack_kernel(gives, marks, field, border, send, rows, *refs):
    *pays, sems, table, table_sems = refs
    width = field.shape[0]
    bs = border.shape[1]
    tables = [pltpu.make_async_copy(ref, table.at[n], table_sems.at[n]) for n, ref in enumerate((rows, send))]
    copies = []
    for n, pay in enumerate(pays):
        give = marks[0] if gives[n] is None else gives[n]
        copies.append(pltpu.make_async_copy(field, pay.at[pl.ds(0, width), :], sems.at[n, SIDE]))
        for s in range(SIDE):
            block = pay.at[pl.ds(width, bs), pl.ds(s * bs, bs)]
            copies.append(pltpu.make_async_copy(border.at[give * SIDE + s], block, sems.at[n, s]))
    for copy in tables + copies:
        copy.start()
    for copy in tables:
        copy.wait()
    count = table.shape[2]
    for pay in pays:
        for n in range(2):
            pay[pl.ds(width + bs + n, 1), pl.ds(0, count)] = table[n].astype(F32)
        pay[pl.ds(width + bs + 2, 1), :] = jnp.full((1, pay.shape[1]), marks[0].astype(F32))
    for copy in copies:
        copy.wait()


def prep_kernel(cols, marks, diag, local, packed, own, pair):
    nblocks, nonzeros, bs, _ = local.shape
    width = nblocks * bs
    patch_len = 2 * nblocks
    base = marks[1] * nblocks
    own[...] = jnp.zeros((width, width), F32)
    pair[...] = jnp.zeros((width, width), F32)
    for b in range(nblocks):
        for k in range(nonzeros):
            spot = lax.rem(cols[b, k] - base + patch_len, patch_len)
            block = local[b, k]
            for c in range(nblocks):

                @pl.when(spot == c)
                def _():
                    own[pl.ds(b * bs, bs), pl.ds(c * bs, bs)] += block

                @pl.when(spot == c + nblocks)
                def _():
                    pair[pl.ds(b * bs, bs), pl.ds(c * bs, bs)] += block

    lower = own[...]
    here = lax.broadcasted_iota(jnp.int32, (width, width), 0)
    there = lax.broadcasted_iota(jnp.int32, (width, width), 1)
    own[...] = lower + lower.T + jnp.where(here == there, diag[...], 0.0)


def edge(take, mine, pay, border):
    bs = border.shape[1]
    width = pay.shape[0] - bs - TAIL
    known = isinstance(take, int)

    def pick(of):
        return of(take) if known else jnp.where(take == 2.0, of(2), of(3))

    def number(ref, line, t):
        return ref[pl.ds(width + bs + line, 1), pl.ds(t * SIDE + s, 1)]

    blocks = [[0.0] * (width // bs) for _ in range(width // bs)]
    for s in range(SIDE):
        turned = pay[pl.ds(width, bs), pl.ds(s * bs, bs)].T
        pairs = [
            (pick(lambda t: border[t * SIDE + s]), pick(lambda t: number(mine, 0, t)), pick(lambda t: number(pay, 1, t))),
            (turned, pick(lambda t: number(mine, 1, t ^ 1)), pick(lambda t: number(pay, 0, t ^ 1))),
        ]
        for block, to, at in pairs:
            for i, line in enumerate(blocks):
                for j in range(len(line)):
                    line[j] = line[j] + jnp.where((to == i) & (at == j), block, 0.0)
    return jnp.concatenate([jnp.concatenate(line, axis=1) for line in blocks], axis=0)


def base_kernel(mine, own, pair, mate, mate_pair, image, coup):
    width = mate.shape[0]
    coup[...] = pair[...] + mate_pair[...].T
    image[...] = dot(own[...], mine[pl.ds(0, width), :]) + dot(coup[...], mate[...])


def left_kernel(mine, part, border, pay, image, once, coup, back):
    width = part.shape[0]
    coup[...] = edge(0, mine, pay, border)
    term = dot(coup[...], pay[pl.ds(0, width), :])
    image[...] = part[...] + term
    once[...] = part[...] + 2.0 * term
    back[...] = dot(coup[...].T, mine[pl.ds(0, width), :])


def turn(mine, width):
    toward = mine[pl.ds(mine.shape[0] - TAIL + 2, 1), :]
    column = lax.broadcasted_iota(jnp.int32, toward.shape, 1)
    return jnp.where((toward == 3.0) == (column < toward.shape[1] // 2), 1.0, 0.0)


def gy_kernel(take, weight, mine, part, single, border, pay, image, once, coup):
    width = coup.shape[0]
    toward = mine[pl.ds(mine.shape[0] - TAIL + 2, 1), pl.ds(0, 1)]
    coup[...] = edge(toward if take is None else take, mine, pay, border)
    term = dot(coup[...], pay[pl.ds(0, width), :])
    image[pl.ds(0, width), :] = part[pl.ds(0, width), :] + term
    image[pl.ds(width, TAIL), :] = jnp.zeros((TAIL, term.shape[1]), F32)
    scale = weight * turn(mine, width) if take is None else weight
    once[...] = single[...] + scale * term


def right_kernel(mine, part, border, pay, image, half):
    width = image.shape[0]
    full = part[pl.ds(0, width), :] + dot(edge(1, mine, pay, border), pay[pl.ds(0, width), :])
    image[...] = full
    middle = full.shape[1] // 2
    toward = mine[pl.ds(mine.shape[0] - TAIL + 2, 1), pl.ds(0, 1)]
    half[...] = jnp.where(toward == 3.0, full[:, middle:], full[:, :middle])


def near_kernel(field, image, once, mate, mate_w, own, coup, pay, back, part, lift, state):
    b = field[...]
    norm = col_sum(b, b)
    c = jnp.where(norm > 0.0, col_sum(b, image[...]) / jnp.where(norm > 0.0, norm, 1.0), 0.0)
    g = image[...] - c * b
    part[...] = dot(own[...], g) + dot(coup[...], mate_w[...] - c * mate[...])
    lift[...] = back[...] - c * pay[pl.ds(0, b.shape[0]), :]
    rows = [(0, norm), (1, c), (2, col_sum(g, g)), (4, -col_sum(g, once[...])), (5, col_sum(b, once[...]))]
    state[...] = stack_rows(rows, state.shape)


def far_kernel(take, field, image, part, near, lift, coup, left, *refs):
    *sides, state = refs
    width = field.shape[0]
    b = field[...]
    c = near[1:2, :]
    acc = part[...] + 2.0 * dot(coup[...], left[pl.ds(0, width), :] + lift[...])
    if sides:
        mine, coup_gy, pay, side = sides
        if take is None:
            toward = mine[pl.ds(mine.shape[0] - TAIL + 2, 1), pl.ds(0, 1)]
            middle = b.shape[1] // 2
            shift = c * pay[pl.ds(0, width), :]
            term = dot(coup_gy[...], side[...] - jnp.where(toward == 3.0, shift[:, :middle], shift[:, middle:]))
            acc += 2.0 * turn(mine, width) * jnp.concatenate([term, term], axis=1)
        else:
            acc += 2.0 * dot(coup_gy[...], side[...] - c * pay[pl.ds(0, width), :])
    state[...] = near[...] + stack_rows([(3, col_sum(image[...] - c * b, acc)), (4, -col_sum(b, acc))], state.shape)


def merge_kernel(*refs):
    *states, out = refs
    norm = sum(s[0:1, :] for s in states)
    base = states[0][1:2, :]
    shift = sum(s[0:1, :] * (s[1:2, :] - base) for s in states)
    c = base + jnp.where(norm > 0.0, shift / jnp.where(norm > 0.0, norm, 1.0), 0.0)
    size, flat, slope, bend = (jnp.zeros_like(c) for _ in range(4))
    for s in states:
        d = c - s[1:2, :]
        size += s[2:3, :] + s[0:1, :] * d * d
        flat += s[3:4, :] + (s[4:5, :] + s[5:6, :] * d) * d
        slope += s[4:5, :] + 2.0 * s[5:6, :] * d
        bend += s[5:6, :]
    out[...] = stack_rows(list(enumerate([norm, c, size, flat, slope, bend])), out.shape)


def shards(right_side, node_diag, local_coup, block_cols, border_coup, border_send, border_rows):
    width, ncols = right_side.shape
    nblocks, _, bs, _ = local_coup.shape
    n_gx, n_gy, n_nd = (lax.axis_size(a) for a in AXES)
    assert n_nd == 2 and border_coup.shape[1] == 4 * SIDE
    swap = [(0, 1), (1, 0)]
    right = [(i, (i + 1) % n_gx) for i in range(n_gx)]
    left = [(j, i) for i, j in right]
    up = [(i, i + 1) for i in range(n_gy - 1)]
    down = [(j, i) for i, j in up]
    facing = jnp.where(lax.axis_index("gy") == 0, 3, 2).astype(jnp.int32)
    if n_gy == 2:
        sides = [(swap, None, 2.0)]
    elif n_gy > 2:
        sides = [(up, 2, 2.0), (down, 3, 0.0)]
    else:
        sides = []
    sends = [("gx", right), ("gx", left)] + [("gy", perm) for perm, _, _ in sides]
    gives = [1, 0] + [None if t is None else t ^ 1 for _, t, _ in sides]
    marks = jnp.stack([facing, lax.axis_index("nd").astype(jnp.int32)])
    border = border_coup[0]

    def smem(n):
        return [pl.BlockSpec(memory_space=pltpu.SMEM)] * n

    pay_shape = (width + bs + TAIL, ncols)

    def pack(gives):
        count = len(gives)
        return pl.pallas_call(
            partial(pack_kernel, gives),
            name="pack",
            in_specs=smem(1) + [pl.BlockSpec(memory_space=pl.ANY)] * 4,
            out_specs=[vmem()] * count,
            out_shape=[pltpu.VMEM(pay_shape, F32)] * count,
            scratch_shapes=[
                pltpu.SemaphoreType.DMA((count, SIDE + 1)),
                pltpu.VMEM((2, 1, 4 * SIDE), jnp.int32),
                pltpu.SemaphoreType.DMA((2,)),
            ],
            compiler_params=pltpu.CompilerParams(vmem_limit_bytes=LIMIT),
        )(marks, *[pltpu.with_memory_space_constraint(a, pltpu.HBM) for a in (right_side, border, border_send, border_rows)])

    packed = [*pack(gives[:1]), *pack(gives[1:])]
    pays = [lax.ppermute(pay, axis, perm) for pay, (axis, perm) in zip(packed, sends)]
    mine = packed[0]
    mate = lax.ppermute(right_side, "nd", swap)

    def tabled(kernel, name, tables, shapes, flops=None):
        def run(*args):
            args = list(args[:tables]) + [pltpu.with_memory_space_constraint(a, pltpu.VMEM) for a in args[tables:]]
            return pl.pallas_call(
                kernel,
                name=name,
                in_specs=smem(tables) + [vmem()] * (len(args) - tables),
                out_specs=[vmem()] * len(shapes),
                out_shape=[pltpu.VMEM(shape, F32) for shape in shapes],
                compiler_params=pltpu.CompilerParams(vmem_limit_bytes=LIMIT),
                cost_estimate=flops and pl.CostEstimate(flops=flops, bytes_accessed=1 << 20, transcendentals=0),
            )(*args)

        return run

    field, square = (width, ncols), (width, width)
    own, pair = tabled(prep_kernel, "prep", 2, [square] * 2, 1 << 24)(
        block_cols, marks, node_diag.reshape(1, width), local_coup, mine
    )
    mate_pair = lax.ppermute(pair, "nd", swap)

    part, coup = call(base_kernel, "base", [field, square])(mine, own, pair, mate, mate_pair)
    part, once, left_coup, back = call(left_kernel, "left", [field, field, square, field])(mine, part, border, pays[0])
    side_coup = []
    for (_, take, weight), pay in zip(sides, pays[2:]):
        part, once, block = call(partial(gy_kernel, take, weight), "gy", [(width + TAIL, ncols), field, square])(mine, part, once, border, pay)
        side_coup.append(block)
    left_w = lax.ppermute(part, "gx", right)
    image, half = call(right_kernel, "right", [field, (width, ncols // 2)])(mine, part, border, pays[1])
    mate_w = lax.ppermute(image, "nd", swap)
    part, lift, state = call(near_kernel, "near", [field, field, (TAIL, ncols)])(
        right_side, image, once, mate, mate_w, own, coup, pays[0], back
    )
    far = []
    take = None
    if sides:
        perm, take, _ = sides[0]
        far = [mine, side_coup[0], pays[2], lax.ppermute(half if take is None else image, "gy", perm)]
    (state,) = call(partial(far_kernel, take), "far", [(TAIL, ncols)])(
        right_side, image, part, state, lift, left_coup, left_w, *far
    )
    state = join(state)
    norm, c, size, form = (row[None] for row in state[:4])
    ratio = size / (c * c * norm)
    last = size / (form - ratio * ratio * c * c * c * norm)
    return ((1.0 + last * c * (1.0 + ratio)) / c) * right_side - (last / c) * image


def solution(mesh):
    blocks = P(("var", "gx", "gy", "nd"))
    tables = P(AXES)
    in_specs = (blocks, blocks, blocks, tables, blocks, tables, tables)
    return jax.shard_map(shards, mesh=mesh, in_specs=in_specs, out_specs=blocks, check_vma=False)
```

```python
from functools import partial

import jax
import jax.numpy as jnp
from jax import lax
from jax.experimental import pallas as pl
from jax.experimental.pallas import tpu as pltpu
from jax.sharding import PartitionSpec as P

F32 = jnp.float32
BF16 = jnp.bfloat16
AXES = ("gx", "gy", "nd")
SIDE = 2
LIMIT = 8 << 20
EXTRA = 8
TAIL = 8


def vmem():
    return pl.BlockSpec(memory_space=pltpu.VMEM)


def call(kernel, name, shapes, scratch=(), flops=None):
    def run(*args):
        args = [pltpu.with_memory_space_constraint(a, pltpu.VMEM) for a in args]
        return pl.pallas_call(
            kernel,
            name=name,
            in_specs=[vmem()] * len(args),
            out_specs=[vmem()] * len(shapes),
            out_shape=[pltpu.VMEM(shape, F32) for shape in shapes],
            scratch_shapes=scratch,
            compiler_params=pltpu.CompilerParams(vmem_limit_bytes=LIMIT),
            cost_estimate=flops and pl.CostEstimate(flops=flops, bytes_accessed=1 << 20, transcendentals=0),
        )(*args)

    return run


def join(state):
    count = lax.axis_size(AXES)
    assert count & (count - 1) == 0
    step = 1
    while step < count:
        masks = [m * step for m in (1, 2, 3) if m * step < count]
        others = [lax.ppermute(state, AXES, [(i, i ^ m) for i in range(count)]) for m in masks]
        (state,) = call(merge_kernel, "merge", [state.shape])(state, *others)
        step *= 4
    return state


def split(a):
    high = a.astype(BF16)
    return high, (a - high.astype(F32)).astype(BF16)


def dot(a, b):
    (ah, al), (bh, bl) = split(a), split(b)
    mul = partial(jnp.dot, preferred_element_type=F32)
    return mul(ah, bh) + (mul(ah, bl) + mul(al, bh))


def mark_line(mine):
    return mine.shape[0] - EXTRA - TAIL + 2


def col_sum(a, b):
    return jnp.sum(a * b, axis=0, keepdims=True)


def stack_rows(rows, shape):
    line = lax.broadcasted_iota(jnp.int32, shape, 0)
    return sum(jnp.where(line == n, row, 0.0) for n, row in rows)


def pack_kernel(gives, marks, field, border, send, rows, *refs):
    *pays, sems, table, table_sems = refs
    width = field.shape[0]
    bs = border.shape[1]
    tables = [pltpu.make_async_copy(ref, table.at[n], table_sems.at[n]) for n, ref in enumerate((rows, send))]
    copies = []
    for n, pay in enumerate(pays):
        give = marks[0] if gives[n] is None else gives[n]
        copies.append(pltpu.make_async_copy(field, pay.at[pl.ds(0, width), :], sems.at[n, SIDE]))
        for s in range(SIDE):
            block = pay.at[pl.ds(width, bs), pl.ds(s * bs, bs)]
            copies.append(pltpu.make_async_copy(border.at[give * SIDE + s], block, sems.at[n, s]))
    for copy in tables + copies:
        copy.start()
    for copy in tables:
        copy.wait()
    count = table.shape[2]
    for pay in pays:
        for n in range(2):
            pay[pl.ds(width + bs + n, 1), pl.ds(0, count)] = table[n].astype(F32)
        pay[pl.ds(width + bs + 2, 1), :] = jnp.full((1, pay.shape[1]), marks[0].astype(F32))
    for copy in copies:
        copy.wait()


def prep_kernel(cols, marks, diag, local, packed, own, pair):
    nblocks, nonzeros, bs, _ = local.shape
    width = nblocks * bs
    patch_len = 2 * nblocks
    base = marks[1] * nblocks
    own[...] = jnp.zeros((width, width), F32)
    pair[...] = jnp.zeros((width, width), F32)
    for b in range(nblocks):
        for k in range(nonzeros):
            spot = lax.rem(cols[b, k] - base + patch_len, patch_len)
            block = local[b, k]
            for c in range(nblocks):

                @pl.when(spot == c)
                def _():
                    own[pl.ds(b * bs, bs), pl.ds(c * bs, bs)] += block

                @pl.when(spot == c + nblocks)
                def _():
                    pair[pl.ds(b * bs, bs), pl.ds(c * bs, bs)] += block

    lower = own[...]
    here = lax.broadcasted_iota(jnp.int32, (width, width), 0)
    there = lax.broadcasted_iota(jnp.int32, (width, width), 1)
    own[...] = lower + lower.T + jnp.where(here == there, diag[...], 0.0)


def edge(take, mine, pay, border):
    bs = border.shape[1]
    width = bs * (pay.shape[0] // bs - 1)
    known = isinstance(take, int)

    def pick(of):
        return of(take) if known else jnp.where(take == 2.0, of(2), of(3))

    def number(ref, line, t):
        return ref[pl.ds(width + bs + line, 1), pl.ds(t * SIDE + s, 1)]

    blocks = [[0.0] * (width // bs) for _ in range(width // bs)]
    for s in range(SIDE):
        turned = pay[pl.ds(width, bs), pl.ds(s * bs, bs)].T
        pairs = [
            (pick(lambda t: border[t * SIDE + s]), pick(lambda t: number(mine, 0, t)), pick(lambda t: number(pay, 1, t))),
            (turned, pick(lambda t: number(mine, 1, t ^ 1)), pick(lambda t: number(pay, 0, t ^ 1))),
        ]
        for block, to, at in pairs:
            for i, line in enumerate(blocks):
                for j in range(len(line)):
                    line[j] = line[j] + jnp.where((to == i) & (at == j), block, 0.0)
    return jnp.concatenate([jnp.concatenate(line, axis=1) for line in blocks], axis=0)


def base_kernel(mine, own, pair, mate, mate_pair, image, coup):
    width = mate.shape[0]
    coup[...] = pair[...] + mate_pair[...].T
    image[...] = dot(own[...], mine[pl.ds(0, width), :]) + dot(coup[...], mate[...])


def turn(mine):
    toward = mine[pl.ds(mark_line(mine), 1), :]
    column = lax.broadcasted_iota(jnp.int32, toward.shape, 1)
    return jnp.where((toward == 3.0) == (column < toward.shape[1] // 2), 1.0, 0.0)


def gy_kernel(take, weight, mine, part, single, border, pay, image, once, coup):
    width = coup.shape[0]
    toward = mine[pl.ds(mark_line(mine), 1), pl.ds(0, 1)]
    coup[...] = edge(toward if take is None else take, mine, pay, border)
    term = dot(coup[...], pay[pl.ds(0, width), :])
    image[...] = part[...] + term
    once[...] = single[...] + (weight * turn(mine) if take is None else weight) * term


def left_kernel(mine, part, single, border, pay, image, once, coup, back):
    width = coup.shape[0]
    coup[...] = edge(0, mine, pay, border)
    back[...] = dot(coup[...].T, mine[pl.ds(0, width), :])
    term = dot(coup[...], pay[pl.ds(0, width), :])
    image[pl.ds(0, width), :] = part[...] + term
    image[pl.ds(width, EXTRA), :] = jnp.zeros((EXTRA, term.shape[1]), F32)
    once[...] = single[...] + 2.0 * term


def right_kernel(mine, part, back, image, half):
    width = image.shape[0]
    full = part[pl.ds(0, width), :] + back[...]
    image[...] = full
    middle = full.shape[1] // 2
    toward = mine[pl.ds(mark_line(mine), 1), pl.ds(0, 1)]
    half[...] = jnp.where(toward == 3.0, full[:, middle:], full[:, :middle])


def near_kernel(field, image, once, mate, mate_w, own, coup, pay, back, part, lift, state):
    b = field[...]
    norm = col_sum(b, b)
    c = jnp.where(norm > 0.0, col_sum(b, image[...]) / jnp.where(norm > 0.0, norm, 1.0), 0.0)
    g = image[...] - c * b
    part[...] = dot(own[...], g) + dot(coup[...], mate_w[...] - c * mate[...])
    lift[...] = back[...] - c * pay[pl.ds(0, b.shape[0]), :]
    rows = [(0, norm), (1, c), (2, col_sum(g, g)), (4, -col_sum(g, once[...])), (5, col_sum(b, once[...]))]
    state[...] = stack_rows(rows, state.shape)


def far_kernel(take, field, image, part, near, lift, coup, left, *refs):
    *sides, state = refs
    width = field.shape[0]
    b = field[...]
    c = near[1:2, :]
    acc = part[...] + 2.0 * dot(coup[...], left[pl.ds(0, width), :] + lift[...])
    if sides:
        mine, coup_gy, pay, side = sides
        if take is None:
            toward = mine[pl.ds(mark_line(mine), 1), pl.ds(0, 1)]
            middle = b.shape[1] // 2
            shift = c * pay[pl.ds(0, width), :]
            term = dot(coup_gy[...], side[...] - jnp.where(toward == 3.0, shift[:, :middle], shift[:, middle:]))
            acc += 2.0 * turn(mine) * jnp.concatenate([term, term], axis=1)
        else:
            acc += 2.0 * dot(coup_gy[...], side[...] - c * pay[pl.ds(0, width), :])
    state[...] = near[...] + stack_rows([(3, col_sum(image[...] - c * b, acc)), (4, -col_sum(b, acc))], state.shape)


def merge_kernel(*refs):
    *states, out = refs
    norm = sum(s[0:1, :] for s in states)
    base = states[0][1:2, :]
    shift = sum(s[0:1, :] * (s[1:2, :] - base) for s in states)
    c = base + jnp.where(norm > 0.0, shift / jnp.where(norm > 0.0, norm, 1.0), 0.0)
    size, flat, slope, bend = (jnp.zeros_like(c) for _ in range(4))
    for s in states:
        d = c - s[1:2, :]
        size += s[2:3, :] + s[0:1, :] * d * d
        flat += s[3:4, :] + (s[4:5, :] + s[5:6, :] * d) * d
        slope += s[4:5, :] + 2.0 * s[5:6, :] * d
        bend += s[5:6, :]
    out[...] = stack_rows(list(enumerate([norm, c, size, flat, slope, bend])), out.shape)


def shards(right_side, node_diag, local_coup, block_cols, border_coup, border_send, border_rows):
    width, ncols = right_side.shape
    nblocks, _, bs, _ = local_coup.shape
    n_gx, n_gy, n_nd = (lax.axis_size(a) for a in AXES)
    assert n_nd == 2 and border_coup.shape[1] == 4 * SIDE
    swap = [(0, 1), (1, 0)]
    right = [(i, (i + 1) % n_gx) for i in range(n_gx)]
    left = [(j, i) for i, j in right]
    up = [(i, i + 1) for i in range(n_gy - 1)]
    down = [(j, i) for i, j in up]
    facing = jnp.where(lax.axis_index("gy") == 0, 3, 2).astype(jnp.int32)
    if n_gy == 2:
        sides = [(swap, None, 2.0)]
    elif n_gy > 2:
        sides = [(up, 2, 2.0), (down, 3, 0.0)]
    else:
        sides = []
    sends = [("gx", right)] + [("gy", perm) for perm, _, _ in sides]
    gives = [1] + [None if t is None else t ^ 1 for _, t, _ in sides]
    marks = jnp.stack([facing, lax.axis_index("nd").astype(jnp.int32)])
    border = border_coup[0]

    def smem(n):
        return [pl.BlockSpec(memory_space=pltpu.SMEM)] * n

    rows = width + bs + TAIL

    def pack(gives, extra):
        count = len(gives)
        return pl.pallas_call(
            partial(pack_kernel, gives),
            name="pack",
            in_specs=smem(1) + [pl.BlockSpec(memory_space=pl.ANY)] * 4,
            out_specs=[vmem()] * count,
            out_shape=[pltpu.VMEM((rows + extra, ncols), F32)] * count,
            scratch_shapes=[
                pltpu.SemaphoreType.DMA((count, SIDE + 1)),
                pltpu.VMEM((2, 1, 4 * SIDE), jnp.int32),
                pltpu.SemaphoreType.DMA((2,)),
            ],
            compiler_params=pltpu.CompilerParams(vmem_limit_bytes=LIMIT),
        )(marks, *[pltpu.with_memory_space_constraint(a, pltpu.HBM) for a in (right_side, border, border_send, border_rows)])

    packed = pack(gives[:1], EXTRA) + (pack(gives[1:], 0) if sides else [])
    pays = [lax.ppermute(pay, axis, perm) for pay, (axis, perm) in zip(packed, sends)]
    mine = packed[0]
    mate = lax.ppermute(right_side, "nd", swap)

    def tabled(kernel, name, tables, shapes, flops=None):
        def run(*args):
            args = list(args[:tables]) + [pltpu.with_memory_space_constraint(a, pltpu.VMEM) for a in args[tables:]]
            return pl.pallas_call(
                kernel,
                name=name,
                in_specs=smem(tables) + [vmem()] * (len(args) - tables),
                out_specs=[vmem()] * len(shapes),
                out_shape=[pltpu.VMEM(shape, F32) for shape in shapes],
                compiler_params=pltpu.CompilerParams(vmem_limit_bytes=LIMIT),
                cost_estimate=flops and pl.CostEstimate(flops=flops, bytes_accessed=1 << 20, transcendentals=0),
            )(*args)

        return run

    field, square = (width, ncols), (width, width)
    own, pair = tabled(prep_kernel, "prep", 2, [square] * 2, 1 << 24)(
        block_cols, marks, node_diag.reshape(1, width), local_coup, mine
    )
    mate_pair = lax.ppermute(pair, "nd", swap)

    part, coup = call(base_kernel, "base", [field, square])(mine, own, pair, mate, mate_pair)
    once = part
    side_coup = []
    for (_, take, weight), pay in zip(sides, pays[1:]):
        part, once, block = call(partial(gy_kernel, take, weight), "gy", [field, field, square])(mine, part, once, border, pay)
        side_coup.append(block)
    part, once, left_coup, back = call(left_kernel, "left", [(width + EXTRA, ncols), field, square, field])(
        mine, part, once, border, pays[0]
    )
    right_part = lax.ppermute(back, "gx", left)
    left_w = lax.ppermute(part, "gx", right)
    image, half = call(right_kernel, "right", [field, (width, ncols // 2)])(mine, part, right_part)
    mate_w = lax.ppermute(image, "nd", swap)
    part, lift, state = call(near_kernel, "near", [field, field, (TAIL, ncols)])(
        right_side, image, once, mate, mate_w, own, coup, pays[0], back
    )
    far = []
    take = None
    if sides:
        perm, take, _ = sides[0]
        far = [mine, side_coup[0], pays[1], lax.ppermute(half if take is None else image, "gy", perm)]
    (state,) = call(partial(far_kernel, take), "far", [(TAIL, ncols)])(
        right_side, image, part, state, lift, left_coup, left_w, *far
    )
    state = join(state)
    norm, c, size, form = (row[None] for row in state[:4])
    ratio = size / (c * c * norm)
    last = size / (form - ratio * ratio * c * c * c * norm)
    return ((1.0 + last * c * (1.0 + ratio)) / c) * right_side - (last / c) * image


def solution(mesh):
    blocks = P(("var", "gx", "gy", "nd"))
    tables = P(AXES)
    in_specs = (blocks, blocks, blocks, tables, blocks, tables, tables)
    return jax.shard_map(shards, mesh=mesh, in_specs=in_specs, out_specs=blocks, check_vma=False)
```

```python
from functools import partial

import jax
import jax.numpy as jnp
from jax import lax
from jax.experimental import pallas as pl
from jax.experimental.pallas import tpu as pltpu
from jax.sharding import PartitionSpec as P

F32 = jnp.float32
BF16 = jnp.bfloat16
AXES = ("gx", "gy", "nd")
SIDE = 2
LIMIT = 8 << 20
EXTRA = 8
TAIL = 8


def vmem():
    return pl.BlockSpec(memory_space=pltpu.VMEM)


def call(kernel, name, shapes, scratch=(), flops=None):
    def run(*args):
        args = [pltpu.with_memory_space_constraint(a, pltpu.VMEM) for a in args]
        return pl.pallas_call(
            kernel,
            name=name,
            in_specs=[vmem()] * len(args),
            out_specs=[vmem()] * len(shapes),
            out_shape=[pltpu.VMEM(shape, F32) for shape in shapes],
            scratch_shapes=scratch,
            compiler_params=pltpu.CompilerParams(vmem_limit_bytes=LIMIT),
            cost_estimate=flops and pl.CostEstimate(flops=flops, bytes_accessed=1 << 20, transcendentals=0),
        )(*args)

    return run


def join(state):
    count = lax.axis_size(AXES)
    assert count & (count - 1) == 0
    step = 1
    while step < count:
        masks = [m * step for m in (1, 2, 3) if m * step < count]
        others = [lax.ppermute(state, AXES, [(i, i ^ m) for i in range(count)]) for m in masks]
        (state,) = call(merge_kernel, "merge", [state.shape])(state, *others)
        step *= 4
    return state


def split(a):
    high = a.astype(BF16)
    return high, (a - high.astype(F32)).astype(BF16)


def dot(a, b):
    (ah, al), (bh, bl) = split(a), split(b)
    mul = partial(jnp.dot, preferred_element_type=F32)
    return mul(ah, bh) + (mul(ah, bl) + mul(al, bh))


def mark_line(mine):
    return mine.shape[0] - EXTRA - TAIL + 2


def col_sum(a, b):
    return jnp.sum(a * b, axis=0, keepdims=True)


def stack_rows(rows, shape):
    line = lax.broadcasted_iota(jnp.int32, shape, 0)
    return sum(jnp.where(line == n, row, 0.0) for n, row in rows)


def pack_kernel(gives, marks, field, border, send, rows, *refs):
    *pays, sems, table, table_sems = refs
    width = field.shape[0]
    bs = border.shape[1]
    tables = [pltpu.make_async_copy(ref, table.at[n], table_sems.at[n]) for n, ref in enumerate((rows, send))]
    copies = []
    for n, pay in enumerate(pays):
        give = marks[0] if gives[n] is None else gives[n]
        copies.append(pltpu.make_async_copy(field, pay.at[pl.ds(0, width), :], sems.at[n, SIDE]))
        for s in range(SIDE):
            block = pay.at[pl.ds(width, bs), pl.ds(s * bs, bs)]
            copies.append(pltpu.make_async_copy(border.at[give * SIDE + s], block, sems.at[n, s]))
    for copy in tables + copies:
        copy.start()
    for copy in tables:
        copy.wait()
    count = table.shape[2]
    for pay in pays:
        for n in range(2):
            pay[pl.ds(width + bs + n, 1), pl.ds(0, count)] = table[n].astype(F32)
        pay[pl.ds(width + bs + 2, 1), :] = jnp.full((1, pay.shape[1]), marks[0].astype(F32))
    for copy in copies:
        copy.wait()


def prep_kernel(cols, marks, diag, local, packed, own, pair):
    nblocks, nonzeros, bs, _ = local.shape
    width = nblocks * bs
    patch_len = 2 * nblocks
    base = marks[1] * nblocks
    own[...] = jnp.zeros((width, width), F32)
    pair[...] = jnp.zeros((width, width), F32)
    for b in range(nblocks):
        for k in range(nonzeros):
            spot = lax.rem(cols[b, k] - base + patch_len, patch_len)
            block = local[b, k]
            for c in range(nblocks):

                @pl.when(spot == c)
                def _():
                    own[pl.ds(b * bs, bs), pl.ds(c * bs, bs)] += block

                @pl.when(spot == c + nblocks)
                def _():
                    pair[pl.ds(b * bs, bs), pl.ds(c * bs, bs)] += block

    lower = own[...]
    here = lax.broadcasted_iota(jnp.int32, (width, width), 0)
    there = lax.broadcasted_iota(jnp.int32, (width, width), 1)
    own[...] = lower + lower.T + jnp.where(here == there, diag[...], 0.0)


def edge(take, mine, pay, border):
    bs = border.shape[1]
    width = bs * (pay.shape[0] // bs - 1)
    known = isinstance(take, int)

    def pick(of):
        return of(take) if known else jnp.where(take == 2.0, of(2), of(3))

    def number(ref, line, t):
        return ref[pl.ds(width + bs + line, 1), pl.ds(t * SIDE + s, 1)]

    blocks = [[0.0] * (width // bs) for _ in range(width // bs)]
    for s in range(SIDE):
        turned = pay[pl.ds(width, bs), pl.ds(s * bs, bs)].T
        pairs = [
            (pick(lambda t: border[t * SIDE + s]), pick(lambda t: number(mine, 0, t)), pick(lambda t: number(pay, 1, t))),
            (turned, pick(lambda t: number(mine, 1, t ^ 1)), pick(lambda t: number(pay, 0, t ^ 1))),
        ]
        for block, to, at in pairs:
            for i, line in enumerate(blocks):
                for j in range(len(line)):
                    line[j] = line[j] + jnp.where((to == i) & (at == j), block, 0.0)
    return jnp.concatenate([jnp.concatenate(line, axis=1) for line in blocks], axis=0)


def base_kernel(mine, own, pair, mate, mate_pair, image, coup):
    width = mate.shape[0]
    coup[...] = pair[...] + mate_pair[...].T
    image[...] = dot(own[...], mine[pl.ds(0, width), :]) + dot(coup[...], mate[...])


def turn(mine):
    toward = mine[pl.ds(mark_line(mine), 1), :]
    column = lax.broadcasted_iota(jnp.int32, toward.shape, 1)
    return jnp.where((toward == 3.0) == (column < toward.shape[1] // 2), 1.0, 0.0)


def gy_kernel(take, weight, mine, part, single, border, pay, image, once, coup):
    width = coup.shape[0]
    toward = mine[pl.ds(mark_line(mine), 1), pl.ds(0, 1)]
    coup[...] = edge(toward if take is None else take, mine, pay, border)
    term = dot(coup[...], pay[pl.ds(0, width), :])
    image[pl.ds(0, width), :] = part[...] + term
    if image.shape[0] > width:
        image[pl.ds(width, EXTRA), :] = jnp.zeros((EXTRA, term.shape[1]), F32)
    once[...] = single[...] + (weight * turn(mine) if take is None else weight) * term


def left_kernel(mine, part, border, pay, image, once, coup, back):
    width = coup.shape[0]
    coup[...] = edge(0, mine, pay, border)
    back[...] = dot(coup[...].T, mine[pl.ds(0, width), :])
    term = dot(coup[...], pay[pl.ds(0, width), :])
    image[...] = part[...] + term
    once[...] = part[...] + 2.0 * term


def right_kernel(mine, part, back, image, half):
    width = image.shape[0]
    full = part[pl.ds(0, width), :] + back[...]
    image[...] = full
    middle = full.shape[1] // 2
    toward = mine[pl.ds(mark_line(mine), 1), pl.ds(0, 1)]
    half[...] = jnp.where(toward == 3.0, full[:, middle:], full[:, :middle])


def near_kernel(field, image, once, mate, mate_w, own, coup, pay, back, part, lift, state):
    b = field[...]
    norm = col_sum(b, b)
    c = jnp.where(norm > 0.0, col_sum(b, image[...]) / jnp.where(norm > 0.0, norm, 1.0), 0.0)
    g = image[...] - c * b
    part[...] = dot(own[...], g) + dot(coup[...], mate_w[...] - c * mate[...])
    lift[...] = back[...] - c * pay[pl.ds(0, b.shape[0]), :]
    rows = [(0, norm), (1, c), (2, col_sum(g, g)), (4, -col_sum(g, once[...])), (5, col_sum(b, once[...]))]
    state[...] = stack_rows(rows, state.shape)


def far_kernel(take, field, image, part, near, lift, coup, left, *refs):
    *sides, state = refs
    width = field.shape[0]
    b = field[...]
    c = near[1:2, :]
    acc = part[...] + 2.0 * dot(coup[...], left[pl.ds(0, width), :] + lift[...])
    if sides:
        mine, coup_gy, pay, side = sides
        if take is None:
            toward = mine[pl.ds(mark_line(mine), 1), pl.ds(0, 1)]
            middle = b.shape[1] // 2
            shift = c * pay[pl.ds(0, width), :]
            term = dot(coup_gy[...], side[...] - jnp.where(toward == 3.0, shift[:, :middle], shift[:, middle:]))
            acc += 2.0 * turn(mine) * jnp.concatenate([term, term], axis=1)
        else:
            acc += 2.0 * dot(coup_gy[...], side[...] - c * pay[pl.ds(0, width), :])
    state[...] = near[...] + stack_rows([(3, col_sum(image[...] - c * b, acc)), (4, -col_sum(b, acc))], state.shape)


def merge_kernel(*refs):
    *states, out = refs
    norm = sum(s[0:1, :] for s in states)
    base = states[0][1:2, :]
    shift = sum(s[0:1, :] * (s[1:2, :] - base) for s in states)
    c = base + jnp.where(norm > 0.0, shift / jnp.where(norm > 0.0, norm, 1.0), 0.0)
    size, flat, slope, bend = (jnp.zeros_like(c) for _ in range(4))
    for s in states:
        d = c - s[1:2, :]
        size += s[2:3, :] + s[0:1, :] * d * d
        flat += s[3:4, :] + (s[4:5, :] + s[5:6, :] * d) * d
        slope += s[4:5, :] + 2.0 * s[5:6, :] * d
        bend += s[5:6, :]
    out[...] = stack_rows(list(enumerate([norm, c, size, flat, slope, bend])), out.shape)


def shards(right_side, node_diag, local_coup, block_cols, border_coup, border_send, border_rows):
    width, ncols = right_side.shape
    nblocks, _, bs, _ = local_coup.shape
    n_gx, n_gy, n_nd = (lax.axis_size(a) for a in AXES)
    assert n_nd == 2 and border_coup.shape[1] == 4 * SIDE
    swap = [(0, 1), (1, 0)]
    right = [(i, (i + 1) % n_gx) for i in range(n_gx)]
    left = [(j, i) for i, j in right]
    up = [(i, i + 1) for i in range(n_gy - 1)]
    down = [(j, i) for i, j in up]
    facing = jnp.where(lax.axis_index("gy") == 0, 3, 2).astype(jnp.int32)
    if n_gy == 2:
        sides = [(swap, None, 2.0)]
    elif n_gy > 2:
        sides = [(up, 2, 2.0), (down, 3, 0.0)]
    else:
        sides = []
    sends = [("gx", right)] + [("gy", perm) for perm, _, _ in sides]
    gives = [1] + [None if t is None else t ^ 1 for _, t, _ in sides]
    marks = jnp.stack([facing, lax.axis_index("nd").astype(jnp.int32)])
    border = border_coup[0]

    def smem(n):
        return [pl.BlockSpec(memory_space=pltpu.SMEM)] * n

    rows = width + bs + TAIL
    count = len(gives)
    packed = pl.pallas_call(
        partial(pack_kernel, gives),
        name="pack",
        in_specs=smem(1) + [pl.BlockSpec(memory_space=pl.ANY)] * 4,
        out_specs=[vmem()] * count,
        out_shape=[pltpu.VMEM((rows + (0 if n else EXTRA), ncols), F32) for n in range(count)],
        scratch_shapes=[
            pltpu.SemaphoreType.DMA((count, SIDE + 1)),
            pltpu.VMEM((2, 1, 4 * SIDE), jnp.int32),
            pltpu.SemaphoreType.DMA((2,)),
        ],
        compiler_params=pltpu.CompilerParams(vmem_limit_bytes=LIMIT),
    )(marks, *[pltpu.with_memory_space_constraint(a, pltpu.HBM) for a in (right_side, border, border_send, border_rows)])
    pays = [lax.ppermute(pay, axis, perm) for pay, (axis, perm) in zip(packed, sends)]
    mine = packed[0]
    mate = lax.ppermute(right_side, "nd", swap)

    def tabled(kernel, name, tables, shapes, flops=None):
        def run(*args):
            args = list(args[:tables]) + [pltpu.with_memory_space_constraint(a, pltpu.VMEM) for a in args[tables:]]
            return pl.pallas_call(
                kernel,
                name=name,
                in_specs=smem(tables) + [vmem()] * (len(args) - tables),
                out_specs=[vmem()] * len(shapes),
                out_shape=[pltpu.VMEM(shape, F32) for shape in shapes],
                compiler_params=pltpu.CompilerParams(vmem_limit_bytes=LIMIT),
                cost_estimate=flops and pl.CostEstimate(flops=flops, bytes_accessed=1 << 20, transcendentals=0),
            )(*args)

        return run

    field, square = (width, ncols), (width, width)
    own, pair = tabled(prep_kernel, "prep", 2, [square] * 2, 1 << 24)(
        block_cols, marks, node_diag.reshape(1, width), local_coup, mine
    )
    mate_pair = lax.ppermute(pair, "nd", swap)

    part, coup = call(base_kernel, "base", [field, square])(mine, own, pair, mate, mate_pair)
    part, once, left_coup, back = call(left_kernel, "left", [field, field, square, field])(mine, part, border, pays[0])
    right_part = lax.ppermute(back, "gx", left)
    side_coup = []
    for n, ((_, take, weight), pay) in enumerate(zip(sides, pays[1:])):
        extra = EXTRA if n == len(sides) - 1 else 0
        part, once, block = call(partial(gy_kernel, take, weight), "gy", [(width + extra, ncols), field, square])(
            mine, part, once, border, pay
        )
        side_coup.append(block)
    left_w = lax.ppermute(part, "gx", right)
    image, half = call(right_kernel, "right", [field, (width, ncols // 2)])(mine, part, right_part)
    mate_w = lax.ppermute(image, "nd", swap)
    part, lift, state = call(near_kernel, "near", [field, field, (TAIL, ncols)])(
        right_side, image, once, mate, mate_w, own, coup, pays[0], back
    )
    far = []
    take = None
    if sides:
        perm, take, _ = sides[0]
        far = [mine, side_coup[0], pays[1], lax.ppermute(half if take is None else image, "gy", perm)]
    (state,) = call(partial(far_kernel, take), "far", [(TAIL, ncols)])(
        right_side, image, part, state, lift, left_coup, left_w, *far
    )
    state = join(state)
    norm, c, size, form = (row[None] for row in state[:4])
    ratio = size / (c * c * norm)
    last = size / (form - ratio * ratio * c * c * c * norm)
    return ((1.0 + last * c * (1.0 + ratio)) / c) * right_side - (last / c) * image


def solution(mesh):
    blocks = P(("var", "gx", "gy", "nd"))
    tables = P(AXES)
    in_specs = (blocks, blocks, blocks, tables, blocks, tables, tables)
    return jax.shard_map(shards, mesh=mesh, in_specs=in_specs, out_specs=blocks, check_vma=False)
```

```python
from functools import partial

import jax
import jax.numpy as jnp
from jax import lax
from jax.experimental import pallas as pl
from jax.experimental.pallas import tpu as pltpu
from jax.sharding import PartitionSpec as P

F32 = jnp.float32
BF16 = jnp.bfloat16
AXES = ("gx", "gy", "nd")
SIDE = 2
LIMIT = 8 << 20
TAIL = 8


def vmem():
    return pl.BlockSpec(memory_space=pltpu.VMEM)


def call(kernel, name, shapes, scratch=(), flops=None):
    def run(*args):
        args = [pltpu.with_memory_space_constraint(a, pltpu.VMEM) for a in args]
        return pl.pallas_call(
            kernel,
            name=name,
            in_specs=[vmem()] * len(args),
            out_specs=[vmem()] * len(shapes),
            out_shape=[pltpu.VMEM(shape, F32) for shape in shapes],
            scratch_shapes=scratch,
            compiler_params=pltpu.CompilerParams(vmem_limit_bytes=LIMIT),
            cost_estimate=flops and pl.CostEstimate(flops=flops, bytes_accessed=1 << 20, transcendentals=0),
        )(*args)

    return run


def join(state):
    count = lax.axis_size(AXES)
    assert count & (count - 1) == 0
    step = 1
    while step < count:
        masks = [m * step for m in (1, 2, 3) if m * step < count]
        others = [lax.ppermute(state, AXES, [(i, i ^ m) for i in range(count)]) for m in masks]
        (state,) = call(merge_kernel, "merge", [state.shape])(state, *others)
        step *= 4
    return state


def split(a):
    high = a.astype(BF16)
    return high, (a - high.astype(F32)).astype(BF16)


def dot(a, b):
    (ah, al), (bh, bl) = split(a), split(b)
    mul = partial(jnp.dot, preferred_element_type=F32)
    return mul(ah, bh) + (mul(ah, bl) + mul(al, bh))


def col_sum(a, b):
    return jnp.sum(a * b, axis=0, keepdims=True)


def stack_rows(rows, shape):
    line = lax.broadcasted_iota(jnp.int32, shape, 0)
    return sum(jnp.where(line == n, row, 0.0) for n, row in rows)


def pack_kernel(gives, *refs):
    marks, refs = (refs[0], refs[1:]) if None in gives else (None, refs)
    field, border, send, rows, toward, *pays, sems, table, table_sems = refs
    width = field.shape[0]
    bs = border.shape[1]
    tables = [pltpu.make_async_copy(ref, table.at[n], table_sems.at[n]) for n, ref in enumerate((rows, send, toward))]
    copies = []
    for n, pay in enumerate(pays):
        give = marks[0] if gives[n] is None else gives[n]
        copies.append(pltpu.make_async_copy(field, pay.at[pl.ds(0, width), :], sems.at[n, SIDE]))
        for s in range(SIDE):
            block = pay.at[pl.ds(width, bs), pl.ds(s * bs, bs)]
            copies.append(pltpu.make_async_copy(border.at[give * SIDE + s], block, sems.at[n, s]))
    for copy in tables + copies:
        copy.start()
    for copy in tables:
        copy.wait()
    count = table.shape[2]
    for pay in pays:
        for n in range(3):
            pay[pl.ds(width + bs + n, 1), pl.ds(0, count)] = table[n].astype(F32)
    for copy in copies:
        copy.wait()


def prep_kernel(cols, marks, diag, local, packed, own, pair):
    nblocks, nonzeros, bs, _ = local.shape
    width = nblocks * bs
    patch_len = 2 * nblocks
    base = marks[1] * nblocks
    own[...] = jnp.zeros((width, width), F32)
    pair[...] = jnp.zeros((width, width), F32)
    for b in range(nblocks):
        for k in range(nonzeros):
            spot = lax.rem(cols[b, k] - base + patch_len, patch_len)
            block = local[b, k]
            for c in range(nblocks):

                @pl.when(spot == c)
                def _():
                    own[pl.ds(b * bs, bs), pl.ds(c * bs, bs)] += block

                @pl.when(spot == c + nblocks)
                def _():
                    pair[pl.ds(b * bs, bs), pl.ds(c * bs, bs)] += block

    lower = own[...]
    here = lax.broadcasted_iota(jnp.int32, (width, width), 0)
    there = lax.broadcasted_iota(jnp.int32, (width, width), 1)
    own[...] = lower + lower.T + jnp.where(here == there, diag[...], 0.0)


def edge(take, mine, pay, border):
    bs = border.shape[1]
    width = pay.shape[0] - bs - TAIL
    known = isinstance(take, int)

    def pick(of):
        return of(take) if known else jnp.where(take == 2.0, of(2), of(3))

    def number(ref, line, t):
        return ref[pl.ds(width + bs + line, 1), pl.ds(t * SIDE + s, 1)]

    blocks = [[0.0] * (width // bs) for _ in range(width // bs)]
    for s in range(SIDE):
        turned = pay[pl.ds(width, bs), pl.ds(s * bs, bs)].T
        pairs = [
            (pick(lambda t: border[t * SIDE + s]), pick(lambda t: number(mine, 0, t)), pick(lambda t: number(pay, 1, t))),
            (turned, pick(lambda t: number(mine, 1, t ^ 1)), pick(lambda t: number(pay, 0, t ^ 1))),
        ]
        for block, to, at in pairs:
            for i, line in enumerate(blocks):
                for j in range(len(line)):
                    line[j] = line[j] + jnp.where((to == i) & (at == j), block, 0.0)
    return jnp.concatenate([jnp.concatenate(line, axis=1) for line in blocks], axis=0)


def base_kernel(mine, own, pair, mate, mate_pair, image, coup):
    width = mate.shape[0]
    coup[...] = pair[...] + mate_pair[...].T
    image[...] = dot(own[...], mine[pl.ds(0, width), :]) + dot(coup[...], mate[...])


def left_kernel(mine, part, border, pay, image, once, coup, back):
    width = part.shape[0]
    coup[...] = edge(0, mine, pay, border)
    term = dot(coup[...], pay[pl.ds(0, width), :])
    image[...] = part[...] + term
    once[...] = part[...] + 2.0 * term
    back[...] = dot(coup[...].T, mine[pl.ds(0, width), :])


def turn(mine, width):
    toward = mine[pl.ds(mine.shape[0] - TAIL + 2, 1), pl.ds(0, 1)]
    count = mine.shape[1]
    first = jnp.where(lax.broadcasted_iota(jnp.int32, (1, count), 1) < count // 2, 1.0, 0.0)
    return jnp.where(toward == 3.0, first, 1.0 - first)


def gy_kernel(take, weight, mine, part, single, border, pay, image, once, coup):
    width = coup.shape[0]
    toward = mine[pl.ds(mine.shape[0] - TAIL + 2, 1), pl.ds(0, 1)]
    coup[...] = edge(toward if take is None else take, mine, pay, border)
    term = dot(coup[...], pay[pl.ds(0, width), :])
    image[...] = part[...] + term
    scale = weight * turn(mine, width) if take is None else weight
    once[...] = single[...] + scale * term


def right_kernel(mine, part, border, pay, image, half):
    width = image.shape[0]
    full = part[...] + dot(edge(1, mine, pay, border), pay[pl.ds(0, width), :])
    image[...] = full
    middle = full.shape[1] // 2
    toward = mine[pl.ds(mine.shape[0] - TAIL + 2, 1), pl.ds(0, 1)]
    half[...] = jnp.where(toward == 3.0, full[:, middle:], full[:, :middle])


def near_kernel(field, image, once, mate, mate_w, own, coup, pay, back, part, lift, state):
    b = field[...]
    norm = col_sum(b, b)
    c = jnp.where(norm > 0.0, col_sum(b, image[...]) / jnp.where(norm > 0.0, norm, 1.0), 0.0)
    g = image[...] - c * b
    part[...] = dot(own[...], g) + dot(coup[...], mate_w[...] - c * mate[...])
    lift[...] = back[...] - c * pay[pl.ds(0, b.shape[0]), :]
    rows = [(0, norm), (1, c), (2, col_sum(g, g)), (4, -col_sum(g, once[...])), (5, col_sum(b, once[...]))]
    state[...] = stack_rows(rows, state.shape)


def far_kernel(take, field, image, part, near, lift, coup, left, *refs):
    *sides, state = refs
    width = field.shape[0]
    b = field[...]
    c = near[1:2, :]
    acc = part[...] + 2.0 * dot(coup[...], left[...] + lift[...])
    if sides:
        mine, coup_gy, pay, side = sides
        if take is None:
            toward = mine[pl.ds(mine.shape[0] - TAIL + 2, 1), pl.ds(0, 1)]
            middle = b.shape[1] // 2
            shift = c * pay[pl.ds(0, width), :]
            term = dot(coup_gy[...], side[...] - jnp.where(toward == 3.0, shift[:, :middle], shift[:, middle:]))
            acc += 2.0 * turn(mine, width) * jnp.concatenate([term, term], axis=1)
        else:
            acc += 2.0 * dot(coup_gy[...], side[...] - c * pay[pl.ds(0, width), :])
    state[...] = near[...] + stack_rows([(3, col_sum(image[...] - c * b, acc)), (4, -col_sum(b, acc))], state.shape)


def merge_kernel(*refs):
    *states, out = refs
    norm = sum(s[0:1, :] for s in states)
    base = states[0][1:2, :]
    shift = sum(s[0:1, :] * (s[1:2, :] - base) for s in states)
    c = base + jnp.where(norm > 0.0, shift / jnp.where(norm > 0.0, norm, 1.0), 0.0)
    size, flat, slope, bend = (jnp.zeros_like(c) for _ in range(4))
    for s in states:
        d = c - s[1:2, :]
        size += s[2:3, :] + s[0:1, :] * d * d
        flat += s[3:4, :] + (s[4:5, :] + s[5:6, :] * d) * d
        slope += s[4:5, :] + 2.0 * s[5:6, :] * d
        bend += s[5:6, :]
    out[...] = stack_rows(list(enumerate([norm, c, size, flat, slope, bend])), out.shape)


def shards(right_side, node_diag, local_coup, block_cols, border_coup, border_send, border_rows):
    width, ncols = right_side.shape
    nblocks, _, bs, _ = local_coup.shape
    n_gx, n_gy, n_nd = (lax.axis_size(a) for a in AXES)
    assert n_nd == 2 and border_coup.shape[1] == 4 * SIDE
    swap = [(0, 1), (1, 0)]
    right = [(i, (i + 1) % n_gx) for i in range(n_gx)]
    left = [(j, i) for i, j in right]
    up = [(i, i + 1) for i in range(n_gy - 1)]
    down = [(j, i) for i, j in up]
    facing = jnp.where(lax.axis_index("gy") == 0, 3, 2).astype(jnp.int32)
    if n_gy == 2:
        sides = [(swap, None, 2.0)]
    elif n_gy > 2:
        sides = [(up, 2, 2.0), (down, 3, 0.0)]
    else:
        sides = []
    sends = [("gx", right), ("gx", left)] + [("gy", perm) for perm, _, _ in sides]
    gives = [1, 0] + [None if t is None else t ^ 1 for _, t, _ in sides]
    toward = jnp.full((1, 4 * SIDE), facing)
    marks = jnp.stack([facing, lax.axis_index("nd").astype(jnp.int32)])
    border = border_coup[0]

    def smem(n):
        return [pl.BlockSpec(memory_space=pltpu.SMEM)] * n

    pay_shape = (width + bs + TAIL, ncols)

    def pack(gives):
        count = len(gives)
        tables = [marks] if None in gives else []
        return pl.pallas_call(
            partial(pack_kernel, gives),
            name="pack",
            in_specs=smem(len(tables)) + [pl.BlockSpec(memory_space=pl.ANY)] * 5,
            out_specs=[vmem()] * count,
            out_shape=[pltpu.VMEM(pay_shape, F32)] * count,
            scratch_shapes=[
                pltpu.SemaphoreType.DMA((count, SIDE + 1)),
                pltpu.VMEM((3, 1, 4 * SIDE), jnp.int32),
                pltpu.SemaphoreType.DMA((3,)),
            ],
            compiler_params=pltpu.CompilerParams(vmem_limit_bytes=LIMIT),
        )(*tables, *[pltpu.with_memory_space_constraint(a, pltpu.HBM) for a in (right_side, border, border_send, border_rows)], toward)

    packed = [*pack(gives[:1]), *pack(gives[1:])]
    pays = [lax.ppermute(pay, axis, perm) for pay, (axis, perm) in zip(packed, sends)]
    mine = packed[0]
    mate = lax.ppermute(right_side, "nd", swap)

    def tabled(kernel, name, tables, shapes, flops=None):
        def run(*args):
            args = list(args[:tables]) + [pltpu.with_memory_space_constraint(a, pltpu.VMEM) for a in args[tables:]]
            return pl.pallas_call(
                kernel,
                name=name,
                in_specs=smem(tables) + [vmem()] * (len(args) - tables),
                out_specs=[vmem()] * len(shapes),
                out_shape=[pltpu.VMEM(shape, F32) for shape in shapes],
                compiler_params=pltpu.CompilerParams(vmem_limit_bytes=LIMIT),
                cost_estimate=flops and pl.CostEstimate(flops=flops, bytes_accessed=1 << 20, transcendentals=0),
            )(*args)

        return run

    field, square = (width, ncols), (width, width)
    own, pair = tabled(prep_kernel, "prep", 2, [square] * 2, 1 << 24)(
        block_cols, marks, node_diag.reshape(1, width), local_coup, mine
    )
    mate_pair = lax.ppermute(pair, "nd", swap)

    part, coup = call(base_kernel, "base", [field, square])(mine, own, pair, mate, mate_pair)
    part, once, left_coup, back = call(left_kernel, "left", [field, field, square, field])(mine, part, border, pays[0])
    side_coup = []
    for (_, take, weight), pay in zip(sides, pays[2:]):
        part, once, block = call(partial(gy_kernel, take, weight), "gy", [field, field, square])(mine, part, once, border, pay)
        side_coup.append(block)
    left_w = lax.ppermute(part, "gx", right)
    image, half = call(right_kernel, "right", [field, (width, ncols // 2)])(mine, part, border, pays[1])
    mate_w = lax.ppermute(image, "nd", swap)
    part, lift, state = call(near_kernel, "near", [field, field, (TAIL, ncols)])(
        right_side, image, once, mate, mate_w, own, coup, pays[0], back
    )
    far = []
    take = None
    if sides:
        perm, take, _ = sides[0]
        far = [mine, side_coup[0], pays[2], lax.ppermute(half if take is None else image, "gy", perm)]
    (state,) = call(partial(far_kernel, take), "far", [(TAIL, ncols)])(
        right_side, image, part, state, lift, left_coup, left_w, *far
    )
    state = join(state)
    norm, c, size, form = (row[None] for row in state[:4])
    ratio = size / (c * c * norm)
    last = size / (form - ratio * ratio * c * c * c * norm)
    return ((1.0 + last * c * (1.0 + ratio)) / c) * right_side - (last / c) * image


def solution(mesh):
    blocks = P(("var", "gx", "gy", "nd"))
    tables = P(AXES)
    in_specs = (blocks, blocks, blocks, tables, blocks, tables, tables)
    return jax.shard_map(shards, mesh=mesh, in_specs=in_specs, out_specs=blocks, check_vma=False)
```

```python
from functools import partial

import jax
import jax.numpy as jnp
from jax import lax
from jax.experimental import pallas as pl
from jax.experimental.pallas import tpu as pltpu
from jax.sharding import PartitionSpec as P

F32 = jnp.float32
BF16 = jnp.bfloat16
AXES = ("gx", "gy", "nd")
SIDE = 2
LIMIT = 8 << 20
EXTRA = 8
TAIL = 8


def vmem():
    return pl.BlockSpec(memory_space=pltpu.VMEM)


def call(kernel, name, shapes, scratch=(), flops=None):
    def run(*args):
        args = [pltpu.with_memory_space_constraint(a, pltpu.VMEM) for a in args]
        return pl.pallas_call(
            kernel,
            name=name,
            in_specs=[vmem()] * len(args),
            out_specs=[vmem()] * len(shapes),
            out_shape=[pltpu.VMEM(shape, F32) for shape in shapes],
            scratch_shapes=scratch,
            compiler_params=pltpu.CompilerParams(vmem_limit_bytes=LIMIT),
            cost_estimate=flops and pl.CostEstimate(flops=flops, bytes_accessed=1 << 20, transcendentals=0),
        )(*args)

    return run


def join(state):
    count = lax.axis_size(AXES)
    assert count & (count - 1) == 0
    step = 1
    while step < count:
        masks = [m * step for m in (1, 2, 3) if m * step < count]
        others = [lax.ppermute(state, AXES, [(i, i ^ m) for i in range(count)]) for m in masks]
        (state,) = call(merge_kernel, "merge", [state.shape])(state, *others)
        step *= 4
    return state


def split(a):
    high = a.astype(BF16)
    return high, (a - high.astype(F32)).astype(BF16)


def dot(a, b):
    (ah, al), (bh, bl) = split(a), split(b)
    mul = partial(jnp.dot, preferred_element_type=F32)
    return mul(ah, bh) + (mul(ah, bl) + mul(al, bh))


def col_sum(a, b):
    return jnp.sum(a * b, axis=0, keepdims=True)


def stack_rows(rows, shape):
    line = lax.broadcasted_iota(jnp.int32, shape, 0)
    return sum(jnp.where(line == n, row, 0.0) for n, row in rows)


def pack_kernel(gives, *refs):
    marks, refs = (refs[0], refs[1:]) if None in gives else (None, refs)
    field, border, send, rows, toward, *pays, sems, table, table_sems = refs
    width = field.shape[0]
    bs = border.shape[1]
    tables = [pltpu.make_async_copy(ref, table.at[n], table_sems.at[n]) for n, ref in enumerate((rows, send, toward))]
    copies = []
    for n, pay in enumerate(pays):
        give = marks[0] if gives[n] is None else gives[n]
        copies.append(pltpu.make_async_copy(field, pay.at[pl.ds(0, width), :], sems.at[n, SIDE]))
        for s in range(SIDE):
            block = pay.at[pl.ds(width, bs), pl.ds(s * bs, bs)]
            copies.append(pltpu.make_async_copy(border.at[give * SIDE + s], block, sems.at[n, s]))
    for copy in tables + copies:
        copy.start()
    for copy in tables:
        copy.wait()
    count = table.shape[2]
    for pay in pays:
        for n in range(3):
            pay[pl.ds(width + bs + n, 1), pl.ds(0, count)] = table[n].astype(F32)
    for copy in copies:
        copy.wait()


def prep_kernel(cols, marks, diag, local, packed, own, pair):
    nblocks, nonzeros, bs, _ = local.shape
    width = nblocks * bs
    patch_len = 2 * nblocks
    base = marks[1] * nblocks
    own[...] = jnp.zeros((width, width), F32)
    pair[...] = jnp.zeros((width, width), F32)
    for b in range(nblocks):
        for k in range(nonzeros):
            spot = lax.rem(cols[b, k] - base + patch_len, patch_len)
            block = local[b, k]
            for c in range(nblocks):

                @pl.when(spot == c)
                def _():
                    own[pl.ds(b * bs, bs), pl.ds(c * bs, bs)] += block

                @pl.when(spot == c + nblocks)
                def _():
                    pair[pl.ds(b * bs, bs), pl.ds(c * bs, bs)] += block

    lower = own[...]
    here = lax.broadcasted_iota(jnp.int32, (width, width), 0)
    there = lax.broadcasted_iota(jnp.int32, (width, width), 1)
    own[...] = lower + lower.T + jnp.where(here == there, diag[...], 0.0)


def edge(take, mine, pay, border):
    bs = border.shape[1]
    width = pay.shape[0] - bs - TAIL
    known = isinstance(take, int)

    def pick(of):
        return of(take) if known else jnp.where(take == 2.0, of(2), of(3))

    def number(ref, line, t):
        return ref[pl.ds(width + bs + line, 1), pl.ds(t * SIDE + s, 1)]

    blocks = [[0.0] * (width // bs) for _ in range(width // bs)]
    for s in range(SIDE):
        turned = pay[pl.ds(width, bs), pl.ds(s * bs, bs)].T
        pairs = [
            (pick(lambda t: border[t * SIDE + s]), pick(lambda t: number(mine, 0, t)), pick(lambda t: number(pay, 1, t))),
            (turned, pick(lambda t: number(mine, 1, t ^ 1)), pick(lambda t: number(pay, 0, t ^ 1))),
        ]
        for block, to, at in pairs:
            for i, line in enumerate(blocks):
                for j in range(len(line)):
                    line[j] = line[j] + jnp.where((to == i) & (at == j), block, 0.0)
    return jnp.concatenate([jnp.concatenate(line, axis=1) for line in blocks], axis=0)


def base_kernel(mine, own, pair, mate, mate_pair, image, coup):
    width = mate.shape[0]
    coup[...] = pair[...] + mate_pair[...].T
    image[...] = dot(own[...], mine[pl.ds(0, width), :]) + dot(coup[...], mate[...])


def left_kernel(mine, part, border, pay, image, once, coup, back):
    width = part.shape[0]
    coup[...] = edge(0, mine, pay, border)
    term = dot(coup[...], pay[pl.ds(0, width), :])
    image[...] = part[...] + term
    once[...] = part[...] + 2.0 * term
    back[...] = dot(coup[...].T, mine[pl.ds(0, width), :])


def turn(mine, width):
    toward = mine[pl.ds(mine.shape[0] - TAIL + 2, 1), pl.ds(0, 1)]
    count = mine.shape[1]
    first = jnp.where(lax.broadcasted_iota(jnp.int32, (1, count), 1) < count // 2, 1.0, 0.0)
    return jnp.where(toward == 3.0, first, 1.0 - first)


def gy_kernel(take, weight, mine, part, single, border, pay, image, once, coup):
    width = coup.shape[0]
    toward = mine[pl.ds(mine.shape[0] - TAIL + 2, 1), pl.ds(0, 1)]
    coup[...] = edge(toward if take is None else take, mine, pay, border)
    term = dot(coup[...], pay[pl.ds(0, width), :])
    image[pl.ds(0, width), :] = part[pl.ds(0, width), :] + term
    if image.shape[0] > width:
        image[pl.ds(width, EXTRA), :] = jnp.zeros((EXTRA, term.shape[1]), F32)
    scale = weight * turn(mine, width) if take is None else weight
    once[...] = single[...] + scale * term


def right_kernel(mine, part, border, pay, image, half):
    width = image.shape[0]
    full = part[pl.ds(0, width), :] + dot(edge(1, mine, pay, border), pay[pl.ds(0, width), :])
    image[...] = full
    middle = full.shape[1] // 2
    toward = mine[pl.ds(mine.shape[0] - TAIL + 2, 1), pl.ds(0, 1)]
    half[...] = jnp.where(toward == 3.0, full[:, middle:], full[:, :middle])


def near_kernel(field, image, once, mate, mate_w, own, coup, pay, back, part, lift, state):
    b = field[...]
    norm = col_sum(b, b)
    c = jnp.where(norm > 0.0, col_sum(b, image[...]) / jnp.where(norm > 0.0, norm, 1.0), 0.0)
    g = image[...] - c * b
    part[...] = dot(own[...], g) + dot(coup[...], mate_w[...] - c * mate[...])
    lift[...] = back[...] - c * pay[pl.ds(0, b.shape[0]), :]
    rows = [(0, norm), (1, c), (2, col_sum(g, g)), (4, -col_sum(g, once[...])), (5, col_sum(b, once[...]))]
    state[...] = stack_rows(rows, state.shape)


def far_kernel(take, field, image, part, near, lift, coup, left, *refs):
    *sides, state = refs
    width = field.shape[0]
    b = field[...]
    c = near[1:2, :]
    acc = part[...] + 2.0 * dot(coup[...], left[pl.ds(0, width), :] + lift[...])
    if sides:
        mine, coup_gy, pay, side = sides
        if take is None:
            toward = mine[pl.ds(mine.shape[0] - TAIL + 2, 1), pl.ds(0, 1)]
            middle = b.shape[1] // 2
            shift = c * pay[pl.ds(0, width), :]
            term = dot(coup_gy[...], side[...] - jnp.where(toward == 3.0, shift[:, :middle], shift[:, middle:]))
            acc += 2.0 * turn(mine, width) * jnp.concatenate([term, term], axis=1)
        else:
            acc += 2.0 * dot(coup_gy[...], side[...] - c * pay[pl.ds(0, width), :])
    state[...] = near[...] + stack_rows([(3, col_sum(image[...] - c * b, acc)), (4, -col_sum(b, acc))], state.shape)


def merge_kernel(*refs):
    *states, out = refs
    norm = sum(s[0:1, :] for s in states)
    base = states[0][1:2, :]
    shift = sum(s[0:1, :] * (s[1:2, :] - base) for s in states)
    c = base + jnp.where(norm > 0.0, shift / jnp.where(norm > 0.0, norm, 1.0), 0.0)
    size, flat, slope, bend = (jnp.zeros_like(c) for _ in range(4))
    for s in states:
        d = c - s[1:2, :]
        size += s[2:3, :] + s[0:1, :] * d * d
        flat += s[3:4, :] + (s[4:5, :] + s[5:6, :] * d) * d
        slope += s[4:5, :] + 2.0 * s[5:6, :] * d
        bend += s[5:6, :]
    out[...] = stack_rows(list(enumerate([norm, c, size, flat, slope, bend])), out.shape)


def shards(right_side, node_diag, local_coup, block_cols, border_coup, border_send, border_rows):
    width, ncols = right_side.shape
    nblocks, _, bs, _ = local_coup.shape
    n_gx, n_gy, n_nd = (lax.axis_size(a) for a in AXES)
    assert n_nd == 2 and border_coup.shape[1] == 4 * SIDE
    swap = [(0, 1), (1, 0)]
    right = [(i, (i + 1) % n_gx) for i in range(n_gx)]
    left = [(j, i) for i, j in right]
    up = [(i, i + 1) for i in range(n_gy - 1)]
    down = [(j, i) for i, j in up]
    facing = jnp.where(lax.axis_index("gy") == 0, 3, 2).astype(jnp.int32)
    if n_gy == 2:
        sides = [(swap, None, 2.0)]
    elif n_gy > 2:
        sides = [(up, 2, 2.0), (down, 3, 0.0)]
    else:
        sides = []
    sends = [("gx", right), ("gx", left)] + [("gy", perm) for perm, _, _ in sides]
    gives = [1, 0] + [None if t is None else t ^ 1 for _, t, _ in sides]
    toward = jnp.full((1, 4 * SIDE), facing)
    marks = jnp.stack([facing, lax.axis_index("nd").astype(jnp.int32)])
    border = border_coup[0]

    def smem(n):
        return [pl.BlockSpec(memory_space=pltpu.SMEM)] * n

    pay_shape = (width + bs + TAIL, ncols)

    def pack(gives):
        count = len(gives)
        tables = [marks] if None in gives else []
        return pl.pallas_call(
            partial(pack_kernel, gives),
            name="pack",
            in_specs=smem(len(tables)) + [pl.BlockSpec(memory_space=pl.ANY)] * 5,
            out_specs=[vmem()] * count,
            out_shape=[pltpu.VMEM(pay_shape, F32)] * count,
            scratch_shapes=[
                pltpu.SemaphoreType.DMA((count, SIDE + 1)),
                pltpu.VMEM((3, 1, 4 * SIDE), jnp.int32),
                pltpu.SemaphoreType.DMA((3,)),
            ],
            compiler_params=pltpu.CompilerParams(vmem_limit_bytes=LIMIT),
        )(*tables, *[pltpu.with_memory_space_constraint(a, pltpu.HBM) for a in (right_side, border, border_send, border_rows)], toward)

    packed = [*pack(gives[:1]), *pack(gives[1:])]
    pays = [lax.ppermute(pay, axis, perm) for pay, (axis, perm) in zip(packed, sends)]
    mine = packed[0]
    mate = lax.ppermute(right_side, "nd", swap)

    def tabled(kernel, name, tables, shapes, flops=None):
        def run(*args):
            args = list(args[:tables]) + [pltpu.with_memory_space_constraint(a, pltpu.VMEM) for a in args[tables:]]
            return pl.pallas_call(
                kernel,
                name=name,
                in_specs=smem(tables) + [vmem()] * (len(args) - tables),
                out_specs=[vmem()] * len(shapes),
                out_shape=[pltpu.VMEM(shape, F32) for shape in shapes],
                compiler_params=pltpu.CompilerParams(vmem_limit_bytes=LIMIT),
                cost_estimate=flops and pl.CostEstimate(flops=flops, bytes_accessed=1 << 20, transcendentals=0),
            )(*args)

        return run

    field, square = (width, ncols), (width, width)
    own, pair = tabled(prep_kernel, "prep", 2, [square] * 2, 1 << 24)(
        block_cols, marks, node_diag.reshape(1, width), local_coup, mine
    )
    mate_pair = lax.ppermute(pair, "nd", swap)

    part, coup = call(base_kernel, "base", [field, square])(mine, own, pair, mate, mate_pair)
    part, once, left_coup, back = call(left_kernel, "left", [field, field, square, field])(mine, part, border, pays[0])
    side_coup = []
    for (_, take, weight), pay in zip(sides, pays[2:]):
        part, once, block = call(partial(gy_kernel, take, weight), "gy", [(width + EXTRA, ncols), field, square])(mine, part, once, border, pay)
        side_coup.append(block)
    left_w = lax.ppermute(part, "gx", right)
    image, half = call(right_kernel, "right", [field, (width, ncols // 2)])(mine, part, border, pays[1])
    mate_w = lax.ppermute(image, "nd", swap)
    part, lift, state = call(near_kernel, "near", [field, field, (TAIL, ncols)])(
        right_side, image, once, mate, mate_w, own, coup, pays[0], back
    )
    far = []
    take = None
    if sides:
        perm, take, _ = sides[0]
        far = [mine, side_coup[0], pays[2], lax.ppermute(half if take is None else image, "gy", perm)]
    (state,) = call(partial(far_kernel, take), "far", [(TAIL, ncols)])(
        right_side, image, part, state, lift, left_coup, left_w, *far
    )
    state = join(state)
    norm, c, size, form = (row[None] for row in state[:4])
    ratio = size / (c * c * norm)
    last = size / (form - ratio * ratio * c * c * c * norm)
    return ((1.0 + last * c * (1.0 + ratio)) / c) * right_side - (last / c) * image


def solution(mesh):
    blocks = P(("var", "gx", "gy", "nd"))
    tables = P(AXES)
    in_specs = (blocks, blocks, blocks, tables, blocks, tables, tables)
    return jax.shard_map(shards, mesh=mesh, in_specs=in_specs, out_specs=blocks, check_vma=False)
```

```python
from functools import partial

import jax
import jax.numpy as jnp
from jax import lax
from jax.experimental import pallas as pl
from jax.experimental.pallas import tpu as pltpu
from jax.sharding import PartitionSpec as P

F32 = jnp.float32
BF16 = jnp.bfloat16
AXES = ("gx", "gy", "nd")
SIDE = 2
LIMIT = 8 << 20
EXTRA = 8
TAIL = 8


def vmem():
    return pl.BlockSpec(memory_space=pltpu.VMEM)


def call(kernel, name, shapes, scratch=(), flops=None):
    def run(*args):
        args = [pltpu.with_memory_space_constraint(a, pltpu.VMEM) for a in args]
        return pl.pallas_call(
            kernel,
            name=name,
            in_specs=[vmem()] * len(args),
            out_specs=[vmem()] * len(shapes),
            out_shape=[pltpu.VMEM(shape, F32) for shape in shapes],
            scratch_shapes=scratch,
            compiler_params=pltpu.CompilerParams(vmem_limit_bytes=LIMIT),
            cost_estimate=flops and pl.CostEstimate(flops=flops, bytes_accessed=1 << 20, transcendentals=0),
        )(*args)

    return run


def join(state):
    count = lax.axis_size(AXES)
    assert count & (count - 1) == 0
    step = 1
    while step < count:
        masks = [m * step for m in (1, 2, 3) if m * step < count]
        others = [lax.ppermute(state, AXES, [(i, i ^ m) for i in range(count)]) for m in masks]
        (state,) = call(merge_kernel, "merge", [state.shape])(state, *others)
        step *= 4
    return state


def split(a):
    high = a.astype(BF16)
    return high, (a - high.astype(F32)).astype(BF16)


def dot(a, b):
    (ah, al), (bh, bl) = split(a), split(b)
    mul = partial(jnp.dot, preferred_element_type=F32)
    return mul(ah, bh) + (mul(ah, bl) + mul(al, bh))


def col_sum(a, b):
    return jnp.sum(a * b, axis=0, keepdims=True)


def stack_rows(rows, shape):
    line = lax.broadcasted_iota(jnp.int32, shape, 0)
    return sum(jnp.where(line == n, row, 0.0) for n, row in rows)


def pack_kernel(gives, *refs):
    marks, refs = (refs[0], refs[1:]) if gives != [1] else (None, refs)
    field, border, send, rows, toward, *pays, sems, table, table_sems, whole = refs
    width = field.shape[0]
    bs = border.shape[1]
    tables = [pltpu.make_async_copy(ref, table.at[n], table_sems.at[n]) for n, ref in enumerate((rows, send, toward))]
    copies, tails, split = [], [], []
    for n, give in enumerate(gives):
        pay = pays.pop(0)
        tails.append(pay)
        if give == "halves":
            other = pays.pop(0)
            for s in range(SIDE):
                copies.append(pltpu.make_async_copy(border.at[s], pay.at[pl.ds(width + s * bs, bs), :], sems.at[n, s]))
            copies.append(pltpu.make_async_copy(field, whole, sems.at[n, SIDE]))
            split.append((pay, other))
        else:
            give = marks[0] if give is None else give
            copies.append(pltpu.make_async_copy(field, pay.at[pl.ds(0, width), :], sems.at[n, SIDE]))
            for s in range(SIDE):
                block = pay.at[pl.ds(width, bs), pl.ds(s * bs, bs)]
                copies.append(pltpu.make_async_copy(border.at[give * SIDE + s], block, sems.at[n, s]))
    for copy in tables + copies:
        copy.start()
    for copy in tables:
        copy.wait()
    count = table.shape[2]
    for pay in tails:
        for n in range(3):
            pay[pl.ds(pay.shape[0] - TAIL + n, 1), pl.ds(0, count)] = table[n].astype(F32)
    for copy in copies:
        copy.wait()
    for pay, other in split:
        low, high = whole[:, : whole.shape[1] // 2], whole[:, whole.shape[1] // 2 :]
        pay[pl.ds(0, width), :] = jnp.where(marks[0] == 3, high, low)
        other[pl.ds(0, width), :] = jnp.where(marks[0] == 3, low, high)


def prep_kernel(cols, marks, diag, local, packed, own, pair):
    nblocks, nonzeros, bs, _ = local.shape
    width = nblocks * bs
    patch_len = 2 * nblocks
    base = marks[1] * nblocks
    own[...] = jnp.zeros((width, width), F32)
    pair[...] = jnp.zeros((width, width), F32)
    for b in range(nblocks):
        for k in range(nonzeros):
            spot = lax.rem(cols[b, k] - base + patch_len, patch_len)
            block = local[b, k]
            for c in range(nblocks):

                @pl.when(spot == c)
                def _():
                    own[pl.ds(b * bs, bs), pl.ds(c * bs, bs)] += block

                @pl.when(spot == c + nblocks)
                def _():
                    pair[pl.ds(b * bs, bs), pl.ds(c * bs, bs)] += block

    lower = own[...]
    here = lax.broadcasted_iota(jnp.int32, (width, width), 0)
    there = lax.broadcasted_iota(jnp.int32, (width, width), 1)
    own[...] = lower + lower.T + jnp.where(here == there, diag[...], 0.0)


def edge(take, width, mine, pay, border):
    bs = border.shape[1]
    known = isinstance(take, int)

    def pick(of):
        return of(take) if known else jnp.where(take == 2.0, of(2), of(3))

    def number(ref, line, t):
        return ref[pl.ds(ref.shape[0] - TAIL + line, 1), pl.ds(t * SIDE + s, 1)]

    blocks = [[0.0] * (width // bs) for _ in range(width // bs)]
    for s in range(SIDE):
        beside = pay.shape[1] > bs
        turned = (pay[pl.ds(width, bs), pl.ds(s * bs, bs)] if beside else pay[pl.ds(width + s * bs, bs), :]).T
        pairs = [
            (pick(lambda t: border[t * SIDE + s]), pick(lambda t: number(mine, 0, t)), pick(lambda t: number(pay, 1, t))),
            (turned, pick(lambda t: number(mine, 1, t ^ 1)), pick(lambda t: number(pay, 0, t ^ 1))),
        ]
        for block, to, at in pairs:
            for i, line in enumerate(blocks):
                for j in range(len(line)):
                    line[j] = line[j] + jnp.where((to == i) & (at == j), block, 0.0)
    return jnp.concatenate([jnp.concatenate(line, axis=1) for line in blocks], axis=0)


def base_kernel(mine, own, pair, mate, mate_pair, image, coup):
    width = mate.shape[0]
    coup[...] = pair[...] + mate_pair[...].T
    image[...] = dot(own[...], mine[pl.ds(0, width), :]) + dot(coup[...], mate[...])


def left_kernel(mine, part, border, pay, image, once, coup, back):
    width = part.shape[0]
    coup[...] = edge(0, width, mine, pay, border)
    term = dot(coup[...], pay[pl.ds(0, width), :])
    image[...] = part[...] + term
    once[...] = part[...] + 2.0 * term
    back[...] = dot(coup[...].T, mine[pl.ds(0, width), :])


def turn(mine, width):
    toward = mine[pl.ds(mine.shape[0] - TAIL + 2, 1), pl.ds(0, 1)]
    count = mine.shape[1]
    first = jnp.where(lax.broadcasted_iota(jnp.int32, (1, count), 1) < count // 2, 1.0, 0.0)
    return jnp.where(toward == 3.0, first, 1.0 - first)


def gy_kernel(take, weight, mine, part, single, border, pay, image, once, coup):
    width = coup.shape[0]
    toward = mine[pl.ds(mine.shape[0] - TAIL + 2, 1), pl.ds(0, 1)]
    coup[...] = edge(toward if take is None else take, width, mine, pay, border)
    term = dot(coup[...], pay[pl.ds(0, width), :])
    image[...] = part[...] + term
    scale = weight * turn(mine, width) if take is None else weight
    once[...] = single[...] + scale * term


def columns(ref, toward, out):
    middle = ref.shape[1] // 2
    return jnp.where((toward == 3.0) == out, ref[:, middle:], ref[:, :middle])


def right_kernel(mine, part, border, pay, half, across, coup, pass_on):
    width = part.shape[0]
    toward = mine[pl.ds(mine.shape[0] - TAIL + 2, 1), pl.ds(0, 1)]
    coup[...] = edge(1, width, mine, pay, border)
    half[...] = columns(part, toward, True) + dot(coup[...], pay[pl.ds(0, width), :])
    across[pl.ds(0, width), :] = half[...]
    across[pl.ds(width, EXTRA), :] = jnp.zeros((EXTRA, half.shape[1]), F32)
    pass_on[...] = part[...]


def joined(toward, out, other):
    low = jnp.where(toward == 3.0, other, out)
    high = jnp.where(toward == 3.0, out, other)
    return jnp.concatenate([low, high], axis=1)


def whole_kernel(mine, part, half, coup, pay, image, other):
    toward = mine[pl.ds(mine.shape[0] - TAIL + 2, 1), pl.ds(0, 1)]
    other[...] = columns(part, toward, False) + dot(coup[...], pay[pl.ds(0, part.shape[0]), :])
    image[...] = joined(toward, half[...], other[...])


def near_kernel(mine, field, image, once, mate, mate_out, mate_other, own, coup, pay, back, part, lift, state):
    b = field[...]
    toward = mine[pl.ds(mine.shape[0] - TAIL + 2, 1), pl.ds(0, 1)]
    mate_w = joined(toward, mate_out[...], mate_other[...])
    norm = col_sum(b, b)
    c = jnp.where(norm > 0.0, col_sum(b, image[...]) / jnp.where(norm > 0.0, norm, 1.0), 0.0)
    g = image[...] - c * b
    part[...] = dot(own[...], g) + dot(coup[...], mate_w - c * mate[...])
    lift[...] = back[...] - c * pay[pl.ds(0, b.shape[0]), :]
    rows = [(0, norm), (1, c), (2, col_sum(g, g)), (4, -col_sum(g, once[...])), (5, col_sum(b, once[...]))]
    state[...] = stack_rows(rows, state.shape)


def far_kernel(take, field, image, part, near, lift, coup, left, *refs):
    *sides, state = refs
    width = field.shape[0]
    b = field[...]
    c = near[1:2, :]
    acc = part[...] + 2.0 * dot(coup[...], left[...] + lift[...])
    if sides:
        mine, coup_gy, pay, side = sides
        if take is None:
            toward = mine[pl.ds(mine.shape[0] - TAIL + 2, 1), pl.ds(0, 1)]
            middle = b.shape[1] // 2
            shift = c * pay[pl.ds(0, width), :]
            term = dot(coup_gy[...], side[pl.ds(0, width), :] - jnp.where(toward == 3.0, shift[:, :middle], shift[:, middle:]))
            acc += 2.0 * turn(mine, width) * jnp.concatenate([term, term], axis=1)
        else:
            acc += 2.0 * dot(coup_gy[...], side[...] - c * pay[pl.ds(0, width), :])
    state[...] = near[...] + stack_rows([(3, col_sum(image[...] - c * b, acc)), (4, -col_sum(b, acc))], state.shape)


def merge_kernel(*refs):
    *states, out = refs
    norm = sum(s[0:1, :] for s in states)
    base = states[0][1:2, :]
    shift = sum(s[0:1, :] * (s[1:2, :] - base) for s in states)
    c = base + jnp.where(norm > 0.0, shift / jnp.where(norm > 0.0, norm, 1.0), 0.0)
    size, flat, slope, bend = (jnp.zeros_like(c) for _ in range(4))
    for s in states:
        d = c - s[1:2, :]
        size += s[2:3, :] + s[0:1, :] * d * d
        flat += s[3:4, :] + (s[4:5, :] + s[5:6, :] * d) * d
        slope += s[4:5, :] + 2.0 * s[5:6, :] * d
        bend += s[5:6, :]
    out[...] = stack_rows(list(enumerate([norm, c, size, flat, slope, bend])), out.shape)


def shards(right_side, node_diag, local_coup, block_cols, border_coup, border_send, border_rows):
    width, ncols = right_side.shape
    nblocks, _, bs, _ = local_coup.shape
    n_gx, n_gy, n_nd = (lax.axis_size(a) for a in AXES)
    assert n_nd == 2 and border_coup.shape[1] == 4 * SIDE
    swap = [(0, 1), (1, 0)]
    right = [(i, (i + 1) % n_gx) for i in range(n_gx)]
    left = [(j, i) for i, j in right]
    up = [(i, i + 1) for i in range(n_gy - 1)]
    down = [(j, i) for i, j in up]
    facing = jnp.where(lax.axis_index("gy") == 0, 3, 2).astype(jnp.int32)
    if n_gy == 2:
        sides = [(swap, None, 2.0)]
    elif n_gy > 2:
        sides = [(up, 2, 2.0), (down, 3, 0.0)]
    else:
        sides = []
    sends = [("gx", right), ("gx", left), ("gx", left)] + [("gy", perm) for perm, _, _ in sides]
    gives = [1, "halves"] + [None if t is None else t ^ 1 for _, t, _ in sides]
    toward = jnp.full((1, 4 * SIDE), facing)
    marks = jnp.stack([facing, lax.axis_index("nd").astype(jnp.int32)])
    border = border_coup[0]

    def smem(n):
        return [pl.BlockSpec(memory_space=pltpu.SMEM)] * n

    wider = width + EXTRA
    full, blocks, half = (width + bs + TAIL, ncols), (width + SIDE * bs + TAIL, ncols // 2), (width, ncols // 2)

    def pack(gives):
        shapes = sum(([blocks, (wider, ncols // 2)] if give == "halves" else [full] for give in gives), [])
        count = len(shapes)
        tables = [marks] if gives != [1] else []
        return pl.pallas_call(
            partial(pack_kernel, gives),
            name="pack",
            in_specs=smem(len(tables)) + [pl.BlockSpec(memory_space=pl.ANY)] * 5,
            out_specs=[vmem()] * count,
            out_shape=[pltpu.VMEM(shape, F32) for shape in shapes],
            scratch_shapes=[
                pltpu.SemaphoreType.DMA((count, SIDE + 1)),
                pltpu.VMEM((3, 1, 4 * SIDE), jnp.int32),
                pltpu.SemaphoreType.DMA((3,)),
                pltpu.VMEM((width, ncols), F32),
            ],
            compiler_params=pltpu.CompilerParams(vmem_limit_bytes=LIMIT),
        )(*tables, *[pltpu.with_memory_space_constraint(a, pltpu.HBM) for a in (right_side, border, border_send, border_rows)], toward)

    packed = [*pack(gives[:1]), *pack(gives[1:])]
    pays = [lax.ppermute(pay, axis, perm) for pay, (axis, perm) in zip(packed, sends)]
    mine = packed[0]
    mate = lax.ppermute(right_side, "nd", swap)

    def tabled(kernel, name, tables, shapes, flops=None):
        def run(*args):
            args = list(args[:tables]) + [pltpu.with_memory_space_constraint(a, pltpu.VMEM) for a in args[tables:]]
            return pl.pallas_call(
                kernel,
                name=name,
                in_specs=smem(tables) + [vmem()] * (len(args) - tables),
                out_specs=[vmem()] * len(shapes),
                out_shape=[pltpu.VMEM(shape, F32) for shape in shapes],
                compiler_params=pltpu.CompilerParams(vmem_limit_bytes=LIMIT),
                cost_estimate=flops and pl.CostEstimate(flops=flops, bytes_accessed=1 << 20, transcendentals=0),
            )(*args)

        return run

    field, square = (width, ncols), (width, width)
    own, pair = tabled(prep_kernel, "prep", 2, [square] * 2, 1 << 24)(
        block_cols, marks, node_diag.reshape(1, width), local_coup, mine
    )
    mate_pair = lax.ppermute(pair, "nd", swap)

    part, coup = call(base_kernel, "base", [field, square])(mine, own, pair, mate, mate_pair)
    part, once, left_coup, back = call(left_kernel, "left", [field, field, square, field])(mine, part, border, pays[0])
    side_coup = []
    for (_, take, weight), pay in zip(sides, pays[3:]):
        part, once, block = call(partial(gy_kernel, take, weight), "gy", [field, field, square])(mine, part, once, border, pay)
        side_coup.append(block)
    half_w, across, right_coup, pass_on = call(right_kernel, "right", [half, (wider, ncols // 2), square, field])(
        mine, part, border, pays[1]
    )
    left_w = lax.ppermute(pass_on, "gx", right)
    image, other_w = call(whole_kernel, "whole", [field, half])(mine, part, half_w, right_coup, pays[2])
    mate_w = [lax.ppermute(w, "nd", swap) for w in (half_w, other_w)]
    part, lift, state = call(near_kernel, "near", [field, field, (TAIL, ncols)])(
        mine, right_side, image, once, mate, *mate_w, own, coup, pays[0], back
    )
    far = []
    take = None
    if sides:
        perm, take, _ = sides[0]
        far = [mine, side_coup[0], pays[3], lax.ppermute(across if take is None else image, "gy", perm)]
    (state,) = call(partial(far_kernel, take), "far", [(TAIL, ncols)])(
        right_side, image, part, state, lift, left_coup, left_w, *far
    )
    state = join(state)
    norm, c, size, form = (row[None] for row in state[:4])
    ratio = size / (c * c * norm)
    last = size / (form - ratio * ratio * c * c * c * norm)
    return ((1.0 + last * c * (1.0 + ratio)) / c) * right_side - (last / c) * image


def solution(mesh):
    blocks = P(("var", "gx", "gy", "nd"))
    tables = P(AXES)
    in_specs = (blocks, blocks, blocks, tables, blocks, tables, tables)
    return jax.shard_map(shards, mesh=mesh, in_specs=in_specs, out_specs=blocks, check_vma=False)
```

```python
from functools import partial

import jax
import jax.numpy as jnp
from jax import lax
from jax.experimental import pallas as pl
from jax.experimental.pallas import tpu as pltpu
from jax.sharding import PartitionSpec as P

F32 = jnp.float32
BF16 = jnp.bfloat16
AXES = ("gx", "gy", "nd")
SIDE = 2
LIMIT = 8 << 20
EXTRA = 8
TAIL = 8


def vmem():
    return pl.BlockSpec(memory_space=pltpu.VMEM)


def call(kernel, name, shapes, scratch=(), flops=None):
    def run(*args):
        args = [pltpu.with_memory_space_constraint(a, pltpu.VMEM) for a in args]
        return pl.pallas_call(
            kernel,
            name=name,
            in_specs=[vmem()] * len(args),
            out_specs=[vmem()] * len(shapes),
            out_shape=[pltpu.VMEM(shape, F32) for shape in shapes],
            scratch_shapes=scratch,
            compiler_params=pltpu.CompilerParams(vmem_limit_bytes=LIMIT),
            cost_estimate=flops and pl.CostEstimate(flops=flops, bytes_accessed=1 << 20, transcendentals=0),
        )(*args)

    return run


def join(state):
    count = lax.axis_size(AXES)
    assert count & (count - 1) == 0
    step = 1
    while step < count:
        masks = [m * step for m in (1, 2, 3) if m * step < count]
        others = [lax.ppermute(state, AXES, [(i, i ^ m) for i in range(count)]) for m in masks]
        (state,) = call(merge_kernel, "merge", [state.shape])(state, *others)
        step *= 4
    return state


def split(a):
    high = a.astype(BF16)
    return high, (a - high.astype(F32)).astype(BF16)


def dot(a, b):
    (ah, al), (bh, bl) = split(a), split(b)
    mul = partial(jnp.dot, preferred_element_type=F32)
    return mul(ah, bh) + (mul(ah, bl) + mul(al, bh))


def col_sum(a, b):
    return jnp.sum(a * b, axis=0, keepdims=True)


def stack_rows(rows, shape):
    line = lax.broadcasted_iota(jnp.int32, shape, 0)
    return sum(jnp.where(line == n, row, 0.0) for n, row in rows)


def pack_kernel(gives, *refs):
    marks, refs = (refs[0], refs[1:]) if gives != [1] else (None, refs)
    field, border, send, rows, toward, *pays, sems, table, table_sems = refs
    width = field.shape[0]
    bs = border.shape[1]
    tables = [pltpu.make_async_copy(ref, table.at[n], table_sems.at[n]) for n, ref in enumerate((rows, send, toward))]
    copies = []
    for n, (give, pay) in enumerate(zip(gives, pays)):
        give = marks[0] if give is None else give
        copies.append(pltpu.make_async_copy(field, pay.at[pl.ds(0, width), :], sems.at[n, SIDE]))
        for s in range(SIDE):
            block = pay.at[pl.ds(width, bs), pl.ds(s * bs, bs)]
            copies.append(pltpu.make_async_copy(border.at[give * SIDE + s], block, sems.at[n, s]))
    for copy in tables + copies:
        copy.start()
    for copy in tables:
        copy.wait()
    count = table.shape[2]
    for pay in pays:
        for n in range(3):
            pay[pl.ds(pay.shape[0] - TAIL + n, 1), pl.ds(0, count)] = table[n].astype(F32)
    for copy in copies:
        copy.wait()


def pack_right_kernel(mine, field, border, low, high, pay, other):
    width = field.shape[0]
    bs = border.shape[1]
    last = mine.shape[0] - TAIL
    toward = mine[pl.ds(last + 2, 1), pl.ds(0, 1)]
    pay[pl.ds(0, width), :] = columns(field, toward, True)
    for s in range(SIDE):
        pay[pl.ds(width + s * bs, bs), :] = border[s]
    pay[pl.ds(width + SIDE * bs, TAIL), :] = mine[pl.ds(last, TAIL), pl.ds(0, bs)]
    other[pl.ds(0, width), :] = columns(field, toward, False)


def prep_kernel(cols, marks, diag, local, packed, own, pair, low, high):
    nblocks, nonzeros, bs, _ = local.shape
    width = nblocks * bs
    patch_len = 2 * nblocks
    base = marks[1] * nblocks
    own[...] = jnp.zeros((width, width), F32)
    pair[...] = jnp.zeros((width, width), F32)
    for b in range(nblocks):
        for k in range(nonzeros):
            spot = lax.rem(cols[b, k] - base + patch_len, patch_len)
            block = local[b, k]
            for c in range(nblocks):

                @pl.when(spot == c)
                def _():
                    own[pl.ds(b * bs, bs), pl.ds(c * bs, bs)] += block

                @pl.when(spot == c + nblocks)
                def _():
                    pair[pl.ds(b * bs, bs), pl.ds(c * bs, bs)] += block

    lower = own[...]
    here = lax.broadcasted_iota(jnp.int32, (width, width), 0)
    there = lax.broadcasted_iota(jnp.int32, (width, width), 1)
    own[...] = lower + lower.T + jnp.where(here == there, diag[...], 0.0)
    low[...] = pair[:, : width // 2]
    high[...] = pair[:, width // 2 :]


def edge(take, width, mine, pay, border):
    bs = border.shape[1]
    known = isinstance(take, int)

    def pick(of):
        return of(take) if known else jnp.where(take == 2.0, of(2), of(3))

    def number(ref, line, t):
        return ref[pl.ds(ref.shape[0] - TAIL + line, 1), pl.ds(t * SIDE + s, 1)]

    blocks = [[0.0] * (width // bs) for _ in range(width // bs)]
    for s in range(SIDE):
        beside = pay.shape[1] > bs
        turned = (pay[pl.ds(width, bs), pl.ds(s * bs, bs)] if beside else pay[pl.ds(width + s * bs, bs), :]).T
        pairs = [
            (pick(lambda t: border[t * SIDE + s]), pick(lambda t: number(mine, 0, t)), pick(lambda t: number(pay, 1, t))),
            (turned, pick(lambda t: number(mine, 1, t ^ 1)), pick(lambda t: number(pay, 0, t ^ 1))),
        ]
        for block, to, at in pairs:
            for i, line in enumerate(blocks):
                for j in range(len(line)):
                    line[j] = line[j] + jnp.where((to == i) & (at == j), block, 0.0)
    return jnp.concatenate([jnp.concatenate(line, axis=1) for line in blocks], axis=0)


def base_kernel(mine, own, pair, mate, low, high, image, coup):
    width = mate.shape[0]
    coup[...] = pair[...] + jnp.concatenate([low[...].T, high[...].T], axis=0)
    image[...] = dot(own[...], mine[pl.ds(0, width), :]) + dot(coup[...], mate[...])


def left_kernel(mine, part, border, pay, image, once, coup, back):
    width = part.shape[0]
    coup[...] = edge(0, width, mine, pay, border)
    term = dot(coup[...], pay[pl.ds(0, width), :])
    image[...] = part[...] + term
    once[...] = part[...] + 2.0 * term
    back[...] = dot(coup[...].T, mine[pl.ds(0, width), :])


def turn(mine, width):
    toward = mine[pl.ds(mine.shape[0] - TAIL + 2, 1), pl.ds(0, 1)]
    count = mine.shape[1]
    first = jnp.where(lax.broadcasted_iota(jnp.int32, (1, count), 1) < count // 2, 1.0, 0.0)
    return jnp.where(toward == 3.0, first, 1.0 - first)


def gy_kernel(take, weight, mine, part, single, border, pay, image, once, coup):
    width = coup.shape[0]
    toward = mine[pl.ds(mine.shape[0] - TAIL + 2, 1), pl.ds(0, 1)]
    coup[...] = edge(toward if take is None else take, width, mine, pay, border)
    term = dot(coup[...], pay[pl.ds(0, width), :])
    image[...] = part[...] + term
    scale = weight * turn(mine, width) if take is None else weight
    once[...] = single[...] + scale * term


def columns(ref, toward, out):
    middle = ref.shape[1] // 2
    return jnp.where((toward == 3.0) == out, ref[:, middle:], ref[:, :middle])


def right_kernel(mine, part, border, pay, half, across, coup, pass_on):
    width = part.shape[0]
    toward = mine[pl.ds(mine.shape[0] - TAIL + 2, 1), pl.ds(0, 1)]
    coup[...] = edge(1, width, mine, pay, border)
    half[...] = columns(part, toward, True) + dot(coup[...], pay[pl.ds(0, width), :])
    across[pl.ds(0, width), :] = half[...]
    across[pl.ds(width, EXTRA), :] = jnp.zeros((EXTRA, half.shape[1]), F32)
    pass_on[...] = part[...]


def joined(toward, out, other):
    low = jnp.where(toward == 3.0, other, out)
    high = jnp.where(toward == 3.0, out, other)
    return jnp.concatenate([low, high], axis=1)


def whole_kernel(mine, part, half, coup, pay, image, other):
    toward = mine[pl.ds(mine.shape[0] - TAIL + 2, 1), pl.ds(0, 1)]
    other[...] = columns(part, toward, False) + dot(coup[...], pay[pl.ds(0, part.shape[0]), :])
    image[...] = joined(toward, half[...], other[...])


def near_kernel(mine, field, image, once, mate, mate_out, mate_other, own, coup, pay, back, part, lift, state):
    b = field[...]
    toward = mine[pl.ds(mine.shape[0] - TAIL + 2, 1), pl.ds(0, 1)]
    mate_w = joined(toward, mate_out[...], mate_other[...])
    norm = col_sum(b, b)
    c = jnp.where(norm > 0.0, col_sum(b, image[...]) / jnp.where(norm > 0.0, norm, 1.0), 0.0)
    g = image[...] - c * b
    part[...] = dot(own[...], g) + dot(coup[...], mate_w - c * mate[...])
    lift[...] = back[...] - c * pay[pl.ds(0, b.shape[0]), :]
    rows = [(0, norm), (1, c), (2, col_sum(g, g)), (4, -col_sum(g, once[...])), (5, col_sum(b, once[...]))]
    state[...] = stack_rows(rows, state.shape)


def far_kernel(take, field, image, part, near, lift, coup, left, *refs):
    *sides, state = refs
    width = field.shape[0]
    b = field[...]
    c = near[1:2, :]
    acc = part[...] + 2.0 * dot(coup[...], left[...] + lift[...])
    if sides:
        mine, coup_gy, pay, side = sides
        if take is None:
            toward = mine[pl.ds(mine.shape[0] - TAIL + 2, 1), pl.ds(0, 1)]
            middle = b.shape[1] // 2
            shift = c * pay[pl.ds(0, width), :]
            term = dot(coup_gy[...], side[pl.ds(0, width), :] - jnp.where(toward == 3.0, shift[:, :middle], shift[:, middle:]))
            acc += 2.0 * turn(mine, width) * jnp.concatenate([term, term], axis=1)
        else:
            acc += 2.0 * dot(coup_gy[...], side[...] - c * pay[pl.ds(0, width), :])
    state[...] = near[...] + stack_rows([(3, col_sum(image[...] - c * b, acc)), (4, -col_sum(b, acc))], state.shape)


def merge_kernel(*refs):
    *states, out = refs
    norm = sum(s[0:1, :] for s in states)
    base = states[0][1:2, :]
    shift = sum(s[0:1, :] * (s[1:2, :] - base) for s in states)
    c = base + jnp.where(norm > 0.0, shift / jnp.where(norm > 0.0, norm, 1.0), 0.0)
    size, flat, slope, bend = (jnp.zeros_like(c) for _ in range(4))
    for s in states:
        d = c - s[1:2, :]
        size += s[2:3, :] + s[0:1, :] * d * d
        flat += s[3:4, :] + (s[4:5, :] + s[5:6, :] * d) * d
        slope += s[4:5, :] + 2.0 * s[5:6, :] * d
        bend += s[5:6, :]
    out[...] = stack_rows(list(enumerate([norm, c, size, flat, slope, bend])), out.shape)


def shards(right_side, node_diag, local_coup, block_cols, border_coup, border_send, border_rows):
    width, ncols = right_side.shape
    nblocks, _, bs, _ = local_coup.shape
    n_gx, n_gy, n_nd = (lax.axis_size(a) for a in AXES)
    assert n_nd == 2 and border_coup.shape[1] == 4 * SIDE
    swap = [(0, 1), (1, 0)]
    right = [(i, (i + 1) % n_gx) for i in range(n_gx)]
    left = [(j, i) for i, j in right]
    up = [(i, i + 1) for i in range(n_gy - 1)]
    down = [(j, i) for i, j in up]
    facing = jnp.where(lax.axis_index("gy") == 0, 3, 2).astype(jnp.int32)
    if n_gy == 2:
        sides = [(swap, None, 2.0)]
    elif n_gy > 2:
        sides = [(up, 2, 2.0), (down, 3, 0.0)]
    else:
        sides = []
    sends = [("gx", right)] + [("gy", perm) for perm, _, _ in sides]
    gives = [1] + [None if t is None else t ^ 1 for _, t, _ in sides]
    toward = jnp.full((1, 4 * SIDE), facing)
    marks = jnp.stack([facing, lax.axis_index("nd").astype(jnp.int32)])
    border = border_coup[0]

    def smem(n):
        return [pl.BlockSpec(memory_space=pltpu.SMEM)] * n

    wider = width + EXTRA
    full, blocks, half = (width + bs + TAIL, ncols), (width + SIDE * bs + TAIL, ncols // 2), (width, ncols // 2)

    def pack(gives):
        count = len(gives)
        tables = [marks] if gives != [1] else []
        return pl.pallas_call(
            partial(pack_kernel, gives),
            name="pack",
            in_specs=smem(len(tables)) + [pl.BlockSpec(memory_space=pl.ANY)] * 5,
            out_specs=[vmem()] * count,
            out_shape=[pltpu.VMEM(full, F32)] * count,
            scratch_shapes=[
                pltpu.SemaphoreType.DMA((count, SIDE + 1)),
                pltpu.VMEM((3, 1, 4 * SIDE), jnp.int32),
                pltpu.SemaphoreType.DMA((3,)),
            ],
            compiler_params=pltpu.CompilerParams(vmem_limit_bytes=LIMIT),
        )(*tables, *[pltpu.with_memory_space_constraint(a, pltpu.HBM) for a in (right_side, border, border_send, border_rows)], toward)

    packed = [*pack(gives[:1]), *(pack(gives[1:]) if sides else [])]
    pays = [lax.ppermute(pay, axis, perm) for pay, (axis, perm) in zip(packed, sends)]
    mine = packed[0]
    mate = lax.ppermute(right_side, "nd", swap)

    def tabled(kernel, name, tables, shapes, flops=None):
        def run(*args):
            args = list(args[:tables]) + [pltpu.with_memory_space_constraint(a, pltpu.VMEM) for a in args[tables:]]
            return pl.pallas_call(
                kernel,
                name=name,
                in_specs=smem(tables) + [vmem()] * (len(args) - tables),
                out_specs=[vmem()] * len(shapes),
                out_shape=[pltpu.VMEM(shape, F32) for shape in shapes],
                compiler_params=pltpu.CompilerParams(vmem_limit_bytes=LIMIT),
                cost_estimate=flops and pl.CostEstimate(flops=flops, bytes_accessed=1 << 20, transcendentals=0),
            )(*args)

        return run

    field, square = (width, ncols), (width, width)
    own, pair, *pieces = tabled(prep_kernel, "prep", 2, [square] * 2 + [(width, width // 2)] * 2, 1 << 24)(
        block_cols, marks, node_diag.reshape(1, width), local_coup, mine
    )
    mate_pair = [lax.ppermute(piece, "nd", swap) for piece in pieces]

    part, coup = call(base_kernel, "base", [field, square])(mine, own, pair, mate, *mate_pair)
    to_left = call(pack_right_kernel, "pack_right", [blocks, (wider, ncols // 2)])(
        mine, right_side, border, *mate_pair
    )
    from_right = [lax.ppermute(pay, "gx", left) for pay in to_left]
    part, once, left_coup, back = call(left_kernel, "left", [field, field, square, field])(mine, part, border, pays[0])
    side_coup = []
    for (_, take, weight), pay in zip(sides, pays[1:]):
        part, once, block = call(partial(gy_kernel, take, weight), "gy", [field, field, square])(mine, part, once, border, pay)
        side_coup.append(block)
    half_w, across, right_coup, pass_on = call(right_kernel, "right", [half, (wider, ncols // 2), square, field])(
        mine, part, border, from_right[0]
    )
    left_w = lax.ppermute(pass_on, "gx", right)
    image, other_w = call(whole_kernel, "whole", [field, half])(mine, part, half_w, right_coup, from_right[1])
    mate_w = [lax.ppermute(w, "nd", swap) for w in (half_w, other_w)]
    part, lift, state = call(near_kernel, "near", [field, field, (TAIL, ncols)])(
        mine, right_side, image, once, mate, *mate_w, own, coup, pays[0], back
    )
    far = []
    take = None
    if sides:
        perm, take, _ = sides[0]
        far = [mine, side_coup[0], pays[1], lax.ppermute(across if take is None else image, "gy", perm)]
    (state,) = call(partial(far_kernel, take), "far", [(TAIL, ncols)])(
        right_side, image, part, state, lift, left_coup, left_w, *far
    )
    state = join(state)
    norm, c, size, form = (row[None] for row in state[:4])
    ratio = size / (c * c * norm)
    last = size / (form - ratio * ratio * c * c * c * norm)
    return ((1.0 + last * c * (1.0 + ratio)) / c) * right_side - (last / c) * image


def solution(mesh):
    blocks = P(("var", "gx", "gy", "nd"))
    tables = P(AXES)
    in_specs = (blocks, blocks, blocks, tables, blocks, tables, tables)
    return jax.shard_map(shards, mesh=mesh, in_specs=in_specs, out_specs=blocks, check_vma=False)
```

```python
from functools import partial

import jax
import jax.numpy as jnp
from jax import lax
from jax.experimental import pallas as pl
from jax.experimental.pallas import tpu as pltpu
from jax.sharding import PartitionSpec as P

F32 = jnp.float32
BF16 = jnp.bfloat16
AXES = ("gx", "gy", "nd")
SIDE = 2
LIMIT = 8 << 20
EXTRA = 8
TAIL = 8


def vmem():
    return pl.BlockSpec(memory_space=pltpu.VMEM)


def call(kernel, name, shapes, scratch=(), flops=None):
    def run(*args):
        args = [pltpu.with_memory_space_constraint(a, pltpu.VMEM) for a in args]
        return pl.pallas_call(
            kernel,
            name=name,
            in_specs=[vmem()] * len(args),
            out_specs=[vmem()] * len(shapes),
            out_shape=[pltpu.VMEM(shape, F32) for shape in shapes],
            scratch_shapes=scratch,
            compiler_params=pltpu.CompilerParams(vmem_limit_bytes=LIMIT),
            cost_estimate=flops and pl.CostEstimate(flops=flops, bytes_accessed=1 << 20, transcendentals=0),
        )(*args)

    return run


def join(state):
    count = lax.axis_size(AXES)
    assert count & (count - 1) == 0
    step = 1
    while step < count:
        masks = [m * step for m in (1, 2, 3) if m * step < count]
        others = [lax.ppermute(state, AXES, [(i, i ^ m) for i in range(count)]) for m in masks]
        (state,) = call(merge_kernel, "merge", [state.shape])(state, *others)
        step *= 4
    return state


def split(a):
    high = a.astype(BF16)
    return high, (a - high.astype(F32)).astype(BF16)


def dot(a, b):
    (ah, al), (bh, bl) = split(a), split(b)
    mul = partial(jnp.dot, preferred_element_type=F32)
    return mul(ah, bh) + (mul(ah, bl) + mul(al, bh))


def col_sum(a, b):
    return jnp.sum(a * b, axis=0, keepdims=True)


def stack_rows(rows, shape):
    line = lax.broadcasted_iota(jnp.int32, shape, 0)
    return sum(jnp.where(line == n, row, 0.0) for n, row in rows)


def pack_kernel(gives, *refs):
    marks, refs = (refs[0], refs[1:]) if gives != [1] else (None, refs)
    field, border, send, rows, toward, *pays, sems, table, table_sems = refs
    width = field.shape[0]
    bs = border.shape[1]
    tables = [pltpu.make_async_copy(ref, table.at[n], table_sems.at[n]) for n, ref in enumerate((rows, send, toward))]
    copies = []
    for n, (give, pay) in enumerate(zip(gives, pays)):
        give = marks[0] if give is None else give
        copies.append(pltpu.make_async_copy(field, pay.at[pl.ds(0, width), :], sems.at[n, SIDE]))
        for s in range(SIDE):
            block = pay.at[pl.ds(width, bs), pl.ds(s * bs, bs)]
            copies.append(pltpu.make_async_copy(border.at[give * SIDE + s], block, sems.at[n, s]))
    for copy in tables + copies:
        copy.start()
    for copy in tables:
        copy.wait()
    count = table.shape[2]
    for pay in pays:
        for n in range(3):
            pay[pl.ds(pay.shape[0] - TAIL + n, 1), pl.ds(0, count)] = table[n].astype(F32)
    for copy in copies:
        copy.wait()


def prep_kernel(cols, marks, diag, local, packed, own, pair, low, high):
    nblocks, nonzeros, bs, _ = local.shape
    width = nblocks * bs
    patch_len = 2 * nblocks
    base = marks[1] * nblocks
    own[...] = jnp.zeros((width, width), F32)
    pair[...] = jnp.zeros((width, width), F32)
    for b in range(nblocks):
        for k in range(nonzeros):
            spot = lax.rem(cols[b, k] - base + patch_len, patch_len)
            block = local[b, k]
            for c in range(nblocks):

                @pl.when(spot == c)
                def _():
                    own[pl.ds(b * bs, bs), pl.ds(c * bs, bs)] += block

                @pl.when(spot == c + nblocks)
                def _():
                    pair[pl.ds(b * bs, bs), pl.ds(c * bs, bs)] += block

    lower = own[...]
    here = lax.broadcasted_iota(jnp.int32, (width, width), 0)
    there = lax.broadcasted_iota(jnp.int32, (width, width), 1)
    own[...] = lower + lower.T + jnp.where(here == there, diag[...], 0.0)
    low[...] = pair[:, : width // 2]
    high[...] = pair[:, width // 2 :]


def edge(take, width, mine, pay, border):
    bs = border.shape[1]
    known = isinstance(take, int)

    def pick(of):
        return of(take) if known else jnp.where(take == 2.0, of(2), of(3))

    def number(ref, line, t):
        return ref[pl.ds(ref.shape[0] - TAIL + line, 1), pl.ds(t * SIDE + s, 1)]

    blocks = [[0.0] * (width // bs) for _ in range(width // bs)]
    for s in range(SIDE):
        beside = pay.shape[1] > bs
        turned = (pay[pl.ds(width, bs), pl.ds(s * bs, bs)] if beside else pay[pl.ds(width + s * bs, bs), :]).T
        pairs = [
            (pick(lambda t: border[t * SIDE + s]), pick(lambda t: number(mine, 0, t)), pick(lambda t: number(pay, 1, t))),
            (turned, pick(lambda t: number(mine, 1, t ^ 1)), pick(lambda t: number(pay, 0, t ^ 1))),
        ]
        for block, to, at in pairs:
            for i, line in enumerate(blocks):
                for j in range(len(line)):
                    line[j] = line[j] + jnp.where((to == i) & (at == j), block, 0.0)
    return jnp.concatenate([jnp.concatenate(line, axis=1) for line in blocks], axis=0)


def base_kernel(mine, own, pair, mate, low, high, image, coup):
    width = mate.shape[0]
    coup[...] = pair[...] + jnp.concatenate([low[...].T, high[...].T], axis=0)
    image[...] = dot(own[...], mine[pl.ds(0, width), :]) + dot(coup[...], mate[...])


def left_kernel(mine, part, border, pay, image, once, coup, back, out, other):
    width = part.shape[0]
    toward = mine[pl.ds(mine.shape[0] - TAIL + 2, 1), pl.ds(0, 1)]
    coup[...] = edge(0, width, mine, pay, border)
    back[...] = dot(coup[...].T, mine[pl.ds(0, width), :])
    out[pl.ds(0, width), :] = columns(back, toward, True)
    other[pl.ds(0, width), :] = columns(back, toward, False)
    term = dot(coup[...], pay[pl.ds(0, width), :])
    image[...] = part[...] + term
    once[...] = part[...] + 2.0 * term


def turn(mine, width):
    toward = mine[pl.ds(mine.shape[0] - TAIL + 2, 1), pl.ds(0, 1)]
    count = mine.shape[1]
    first = jnp.where(lax.broadcasted_iota(jnp.int32, (1, count), 1) < count // 2, 1.0, 0.0)
    return jnp.where(toward == 3.0, first, 1.0 - first)


def gy_kernel(take, weight, mine, part, single, border, pay, image, once, coup):
    width = coup.shape[0]
    toward = mine[pl.ds(mine.shape[0] - TAIL + 2, 1), pl.ds(0, 1)]
    coup[...] = edge(toward if take is None else take, width, mine, pay, border)
    term = dot(coup[...], pay[pl.ds(0, width), :])
    image[...] = part[...] + term
    scale = weight * turn(mine, width) if take is None else weight
    once[...] = single[...] + scale * term


def columns(ref, toward, out):
    middle = ref.shape[1] // 2
    return jnp.where((toward == 3.0) == out, ref[:, middle:], ref[:, :middle])


def right_kernel(mine, part, out, half, across, pass_on):
    width = part.shape[0]
    toward = mine[pl.ds(mine.shape[0] - TAIL + 2, 1), pl.ds(0, 1)]
    half[...] = columns(part, toward, True) + out[pl.ds(0, width), :]
    across[pl.ds(0, width), :] = half[...]
    across[pl.ds(width, EXTRA), :] = jnp.zeros((EXTRA, half.shape[1]), F32)
    pass_on[...] = part[...]


def joined(toward, out, other):
    low = jnp.where(toward == 3.0, other, out)
    high = jnp.where(toward == 3.0, out, other)
    return jnp.concatenate([low, high], axis=1)


def whole_kernel(mine, part, half, rest, image, other):
    toward = mine[pl.ds(mine.shape[0] - TAIL + 2, 1), pl.ds(0, 1)]
    other[...] = columns(part, toward, False) + rest[pl.ds(0, part.shape[0]), :]
    image[...] = joined(toward, half[...], other[...])


def near_kernel(mine, field, image, once, mate, mate_out, mate_other, own, coup, pay, back, part, lift, state):
    b = field[...]
    toward = mine[pl.ds(mine.shape[0] - TAIL + 2, 1), pl.ds(0, 1)]
    mate_w = joined(toward, mate_out[...], mate_other[...])
    norm = col_sum(b, b)
    c = jnp.where(norm > 0.0, col_sum(b, image[...]) / jnp.where(norm > 0.0, norm, 1.0), 0.0)
    g = image[...] - c * b
    part[...] = dot(own[...], g) + dot(coup[...], mate_w - c * mate[...])
    lift[...] = back[...] - c * pay[pl.ds(0, b.shape[0]), :]
    rows = [(0, norm), (1, c), (2, col_sum(g, g)), (4, -col_sum(g, once[...])), (5, col_sum(b, once[...]))]
    state[...] = stack_rows(rows, state.shape)


def far_kernel(take, field, image, part, near, lift, coup, left, *refs):
    *sides, state = refs
    width = field.shape[0]
    b = field[...]
    c = near[1:2, :]
    acc = part[...] + 2.0 * dot(coup[...], left[...] + lift[...])
    if sides:
        mine, coup_gy, pay, side = sides
        if take is None:
            toward = mine[pl.ds(mine.shape[0] - TAIL + 2, 1), pl.ds(0, 1)]
            middle = b.shape[1] // 2
            shift = c * pay[pl.ds(0, width), :]
            term = dot(coup_gy[...], side[pl.ds(0, width), :] - jnp.where(toward == 3.0, shift[:, :middle], shift[:, middle:]))
            acc += 2.0 * turn(mine, width) * jnp.concatenate([term, term], axis=1)
        else:
            acc += 2.0 * dot(coup_gy[...], side[...] - c * pay[pl.ds(0, width), :])
    state[...] = near[...] + stack_rows([(3, col_sum(image[...] - c * b, acc)), (4, -col_sum(b, acc))], state.shape)


def merge_kernel(*refs):
    *states, out = refs
    norm = sum(s[0:1, :] for s in states)
    base = states[0][1:2, :]
    shift = sum(s[0:1, :] * (s[1:2, :] - base) for s in states)
    c = base + jnp.where(norm > 0.0, shift / jnp.where(norm > 0.0, norm, 1.0), 0.0)
    size, flat, slope, bend = (jnp.zeros_like(c) for _ in range(4))
    for s in states:
        d = c - s[1:2, :]
        size += s[2:3, :] + s[0:1, :] * d * d
        flat += s[3:4, :] + (s[4:5, :] + s[5:6, :] * d) * d
        slope += s[4:5, :] + 2.0 * s[5:6, :] * d
        bend += s[5:6, :]
    out[...] = stack_rows(list(enumerate([norm, c, size, flat, slope, bend])), out.shape)


def shards(right_side, node_diag, local_coup, block_cols, border_coup, border_send, border_rows):
    width, ncols = right_side.shape
    nblocks, _, bs, _ = local_coup.shape
    n_gx, n_gy, n_nd = (lax.axis_size(a) for a in AXES)
    assert n_nd == 2 and border_coup.shape[1] == 4 * SIDE
    swap = [(0, 1), (1, 0)]
    right = [(i, (i + 1) % n_gx) for i in range(n_gx)]
    left = [(j, i) for i, j in right]
    up = [(i, i + 1) for i in range(n_gy - 1)]
    down = [(j, i) for i, j in up]
    facing = jnp.where(lax.axis_index("gy") == 0, 3, 2).astype(jnp.int32)
    if n_gy == 2:
        sides = [(swap, None, 2.0)]
    elif n_gy > 2:
        sides = [(up, 2, 2.0), (down, 3, 0.0)]
    else:
        sides = []
    sends = [("gx", right)] + [("gy", perm) for perm, _, _ in sides]
    gives = [1] + [None if t is None else t ^ 1 for _, t, _ in sides]
    toward = jnp.full((1, 4 * SIDE), facing)
    marks = jnp.stack([facing, lax.axis_index("nd").astype(jnp.int32)])
    border = border_coup[0]

    def smem(n):
        return [pl.BlockSpec(memory_space=pltpu.SMEM)] * n

    full, half, longer = (width + bs + TAIL, ncols), (width, ncols // 2), (width + EXTRA, ncols // 2)

    def pack(gives):
        count = len(gives)
        tables = [marks] if gives != [1] else []
        return pl.pallas_call(
            partial(pack_kernel, gives),
            name="pack",
            in_specs=smem(len(tables)) + [pl.BlockSpec(memory_space=pl.ANY)] * 5,
            out_specs=[vmem()] * count,
            out_shape=[pltpu.VMEM(full, F32)] * count,
            scratch_shapes=[
                pltpu.SemaphoreType.DMA((count, SIDE + 1)),
                pltpu.VMEM((3, 1, 4 * SIDE), jnp.int32),
                pltpu.SemaphoreType.DMA((3,)),
            ],
            compiler_params=pltpu.CompilerParams(vmem_limit_bytes=LIMIT),
        )(*tables, *[pltpu.with_memory_space_constraint(a, pltpu.HBM) for a in (right_side, border, border_send, border_rows)], toward)

    packed = [*pack(gives[:1]), *(pack(gives[1:]) if sides else [])]
    pays = [lax.ppermute(pay, axis, perm) for pay, (axis, perm) in zip(packed, sends)]
    mine = packed[0]
    mate = lax.ppermute(right_side, "nd", swap)

    def tabled(kernel, name, tables, shapes, flops=None):
        def run(*args):
            args = list(args[:tables]) + [pltpu.with_memory_space_constraint(a, pltpu.VMEM) for a in args[tables:]]
            return pl.pallas_call(
                kernel,
                name=name,
                in_specs=smem(tables) + [vmem()] * (len(args) - tables),
                out_specs=[vmem()] * len(shapes),
                out_shape=[pltpu.VMEM(shape, F32) for shape in shapes],
                compiler_params=pltpu.CompilerParams(vmem_limit_bytes=LIMIT),
                cost_estimate=flops and pl.CostEstimate(flops=flops, bytes_accessed=1 << 20, transcendentals=0),
            )(*args)

        return run

    field, square = (width, ncols), (width, width)
    own, pair, *pieces = tabled(prep_kernel, "prep", 2, [square] * 2 + [(width, width // 2)] * 2, 1 << 24)(
        block_cols, marks, node_diag.reshape(1, width), local_coup, mine
    )
    mate_pair = [lax.ppermute(piece, "nd", swap) for piece in pieces]

    part, coup = call(base_kernel, "base", [field, square])(mine, own, pair, mate, *mate_pair)
    part, once, left_coup, back, *to_left = call(left_kernel, "left", [field, field, square, field] + [longer] * 2)(
        mine, part, border, pays[0]
    )
    from_right = [lax.ppermute(piece, "gx", left) for piece in to_left]
    side_coup = []
    for (_, take, weight), pay in zip(sides, pays[1:]):
        part, once, block = call(partial(gy_kernel, take, weight), "gy", [field, field, square])(mine, part, once, border, pay)
        side_coup.append(block)
    half_w, across, pass_on = call(right_kernel, "right", [half, longer, field])(mine, part, from_right[0])
    left_w = lax.ppermute(pass_on, "gx", right)
    image, other_w = call(whole_kernel, "whole", [field, half])(mine, part, half_w, from_right[1])
    mate_w = [lax.ppermute(w, "nd", swap) for w in (half_w, other_w)]
    part, lift, state = call(near_kernel, "near", [field, field, (TAIL, ncols)])(
        mine, right_side, image, once, mate, *mate_w, own, coup, pays[0], back
    )
    far = []
    take = None
    if sides:
        perm, take, _ = sides[0]
        far = [mine, side_coup[0], pays[1], lax.ppermute(across if take is None else image, "gy", perm)]
    (state,) = call(partial(far_kernel, take), "far", [(TAIL, ncols)])(
        right_side, image, part, state, lift, left_coup, left_w, *far
    )
    state = join(state)
    norm, c, size, form = (row[None] for row in state[:4])
    ratio = size / (c * c * norm)
    last = size / (form - ratio * ratio * c * c * c * norm)
    return ((1.0 + last * c * (1.0 + ratio)) / c) * right_side - (last / c) * image


def solution(mesh):
    blocks = P(("var", "gx", "gy", "nd"))
    tables = P(AXES)
    in_specs = (blocks, blocks, blocks, tables, blocks, tables, tables)
    return jax.shard_map(shards, mesh=mesh, in_specs=in_specs, out_specs=blocks, check_vma=False)
```

```python
from functools import partial

import jax
import jax.numpy as jnp
from jax import lax
from jax.experimental import pallas as pl
from jax.experimental.pallas import tpu as pltpu
from jax.sharding import PartitionSpec as P

F32 = jnp.float32
BF16 = jnp.bfloat16
AXES = ("gx", "gy", "nd")
SIDE = 2
LIMIT = 8 << 20
EXTRA = 8
TAIL = 8


def vmem():
    return pl.BlockSpec(memory_space=pltpu.VMEM)


def call(kernel, name, shapes, scratch=(), flops=None):
    def run(*args):
        args = [pltpu.with_memory_space_constraint(a, pltpu.VMEM) for a in args]
        return pl.pallas_call(
            kernel,
            name=name,
            in_specs=[vmem()] * len(args),
            out_specs=[vmem()] * len(shapes),
            out_shape=[pltpu.VMEM(shape, F32) for shape in shapes],
            scratch_shapes=scratch,
            compiler_params=pltpu.CompilerParams(vmem_limit_bytes=LIMIT),
            cost_estimate=flops and pl.CostEstimate(flops=flops, bytes_accessed=1 << 20, transcendentals=0),
        )(*args)

    return run


def join(state):
    count = lax.axis_size(AXES)
    assert count & (count - 1) == 0
    step = 1
    while step < count:
        masks = [m * step for m in (1, 2, 3) if m * step < count]
        others = [lax.ppermute(state, AXES, [(i, i ^ m) for i in range(count)]) for m in masks]
        (state,) = call(merge_kernel, "merge", [state.shape])(state, *others)
        step *= 4
    return state


def split(a):
    high = a.astype(BF16)
    return high, (a - high.astype(F32)).astype(BF16)


def dot(a, b):
    (ah, al), (bh, bl) = split(a), split(b)
    mul = partial(jnp.dot, preferred_element_type=F32)
    return mul(ah, bh) + (mul(ah, bl) + mul(al, bh))


def col_sum(a, b):
    return jnp.sum(a * b, axis=0, keepdims=True)


def stack_rows(rows, shape):
    line = lax.broadcasted_iota(jnp.int32, shape, 0)
    return sum(jnp.where(line == n, row, 0.0) for n, row in rows)


def pack_kernel(gives, *refs):
    marks, refs = (refs[0], refs[1:]) if gives != [1] else (None, refs)
    field, border, send, rows, toward, *pays, sems, table, table_sems = refs
    width = field.shape[0]
    bs = border.shape[1]
    tables = [pltpu.make_async_copy(ref, table.at[n], table_sems.at[n]) for n, ref in enumerate((rows, send, toward))]
    copies = []
    for n, (give, pay) in enumerate(zip(gives, pays)):
        give = marks[0] if give is None else give
        copies.append(pltpu.make_async_copy(field, pay.at[pl.ds(0, width), :], sems.at[n, SIDE]))
        for s in range(SIDE):
            block = pay.at[pl.ds(width, bs), pl.ds(s * bs, bs)]
            copies.append(pltpu.make_async_copy(border.at[give * SIDE + s], block, sems.at[n, s]))
    for copy in tables + copies:
        copy.start()
    for copy in tables:
        copy.wait()
    count = table.shape[2]
    for pay in pays:
        for n in range(3):
            pay[pl.ds(pay.shape[0] - TAIL + n, 1), pl.ds(0, count)] = table[n].astype(F32)
    for copy in copies:
        copy.wait()


def prep_kernel(cols, marks, diag, local, packed, own, pair, low, high):
    nblocks, nonzeros, bs, _ = local.shape
    width = nblocks * bs
    patch_len = 2 * nblocks
    base = marks[1] * nblocks
    own[...] = jnp.zeros((width, width), F32)
    pair[...] = jnp.zeros((width, width), F32)
    for b in range(nblocks):
        for k in range(nonzeros):
            spot = lax.rem(cols[b, k] - base + patch_len, patch_len)
            block = local[b, k]
            for c in range(nblocks):

                @pl.when(spot == c)
                def _():
                    own[pl.ds(b * bs, bs), pl.ds(c * bs, bs)] += block

                @pl.when(spot == c + nblocks)
                def _():
                    pair[pl.ds(b * bs, bs), pl.ds(c * bs, bs)] += block

    lower = own[...]
    here = lax.broadcasted_iota(jnp.int32, (width, width), 0)
    there = lax.broadcasted_iota(jnp.int32, (width, width), 1)
    own[...] = lower + lower.T + jnp.where(here == there, diag[...], 0.0)
    low[...] = pair[:, : width // 2]
    high[...] = pair[:, width // 2 :]


def edge(take, width, mine, pay, border):
    bs = border.shape[1]
    known = isinstance(take, int)

    def pick(of):
        return of(take) if known else jnp.where(take == 2.0, of(2), of(3))

    def number(ref, line, t):
        return ref[pl.ds(ref.shape[0] - TAIL + line, 1), pl.ds(t * SIDE + s, 1)]

    blocks = [[0.0] * (width // bs) for _ in range(width // bs)]
    for s in range(SIDE):
        beside = pay.shape[1] > bs
        turned = (pay[pl.ds(width, bs), pl.ds(s * bs, bs)] if beside else pay[pl.ds(width + s * bs, bs), :]).T
        pairs = [
            (pick(lambda t: border[t * SIDE + s]), pick(lambda t: number(mine, 0, t)), pick(lambda t: number(pay, 1, t))),
            (turned, pick(lambda t: number(mine, 1, t ^ 1)), pick(lambda t: number(pay, 0, t ^ 1))),
        ]
        for block, to, at in pairs:
            for i, line in enumerate(blocks):
                for j in range(len(line)):
                    line[j] = line[j] + jnp.where((to == i) & (at == j), block, 0.0)
    return jnp.concatenate([jnp.concatenate(line, axis=1) for line in blocks], axis=0)


def base_kernel(mine, own, pair, mate, low, high, image, coup):
    width = mate.shape[0]
    coup[...] = pair[...] + jnp.concatenate([low[...].T, high[...].T], axis=0)
    image[...] = dot(own[...], mine[pl.ds(0, width), :]) + dot(coup[...], mate[...])


def left_kernel(mine, part, border, pay, image, once, coup, back, out, other):
    width = part.shape[0]
    toward = mine[pl.ds(mine.shape[0] - TAIL + 2, 1), pl.ds(0, 1)]
    coup[...] = edge(0, width, mine, pay, border)
    back[...] = dot(coup[...].T, mine[pl.ds(0, width), :])
    out[pl.ds(0, width), :] = columns(back, toward, True)
    other[pl.ds(0, width), :] = columns(back, toward, False)
    term = dot(coup[...], pay[pl.ds(0, width), :])
    image[...] = part[...] + term
    once[...] = part[...] + 2.0 * term


def turn(mine, width):
    toward = mine[pl.ds(mine.shape[0] - TAIL + 2, 1), pl.ds(0, 1)]
    count = mine.shape[1]
    first = jnp.where(lax.broadcasted_iota(jnp.int32, (1, count), 1) < count // 2, 1.0, 0.0)
    return jnp.where(toward == 3.0, first, 1.0 - first)


def gy_kernel(take, weight, mine, part, single, border, pay, image, once, coup):
    width = coup.shape[0]
    toward = mine[pl.ds(mine.shape[0] - TAIL + 2, 1), pl.ds(0, 1)]
    coup[...] = edge(toward if take is None else take, width, mine, pay, border)
    term = dot(coup[...], pay[pl.ds(0, width), :])
    image[...] = part[...] + term
    scale = weight * turn(mine, width) if take is None else weight
    once[...] = single[...] + scale * term


def columns(ref, toward, out):
    middle = ref.shape[1] // 2
    return jnp.where((toward == 3.0) == out, ref[:, middle:], ref[:, :middle])


def right_kernel(mine, part, out, half, across):
    width = part.shape[0]
    toward = mine[pl.ds(mine.shape[0] - TAIL + 2, 1), pl.ds(0, 1)]
    half[...] = columns(part, toward, True) + out[pl.ds(0, width), :]
    across[pl.ds(0, width), :] = half[...]
    across[pl.ds(width, EXTRA), :] = jnp.zeros((EXTRA, half.shape[1]), F32)


def joined(toward, out, other):
    low = jnp.where(toward == 3.0, other, out)
    high = jnp.where(toward == 3.0, out, other)
    return jnp.concatenate([low, high], axis=1)


def whole_kernel(mine, part, half, rest, image, other):
    toward = mine[pl.ds(mine.shape[0] - TAIL + 2, 1), pl.ds(0, 1)]
    other[...] = columns(part, toward, False) + rest[pl.ds(0, part.shape[0]), :]
    image[...] = joined(toward, half[...], other[...])


def near_kernel(mine, field, image, once, mate, mate_out, mate_other, own, coup, pay, back, part, lift, state):
    b = field[...]
    toward = mine[pl.ds(mine.shape[0] - TAIL + 2, 1), pl.ds(0, 1)]
    mate_w = joined(toward, mate_out[...], mate_other[...])
    norm = col_sum(b, b)
    c = jnp.where(norm > 0.0, col_sum(b, image[...]) / jnp.where(norm > 0.0, norm, 1.0), 0.0)
    g = image[...] - c * b
    part[...] = dot(own[...], g) + dot(coup[...], mate_w - c * mate[...])
    lift[...] = back[...] - c * pay[pl.ds(0, b.shape[0]), :]
    rows = [(0, norm), (1, c), (2, col_sum(g, g)), (4, -col_sum(g, once[...])), (5, col_sum(b, once[...]))]
    state[...] = stack_rows(rows, state.shape)


def far_kernel(take, field, image, part, near, lift, coup, left, *refs):
    *sides, state = refs
    width = field.shape[0]
    b = field[...]
    c = near[1:2, :]
    acc = part[...] + 2.0 * dot(coup[...], left[...] + lift[...])
    if sides:
        mine, coup_gy, pay, side = sides
        if take is None:
            toward = mine[pl.ds(mine.shape[0] - TAIL + 2, 1), pl.ds(0, 1)]
            middle = b.shape[1] // 2
            shift = c * pay[pl.ds(0, width), :]
            term = dot(coup_gy[...], side[pl.ds(0, width), :] - jnp.where(toward == 3.0, shift[:, :middle], shift[:, middle:]))
            acc += 2.0 * turn(mine, width) * jnp.concatenate([term, term], axis=1)
        else:
            acc += 2.0 * dot(coup_gy[...], side[...] - c * pay[pl.ds(0, width), :])
    state[...] = near[...] + stack_rows([(3, col_sum(image[...] - c * b, acc)), (4, -col_sum(b, acc))], state.shape)


def merge_kernel(*refs):
    *states, out = refs
    norm = sum(s[0:1, :] for s in states)
    base = states[0][1:2, :]
    shift = sum(s[0:1, :] * (s[1:2, :] - base) for s in states)
    c = base + jnp.where(norm > 0.0, shift / jnp.where(norm > 0.0, norm, 1.0), 0.0)
    size, flat, slope, bend = (jnp.zeros_like(c) for _ in range(4))
    for s in states:
        d = c - s[1:2, :]
        size += s[2:3, :] + s[0:1, :] * d * d
        flat += s[3:4, :] + (s[4:5, :] + s[5:6, :] * d) * d
        slope += s[4:5, :] + 2.0 * s[5:6, :] * d
        bend += s[5:6, :]
    out[...] = stack_rows(list(enumerate([norm, c, size, flat, slope, bend])), out.shape)


def shards(right_side, node_diag, local_coup, block_cols, border_coup, border_send, border_rows):
    width, ncols = right_side.shape
    nblocks, _, bs, _ = local_coup.shape
    n_gx, n_gy, n_nd = (lax.axis_size(a) for a in AXES)
    assert n_nd == 2 and border_coup.shape[1] == 4 * SIDE
    swap = [(0, 1), (1, 0)]
    right = [(i, (i + 1) % n_gx) for i in range(n_gx)]
    left = [(j, i) for i, j in right]
    up = [(i, i + 1) for i in range(n_gy - 1)]
    down = [(j, i) for i, j in up]
    facing = jnp.where(lax.axis_index("gy") == 0, 3, 2).astype(jnp.int32)
    if n_gy == 2:
        sides = [(swap, None, 2.0)]
    elif n_gy > 2:
        sides = [(up, 2, 2.0), (down, 3, 0.0)]
    else:
        sides = []
    sends = [("gx", right)] + [("gy", perm) for perm, _, _ in sides]
    gives = [1] + [None if t is None else t ^ 1 for _, t, _ in sides]
    toward = jnp.full((1, 4 * SIDE), facing)
    marks = jnp.stack([facing, lax.axis_index("nd").astype(jnp.int32)])
    border = border_coup[0]

    def smem(n):
        return [pl.BlockSpec(memory_space=pltpu.SMEM)] * n

    full, half, longer = (width + bs + TAIL, ncols), (width, ncols // 2), (width + EXTRA, ncols // 2)

    def pack(gives):
        count = len(gives)
        tables = [marks] if gives != [1] else []
        return pl.pallas_call(
            partial(pack_kernel, gives),
            name="pack",
            in_specs=smem(len(tables)) + [pl.BlockSpec(memory_space=pl.ANY)] * 5,
            out_specs=[vmem()] * count,
            out_shape=[pltpu.VMEM(full, F32)] * count,
            scratch_shapes=[
                pltpu.SemaphoreType.DMA((count, SIDE + 1)),
                pltpu.VMEM((3, 1, 4 * SIDE), jnp.int32),
                pltpu.SemaphoreType.DMA((3,)),
            ],
            compiler_params=pltpu.CompilerParams(vmem_limit_bytes=LIMIT),
        )(*tables, *[pltpu.with_memory_space_constraint(a, pltpu.HBM) for a in (right_side, border, border_send, border_rows)], toward)

    packed = [*pack(gives[:1]), *(pack(gives[1:]) if sides else [])]
    pays = [lax.ppermute(pay, axis, perm) for pay, (axis, perm) in zip(packed, sends)]
    mine = packed[0]
    mate = lax.ppermute(right_side, "nd", swap)

    def tabled(kernel, name, tables, shapes, flops=None):
        def run(*args):
            args = list(args[:tables]) + [pltpu.with_memory_space_constraint(a, pltpu.VMEM) for a in args[tables:]]
            return pl.pallas_call(
                kernel,
                name=name,
                in_specs=smem(tables) + [vmem()] * (len(args) - tables),
                out_specs=[vmem()] * len(shapes),
                out_shape=[pltpu.VMEM(shape, F32) for shape in shapes],
                compiler_params=pltpu.CompilerParams(vmem_limit_bytes=LIMIT),
                cost_estimate=flops and pl.CostEstimate(flops=flops, bytes_accessed=1 << 20, transcendentals=0),
            )(*args)

        return run

    field, square = (width, ncols), (width, width)
    own, pair, *pieces = tabled(prep_kernel, "prep", 2, [square] * 2 + [(width, width // 2)] * 2, 1 << 24)(
        block_cols, marks, node_diag.reshape(1, width), local_coup, mine
    )
    mate_pair = [lax.ppermute(piece, "nd", swap) for piece in pieces]

    part, coup = call(base_kernel, "base", [field, square])(mine, own, pair, mate, *mate_pair)
    part, once, left_coup, back, *to_left = call(left_kernel, "left", [field, field, square, field] + [longer] * 2)(
        mine, part, border, pays[0]
    )
    from_right = [lax.ppermute(piece, "gx", left) for piece in to_left]
    side_coup = []
    for (_, take, weight), pay in zip(sides, pays[1:]):
        part, once, block = call(partial(gy_kernel, take, weight), "gy", [field, field, square])(mine, part, once, border, pay)
        side_coup.append(block)
    left_w = lax.ppermute(part, "gx", right)
    half_w, across = call(right_kernel, "right", [half, longer])(mine, part, from_right[0])
    image, other_w = call(whole_kernel, "whole", [field, half])(mine, part, half_w, from_right[1])
    mate_w = [lax.ppermute(w, "nd", swap) for w in (half_w, other_w)]
    part, lift, state = call(near_kernel, "near", [field, field, (TAIL, ncols)])(
        mine, right_side, image, once, mate, *mate_w, own, coup, pays[0], back
    )
    far = []
    take = None
    if sides:
        perm, take, _ = sides[0]
        far = [mine, side_coup[0], pays[1], lax.ppermute(across if take is None else image, "gy", perm)]
    (state,) = call(partial(far_kernel, take), "far", [(TAIL, ncols)])(
        right_side, image, part, state, lift, left_coup, left_w, *far
    )
    state = join(state)
    norm, c, size, form = (row[None] for row in state[:4])
    ratio = size / (c * c * norm)
    last = size / (form - ratio * ratio * c * c * c * norm)
    return ((1.0 + last * c * (1.0 + ratio)) / c) * right_side - (last / c) * image


def solution(mesh):
    blocks = P(("var", "gx", "gy", "nd"))
    tables = P(AXES)
    in_specs = (blocks, blocks, blocks, tables, blocks, tables, tables)
    return jax.shard_map(shards, mesh=mesh, in_specs=in_specs, out_specs=blocks, check_vma=False)
```

```python
from functools import partial

import jax
import jax.numpy as jnp
from jax import lax
from jax.experimental import pallas as pl
from jax.experimental.pallas import tpu as pltpu
from jax.sharding import PartitionSpec as P

F32 = jnp.float32
BF16 = jnp.bfloat16
AXES = ("gx", "gy", "nd")
SIDE = 2
LIMIT = 8 << 20
EXTRA = 8
TAIL = 8


def vmem():
    return pl.BlockSpec(memory_space=pltpu.VMEM)


def call(kernel, name, shapes, scratch=(), flops=None):
    def run(*args):
        args = [pltpu.with_memory_space_constraint(a, pltpu.VMEM) for a in args]
        return pl.pallas_call(
            kernel,
            name=name,
            in_specs=[vmem()] * len(args),
            out_specs=[vmem()] * len(shapes),
            out_shape=[pltpu.VMEM(shape, F32) for shape in shapes],
            scratch_shapes=scratch,
            compiler_params=pltpu.CompilerParams(vmem_limit_bytes=LIMIT),
            cost_estimate=flops and pl.CostEstimate(flops=flops, bytes_accessed=1 << 20, transcendentals=0),
        )(*args)

    return run


def join(state):
    count = lax.axis_size(AXES)
    assert count & (count - 1) == 0
    step = 1
    while step < count:
        masks = [m * step for m in (1, 2, 3) if m * step < count]
        others = [lax.ppermute(state, AXES, [(i, i ^ m) for i in range(count)]) for m in masks]
        (state,) = call(merge_kernel, "merge", [state.shape])(state, *others)
        step *= 4
    return state


def split(a):
    high = a.astype(BF16)
    return high, (a - high.astype(F32)).astype(BF16)


def dot(a, b):
    (ah, al), (bh, bl) = split(a), split(b)
    mul = partial(jnp.dot, preferred_element_type=F32)
    return mul(ah, bh) + (mul(ah, bl) + mul(al, bh))


def col_sum(a, b):
    return jnp.sum(a * b, axis=0, keepdims=True)


def stack_rows(rows, shape):
    line = lax.broadcasted_iota(jnp.int32, shape, 0)
    return sum(jnp.where(line == n, row, 0.0) for n, row in rows)


def pack_kernel(gives, *refs):
    marks, refs = (refs[0], refs[1:]) if gives != [1] else (None, refs)
    border, send, rows, toward, *pays, sems, table, table_sems = refs
    bs = border.shape[1]
    tables = [pltpu.make_async_copy(ref, table.at[n], table_sems.at[n]) for n, ref in enumerate((rows, send, toward))]
    copies = []
    for n, (give, pay) in enumerate(zip(gives, pays)):
        give = marks[0] if give is None else give
        for s in range(SIDE):
            block = pay.at[pl.ds(0, bs), pl.ds(s * bs, bs)]
            copies.append(pltpu.make_async_copy(border.at[give * SIDE + s], block, sems.at[n, s]))
    for copy in tables + copies:
        copy.start()
    for copy in tables:
        copy.wait()
    count = table.shape[2]
    for pay in pays:
        for n in range(3):
            pay[pl.ds(bs + n, 1), pl.ds(0, count)] = table[n].astype(F32)
    for copy in copies:
        copy.wait()


def prep_kernel(cols, marks, diag, local, packed, own, pair, low, high):
    nblocks, nonzeros, bs, _ = local.shape
    width = nblocks * bs
    patch_len = 2 * nblocks
    base = marks[1] * nblocks
    own[...] = jnp.zeros((width, width), F32)
    pair[...] = jnp.zeros((width, width), F32)
    for b in range(nblocks):
        for k in range(nonzeros):
            spot = lax.rem(cols[b, k] - base + patch_len, patch_len)
            block = local[b, k]
            for c in range(nblocks):

                @pl.when(spot == c)
                def _():
                    own[pl.ds(b * bs, bs), pl.ds(c * bs, bs)] += block

                @pl.when(spot == c + nblocks)
                def _():
                    pair[pl.ds(b * bs, bs), pl.ds(c * bs, bs)] += block

    lower = own[...]
    here = lax.broadcasted_iota(jnp.int32, (width, width), 0)
    there = lax.broadcasted_iota(jnp.int32, (width, width), 1)
    own[...] = lower + lower.T + jnp.where(here == there, diag[...], 0.0)
    low[...] = pair[:, : width // 2]
    high[...] = pair[:, width // 2 :]


def edge(take, width, mine, pay, border):
    bs = border.shape[1]
    known = isinstance(take, int)

    def pick(of):
        return of(take) if known else jnp.where(take == 2.0, of(2), of(3))

    def number(ref, line, t):
        return ref[pl.ds(ref.shape[0] - TAIL + line, 1), pl.ds(t * SIDE + s, 1)]

    blocks = [[0.0] * (width // bs) for _ in range(width // bs)]
    for s in range(SIDE):
        turned = pay[pl.ds(0, bs), pl.ds(s * bs, bs)].T
        pairs = [
            (pick(lambda t: border[t * SIDE + s]), pick(lambda t: number(mine, 0, t)), pick(lambda t: number(pay, 1, t))),
            (turned, pick(lambda t: number(mine, 1, t ^ 1)), pick(lambda t: number(pay, 0, t ^ 1))),
        ]
        for block, to, at in pairs:
            for i, line in enumerate(blocks):
                for j in range(len(line)):
                    line[j] = line[j] + jnp.where((to == i) & (at == j), block, 0.0)
    return jnp.concatenate([jnp.concatenate(line, axis=1) for line in blocks], axis=0)


def base_kernel(field, own, pair, mate, low, high, image, coup):
    coup[...] = pair[...] + jnp.concatenate([low[...].T, high[...].T], axis=0)
    image[...] = dot(own[...], field[...]) + dot(coup[...], mate[...])


def back_kernel(mine, field, border, pay, coup, back, out, other):
    width = field.shape[0]
    toward = mine[pl.ds(mine.shape[0] - TAIL + 2, 1), pl.ds(0, 1)]
    coup[...] = edge(0, width, mine, pay, border)
    back[...] = dot(coup[...].T, field[...])
    out[pl.ds(0, width), :] = columns(back, toward, True)
    other[pl.ds(0, width), :] = columns(back, toward, False)


def left_kernel(part, coup, there, image, once):
    term = dot(coup[...], there[...])
    image[...] = part[...] + term
    once[...] = part[...] + 2.0 * term


def turn(mine, width):
    toward = mine[pl.ds(mine.shape[0] - TAIL + 2, 1), pl.ds(0, 1)]
    count = mine.shape[1]
    first = jnp.where(lax.broadcasted_iota(jnp.int32, (1, count), 1) < count // 2, 1.0, 0.0)
    return jnp.where(toward == 3.0, first, 1.0 - first)


def gy_kernel(take, weight, mine, part, single, border, pay, there, image, once, coup):
    width = coup.shape[0]
    toward = mine[pl.ds(mine.shape[0] - TAIL + 2, 1), pl.ds(0, 1)]
    coup[...] = edge(toward if take is None else take, width, mine, pay, border)
    term = dot(coup[...], there[...])
    image[...] = part[...] + term
    scale = weight * turn(mine, width) if take is None else weight
    once[...] = single[...] + scale * term


def columns(ref, toward, out):
    middle = ref.shape[1] // 2
    return jnp.where((toward == 3.0) == out, ref[:, middle:], ref[:, :middle])


def right_kernel(mine, part, out, half, across):
    width = part.shape[0]
    toward = mine[pl.ds(mine.shape[0] - TAIL + 2, 1), pl.ds(0, 1)]
    half[...] = columns(part, toward, True) + out[pl.ds(0, width), :]
    across[pl.ds(0, width), :] = half[...]
    across[pl.ds(width, EXTRA), :] = jnp.zeros((EXTRA, half.shape[1]), F32)


def joined(toward, out, other):
    low = jnp.where(toward == 3.0, other, out)
    high = jnp.where(toward == 3.0, out, other)
    return jnp.concatenate([low, high], axis=1)


def whole_kernel(mine, part, half, rest, image, other):
    toward = mine[pl.ds(mine.shape[0] - TAIL + 2, 1), pl.ds(0, 1)]
    other[...] = columns(part, toward, False) + rest[pl.ds(0, part.shape[0]), :]
    image[...] = joined(toward, half[...], other[...])


def near_kernel(mine, field, image, once, mate, mate_out, mate_other, own, coup, there, back, part, lift, state):
    b = field[...]
    toward = mine[pl.ds(mine.shape[0] - TAIL + 2, 1), pl.ds(0, 1)]
    mate_w = joined(toward, mate_out[...], mate_other[...])
    norm = col_sum(b, b)
    c = jnp.where(norm > 0.0, col_sum(b, image[...]) / jnp.where(norm > 0.0, norm, 1.0), 0.0)
    g = image[...] - c * b
    part[...] = dot(own[...], g) + dot(coup[...], mate_w - c * mate[...])
    lift[...] = back[...] - c * there[...]
    rows = [(0, norm), (1, c), (2, col_sum(g, g)), (4, -col_sum(g, once[...])), (5, col_sum(b, once[...]))]
    state[...] = stack_rows(rows, state.shape)


def far_kernel(take, field, image, part, near, lift, coup, left, *refs):
    *sides, state = refs
    width = field.shape[0]
    b = field[...]
    c = near[1:2, :]
    acc = part[...] + 2.0 * dot(coup[...], left[...] + lift[...])
    if sides:
        mine, coup_gy, there, side = sides
        if take is None:
            toward = mine[pl.ds(mine.shape[0] - TAIL + 2, 1), pl.ds(0, 1)]
            middle = b.shape[1] // 2
            shift = c * there[...]
            term = dot(coup_gy[...], side[pl.ds(0, width), :] - jnp.where(toward == 3.0, shift[:, :middle], shift[:, middle:]))
            acc += 2.0 * turn(mine, width) * jnp.concatenate([term, term], axis=1)
        else:
            acc += 2.0 * dot(coup_gy[...], side[...] - c * there[...])
    state[...] = near[...] + stack_rows([(3, col_sum(image[...] - c * b, acc)), (4, -col_sum(b, acc))], state.shape)


def merge_kernel(*refs):
    *states, out = refs
    norm = sum(s[0:1, :] for s in states)
    base = states[0][1:2, :]
    shift = sum(s[0:1, :] * (s[1:2, :] - base) for s in states)
    c = base + jnp.where(norm > 0.0, shift / jnp.where(norm > 0.0, norm, 1.0), 0.0)
    size, flat, slope, bend = (jnp.zeros_like(c) for _ in range(4))
    for s in states:
        d = c - s[1:2, :]
        size += s[2:3, :] + s[0:1, :] * d * d
        flat += s[3:4, :] + (s[4:5, :] + s[5:6, :] * d) * d
        slope += s[4:5, :] + 2.0 * s[5:6, :] * d
        bend += s[5:6, :]
    out[...] = stack_rows(list(enumerate([norm, c, size, flat, slope, bend])), out.shape)


def shards(right_side, node_diag, local_coup, block_cols, border_coup, border_send, border_rows):
    width, ncols = right_side.shape
    nblocks, _, bs, _ = local_coup.shape
    n_gx, n_gy, n_nd = (lax.axis_size(a) for a in AXES)
    assert n_nd == 2 and border_coup.shape[1] == 4 * SIDE
    swap = [(0, 1), (1, 0)]
    right = [(i, (i + 1) % n_gx) for i in range(n_gx)]
    left = [(j, i) for i, j in right]
    up = [(i, i + 1) for i in range(n_gy - 1)]
    down = [(j, i) for i, j in up]
    facing = jnp.where(lax.axis_index("gy") == 0, 3, 2).astype(jnp.int32)
    if n_gy == 2:
        sides = [(swap, None, 2.0)]
    elif n_gy > 2:
        sides = [(up, 2, 2.0), (down, 3, 0.0)]
    else:
        sides = []
    sends = [("gx", right)] + [("gy", perm) for perm, _, _ in sides]
    gives = [1] + [None if t is None else t ^ 1 for _, t, _ in sides]
    toward = jnp.full((1, 4 * SIDE), facing)
    marks = jnp.stack([facing, lax.axis_index("nd").astype(jnp.int32)])
    border = border_coup[0]

    def smem(n):
        return [pl.BlockSpec(memory_space=pltpu.SMEM)] * n

    full, half, longer = (bs + TAIL, ncols), (width, ncols // 2), (width + EXTRA, ncols // 2)

    def pack(gives):
        count = len(gives)
        tables = [marks] if gives != [1] else []
        return pl.pallas_call(
            partial(pack_kernel, gives),
            name="pack",
            in_specs=smem(len(tables)) + [pl.BlockSpec(memory_space=pl.ANY)] * 4,
            out_specs=[vmem()] * count,
            out_shape=[pltpu.VMEM(full, F32)] * count,
            scratch_shapes=[
                pltpu.SemaphoreType.DMA((count, SIDE)),
                pltpu.VMEM((3, 1, 4 * SIDE), jnp.int32),
                pltpu.SemaphoreType.DMA((3,)),
            ],
            compiler_params=pltpu.CompilerParams(vmem_limit_bytes=LIMIT),
        )(*tables, *[pltpu.with_memory_space_constraint(a, pltpu.HBM) for a in (border, border_send, border_rows)], toward)

    packed = [*pack(gives[:1]), *(pack(gives[1:]) if sides else [])]
    pays = [lax.ppermute(pay, axis, perm) for pay, (axis, perm) in zip(packed, sends)]
    mine = packed[0]
    fields = [lax.ppermute(right_side, axis, perm) for axis, perm in sends]
    mate = lax.ppermute(right_side, "nd", swap)

    def tabled(kernel, name, tables, shapes, flops=None):
        def run(*args):
            args = list(args[:tables]) + [pltpu.with_memory_space_constraint(a, pltpu.VMEM) for a in args[tables:]]
            return pl.pallas_call(
                kernel,
                name=name,
                in_specs=smem(tables) + [vmem()] * (len(args) - tables),
                out_specs=[vmem()] * len(shapes),
                out_shape=[pltpu.VMEM(shape, F32) for shape in shapes],
                compiler_params=pltpu.CompilerParams(vmem_limit_bytes=LIMIT),
                cost_estimate=flops and pl.CostEstimate(flops=flops, bytes_accessed=1 << 20, transcendentals=0),
            )(*args)

        return run

    field, square = (width, ncols), (width, width)
    own, pair, *pieces = tabled(prep_kernel, "prep", 2, [square] * 2 + [(width, width // 2)] * 2, 1 << 24)(
        block_cols, marks, node_diag.reshape(1, width), local_coup, mine
    )
    mate_pair = [lax.ppermute(piece, "nd", swap) for piece in pieces]

    part, coup = call(base_kernel, "base", [field, square])(right_side, own, pair, mate, *mate_pair)
    left_coup, back, *to_left = call(back_kernel, "back", [square, field] + [longer] * 2)(mine, right_side, border, pays[0])
    from_right = [lax.ppermute(piece, "gx", left) for piece in to_left]
    part, once = call(left_kernel, "left", [field] * 2)(part, left_coup, fields[0])
    side_coup = []
    for (_, take, weight), pay, there in zip(sides, pays[1:], fields[1:]):
        part, once, block = call(partial(gy_kernel, take, weight), "gy", [field, field, square])(mine, part, once, border, pay, there)
        side_coup.append(block)
    left_w = lax.ppermute(part, "gx", right)
    half_w, across = call(right_kernel, "right", [half, longer])(mine, part, from_right[0])
    image, other_w = call(whole_kernel, "whole", [field, half])(mine, part, half_w, from_right[1])
    mate_w = [lax.ppermute(w, "nd", swap) for w in (half_w, other_w)]
    part, lift, state = call(near_kernel, "near", [field, field, (TAIL, ncols)])(
        mine, right_side, image, once, mate, *mate_w, own, coup, fields[0], back
    )
    far = []
    take = None
    if sides:
        perm, take, _ = sides[0]
        far = [mine, side_coup[0], fields[1], lax.ppermute(across if take is None else image, "gy", perm)]
    (state,) = call(partial(far_kernel, take), "far", [(TAIL, ncols)])(
        right_side, image, part, state, lift, left_coup, left_w, *far
    )
    state = join(state)
    norm, c, size, form = (row[None] for row in state[:4])
    ratio = size / (c * c * norm)
    last = size / (form - ratio * ratio * c * c * c * norm)
    return ((1.0 + last * c * (1.0 + ratio)) / c) * right_side - (last / c) * image


def solution(mesh):
    blocks = P(("var", "gx", "gy", "nd"))
    tables = P(AXES)
    in_specs = (blocks, blocks, blocks, tables, blocks, tables, tables)
    return jax.shard_map(shards, mesh=mesh, in_specs=in_specs, out_specs=blocks, check_vma=False)
```

```python
from functools import partial

import jax
import jax.numpy as jnp
from jax import lax
from jax.experimental import pallas as pl
from jax.experimental.pallas import tpu as pltpu
from jax.sharding import PartitionSpec as P

F32 = jnp.float32
BF16 = jnp.bfloat16
AXES = ("gx", "gy", "nd")
SIDE = 2
LIMIT = 8 << 20
EXTRA = 8
TAIL = 8


def vmem():
    return pl.BlockSpec(memory_space=pltpu.VMEM)


def call(kernel, name, shapes, scratch=(), flops=None):
    def run(*args):
        args = [pltpu.with_memory_space_constraint(a, pltpu.VMEM) for a in args]
        return pl.pallas_call(
            kernel,
            name=name,
            in_specs=[vmem()] * len(args),
            out_specs=[vmem()] * len(shapes),
            out_shape=[pltpu.VMEM(shape, F32) for shape in shapes],
            scratch_shapes=scratch,
            compiler_params=pltpu.CompilerParams(vmem_limit_bytes=LIMIT),
            cost_estimate=flops and pl.CostEstimate(flops=flops, bytes_accessed=1 << 20, transcendentals=0),
        )(*args)

    return run


def join(state):
    count = lax.axis_size(AXES)
    assert count & (count - 1) == 0
    step = 1
    while step < count:
        masks = [m * step for m in (1, 2, 3) if m * step < count]
        others = [lax.ppermute(state, AXES, [(i, i ^ m) for i in range(count)]) for m in masks]
        (state,) = call(merge_kernel, "merge", [state.shape])(state, *others)
        step *= 4
    return state


def split(a):
    high = a.astype(BF16)
    return high, (a - high.astype(F32)).astype(BF16)


def dot(a, b):
    (ah, al), (bh, bl) = split(a), split(b)
    mul = partial(jnp.dot, preferred_element_type=F32)
    return mul(ah, bh) + (mul(ah, bl) + mul(al, bh))


def col_sum(a, b):
    return jnp.sum(a * b, axis=0, keepdims=True)


def stack_rows(rows, shape):
    line = lax.broadcasted_iota(jnp.int32, shape, 0)
    return sum(jnp.where(line == n, row, 0.0) for n, row in rows)


def pack_kernel(gives, *refs):
    marks, refs = (refs[0], refs[1:]) if gives != [1] else (None, refs)
    border, send, rows, toward, *pays, sems, table, table_sems = refs
    bs = border.shape[1]
    tables = [pltpu.make_async_copy(ref, table.at[n], table_sems.at[n]) for n, ref in enumerate((rows, send, toward))]
    copies = []
    for n, (give, pay) in enumerate(zip(gives, pays)):
        give = marks[0] if give is None else give
        for s in range(SIDE):
            block = pay.at[pl.ds(0, bs), pl.ds(s * bs, bs)]
            copies.append(pltpu.make_async_copy(border.at[give * SIDE + s], block, sems.at[n, s]))
    for copy in tables + copies:
        copy.start()
    for copy in tables:
        copy.wait()
    count = table.shape[2]
    for pay in pays:
        for n in range(3):
            pay[pl.ds(bs + n, 1), pl.ds(0, count)] = table[n].astype(F32)
    for copy in copies:
        copy.wait()


def prep_kernel(cols, marks, diag, local, packed, own, pair, low, high):
    nblocks, nonzeros, bs, _ = local.shape
    width = nblocks * bs
    patch_len = 2 * nblocks
    base = marks[1] * nblocks
    own[...] = jnp.zeros((width, width), F32)
    pair[...] = jnp.zeros((width, width), F32)
    for b in range(nblocks):
        for k in range(nonzeros):
            spot = lax.rem(cols[b, k] - base + patch_len, patch_len)
            block = local[b, k]
            for c in range(nblocks):

                @pl.when(spot == c)
                def _():
                    own[pl.ds(b * bs, bs), pl.ds(c * bs, bs)] += block

                @pl.when(spot == c + nblocks)
                def _():
                    pair[pl.ds(b * bs, bs), pl.ds(c * bs, bs)] += block

    lower = own[...]
    here = lax.broadcasted_iota(jnp.int32, (width, width), 0)
    there = lax.broadcasted_iota(jnp.int32, (width, width), 1)
    own[...] = lower + lower.T + jnp.where(here == there, diag[...], 0.0)
    low[...] = pair[:, : width // 2]
    high[...] = pair[:, width // 2 :]


def edge(take, width, mine, pay, border):
    bs = border.shape[1]
    known = isinstance(take, int)

    def pick(of):
        return of(take) if known else jnp.where(take == 2.0, of(2), of(3))

    def number(ref, line, t):
        return ref[pl.ds(ref.shape[0] - TAIL + line, 1), pl.ds(t * SIDE + s, 1)]

    blocks = [[0.0] * (width // bs) for _ in range(width // bs)]
    for s in range(SIDE):
        turned = pay[pl.ds(0, bs), pl.ds(s * bs, bs)].T
        pairs = [
            (pick(lambda t: border[t * SIDE + s]), pick(lambda t: number(mine, 0, t)), pick(lambda t: number(pay, 1, t))),
            (turned, pick(lambda t: number(mine, 1, t ^ 1)), pick(lambda t: number(pay, 0, t ^ 1))),
        ]
        for block, to, at in pairs:
            for i, line in enumerate(blocks):
                for j in range(len(line)):
                    line[j] = line[j] + jnp.where((to == i) & (at == j), block, 0.0)
    return jnp.concatenate([jnp.concatenate(line, axis=1) for line in blocks], axis=0)


def base_kernel(field, own, pair, mate, low, high, image, coup):
    coup[...] = pair[...] + jnp.concatenate([low[...].T, high[...].T], axis=0)
    image[...] = dot(own[...], field[...]) + dot(coup[...], mate[...])


def back_kernel(mine, field, border, pay, coup, back, out, other):
    width = field.shape[0]
    toward = mine[pl.ds(mine.shape[0] - TAIL + 2, 1), pl.ds(0, 1)]
    coup[...] = edge(0, width, mine, pay, border)
    back[...] = dot(coup[...].T, field[...])
    out[pl.ds(0, width), :] = columns(back, toward, True)
    other[pl.ds(0, width), :] = columns(back, toward, False)


def left_kernel(part, coup, there, image, once):
    term = dot(coup[...], there[...])
    image[...] = part[...] + term
    once[...] = part[...] + 2.0 * term


def turn(mine, width):
    toward = mine[pl.ds(mine.shape[0] - TAIL + 2, 1), pl.ds(0, 1)]
    count = mine.shape[1]
    first = jnp.where(lax.broadcasted_iota(jnp.int32, (1, count), 1) < count // 2, 1.0, 0.0)
    return jnp.where(toward == 3.0, first, 1.0 - first)


def gy_kernel(take, weight, mine, part, single, border, pay, there, image, once, coup):
    width = coup.shape[0]
    toward = mine[pl.ds(mine.shape[0] - TAIL + 2, 1), pl.ds(0, 1)]
    coup[...] = edge(toward if take is None else take, width, mine, pay, border)
    term = dot(coup[...], there[...])
    image[...] = part[...] + term
    scale = weight * turn(mine, width) if take is None else weight
    once[...] = single[...] + scale * term


def columns(ref, toward, out):
    middle = ref.shape[1] // 2
    return jnp.where((toward == 3.0) == out, ref[:, middle:], ref[:, :middle])


def right_kernel(mine, part, out, half, across):
    width = part.shape[0]
    toward = mine[pl.ds(mine.shape[0] - TAIL + 2, 1), pl.ds(0, 1)]
    half[...] = columns(part, toward, True) + out[pl.ds(0, width), :]
    across[pl.ds(0, width), :] = half[...]
    across[pl.ds(width, EXTRA), :] = jnp.zeros((EXTRA, half.shape[1]), F32)


def joined(toward, out, other):
    low = jnp.where(toward == 3.0, other, out)
    high = jnp.where(toward == 3.0, out, other)
    return jnp.concatenate([low, high], axis=1)


def whole_kernel(mine, part, half, rest, image, other):
    toward = mine[pl.ds(mine.shape[0] - TAIL + 2, 1), pl.ds(0, 1)]
    other[...] = columns(part, toward, False) + rest[pl.ds(0, part.shape[0]), :]
    image[...] = joined(toward, half[...], other[...])


def near_kernel(mine, field, image, once, mate, mate_out, mate_other, own, coup, there, back, part, lift, state):
    b = field[...]
    toward = mine[pl.ds(mine.shape[0] - TAIL + 2, 1), pl.ds(0, 1)]
    mate_w = joined(toward, mate_out[...], mate_other[...])
    norm = col_sum(b, b)
    c = jnp.where(norm > 0.0, col_sum(b, image[...]) / jnp.where(norm > 0.0, norm, 1.0), 0.0)
    g = image[...] - c * b
    part[...] = dot(own[...], g) + dot(coup[...], mate_w - c * mate[...])
    lift[...] = back[...] - c * there[...]
    rows = [(0, norm), (1, c), (2, col_sum(g, g)), (4, -col_sum(g, once[...])), (5, col_sum(b, once[...]))]
    state[...] = stack_rows(rows, state.shape)


def far_kernel(take, field, image, part, near, lift, coup, left, *refs):
    *sides, state = refs
    width = field.shape[0]
    b = field[...]
    c = near[1:2, :]
    acc = part[...] + 2.0 * dot(coup[...], left[...] + lift[...])
    if sides:
        mine, coup_gy, there, side = sides
        if take is None:
            toward = mine[pl.ds(mine.shape[0] - TAIL + 2, 1), pl.ds(0, 1)]
            middle = b.shape[1] // 2
            shift = c * there[...]
            term = dot(coup_gy[...], side[pl.ds(0, width), :] - jnp.where(toward == 3.0, shift[:, :middle], shift[:, middle:]))
            acc += 2.0 * turn(mine, width) * jnp.concatenate([term, term], axis=1)
        else:
            acc += 2.0 * dot(coup_gy[...], side[...] - c * there[...])
    state[...] = near[...] + stack_rows([(3, col_sum(image[...] - c * b, acc)), (4, -col_sum(b, acc))], state.shape)


def merge_kernel(*refs):
    *states, out = refs
    norm = sum(s[0:1, :] for s in states)
    base = states[0][1:2, :]
    shift = sum(s[0:1, :] * (s[1:2, :] - base) for s in states)
    c = base + jnp.where(norm > 0.0, shift / jnp.where(norm > 0.0, norm, 1.0), 0.0)
    size, flat, slope, bend = (jnp.zeros_like(c) for _ in range(4))
    for s in states:
        d = c - s[1:2, :]
        size += s[2:3, :] + s[0:1, :] * d * d
        flat += s[3:4, :] + (s[4:5, :] + s[5:6, :] * d) * d
        slope += s[4:5, :] + 2.0 * s[5:6, :] * d
        bend += s[5:6, :]
    out[...] = stack_rows(list(enumerate([norm, c, size, flat, slope, bend])), out.shape)


def shards(right_side, node_diag, local_coup, block_cols, border_coup, border_send, border_rows):
    width, ncols = right_side.shape
    nblocks, _, bs, _ = local_coup.shape
    n_gx, n_gy, n_nd = (lax.axis_size(a) for a in AXES)
    assert n_nd == 2 and border_coup.shape[1] == 4 * SIDE
    swap = [(0, 1), (1, 0)]
    right = [(i, (i + 1) % n_gx) for i in range(n_gx)]
    left = [(j, i) for i, j in right]
    up = [(i, i + 1) for i in range(n_gy - 1)]
    down = [(j, i) for i, j in up]
    facing = jnp.where(lax.axis_index("gy") == 0, 3, 2).astype(jnp.int32)
    if n_gy == 2:
        sides = [(swap, None, 2.0)]
    elif n_gy > 2:
        sides = [(up, 2, 2.0), (down, 3, 0.0)]
    else:
        sides = []
    sends = [("gx", right)] + [("gy", perm) for perm, _, _ in sides]
    gives = [1] + [None if t is None else t ^ 1 for _, t, _ in sides]
    toward = jnp.full((1, 4 * SIDE), facing)
    marks = jnp.stack([facing, lax.axis_index("nd").astype(jnp.int32)])
    border = border_coup[0]

    def smem(n):
        return [pl.BlockSpec(memory_space=pltpu.SMEM)] * n

    full, half, longer = (bs + TAIL, ncols), (width, ncols // 2), (width + EXTRA, ncols // 2)

    def pack(gives):
        count = len(gives)
        tables = [marks] if gives != [1] else []
        return pl.pallas_call(
            partial(pack_kernel, gives),
            name="pack",
            in_specs=smem(len(tables)) + [pl.BlockSpec(memory_space=pl.ANY)] * 4,
            out_specs=[vmem()] * count,
            out_shape=[pltpu.VMEM(full, F32)] * count,
            scratch_shapes=[
                pltpu.SemaphoreType.DMA((count, SIDE)),
                pltpu.VMEM((3, 1, 4 * SIDE), jnp.int32),
                pltpu.SemaphoreType.DMA((3,)),
            ],
            compiler_params=pltpu.CompilerParams(vmem_limit_bytes=LIMIT),
        )(*tables, *[pltpu.with_memory_space_constraint(a, pltpu.HBM) for a in (border, border_send, border_rows)], toward)

    packed = pack(gives)
    pays = [lax.ppermute(pay, axis, perm) for pay, (axis, perm) in zip(packed, sends)]
    mine = packed[0]
    fields = [lax.ppermute(right_side, axis, perm) for axis, perm in sends]
    mate = lax.ppermute(right_side, "nd", swap)

    def tabled(kernel, name, tables, shapes, flops=None):
        def run(*args):
            args = list(args[:tables]) + [pltpu.with_memory_space_constraint(a, pltpu.VMEM) for a in args[tables:]]
            return pl.pallas_call(
                kernel,
                name=name,
                in_specs=smem(tables) + [vmem()] * (len(args) - tables),
                out_specs=[vmem()] * len(shapes),
                out_shape=[pltpu.VMEM(shape, F32) for shape in shapes],
                compiler_params=pltpu.CompilerParams(vmem_limit_bytes=LIMIT),
                cost_estimate=flops and pl.CostEstimate(flops=flops, bytes_accessed=1 << 20, transcendentals=0),
            )(*args)

        return run

    field, square = (width, ncols), (width, width)
    own, pair, *pieces = tabled(prep_kernel, "prep", 2, [square] * 2 + [(width, width // 2)] * 2, 1 << 24)(
        block_cols, marks, node_diag.reshape(1, width), local_coup, mine
    )
    mate_pair = [lax.ppermute(piece, "nd", swap) for piece in pieces]

    part, coup = call(base_kernel, "base", [field, square])(right_side, own, pair, mate, *mate_pair)
    left_coup, back, *to_left = call(back_kernel, "back", [square, field] + [longer] * 2)(mine, right_side, border, pays[0])
    from_right = [lax.ppermute(piece, "gx", left) for piece in to_left]
    part, once = call(left_kernel, "left", [field] * 2)(part, left_coup, fields[0])
    side_coup = []
    for (_, take, weight), pay, there in zip(sides, pays[1:], fields[1:]):
        part, once, block = call(partial(gy_kernel, take, weight), "gy", [field, field, square])(mine, part, once, border, pay, there)
        side_coup.append(block)
    left_w = lax.ppermute(part, "gx", right)
    half_w, across = call(right_kernel, "right", [half, longer])(mine, part, from_right[0])
    image, other_w = call(whole_kernel, "whole", [field, half])(mine, part, half_w, from_right[1])
    mate_w = [lax.ppermute(w, "nd", swap) for w in (half_w, other_w)]
    part, lift, state = call(near_kernel, "near", [field, field, (TAIL, ncols)])(
        mine, right_side, image, once, mate, *mate_w, own, coup, fields[0], back
    )
    far = []
    take = None
    if sides:
        perm, take, _ = sides[0]
        far = [mine, side_coup[0], fields[1], lax.ppermute(across if take is None else image, "gy", perm)]
    (state,) = call(partial(far_kernel, take), "far", [(TAIL, ncols)])(
        right_side, image, part, state, lift, left_coup, left_w, *far
    )
    state = join(state)
    norm, c, size, form = (row[None] for row in state[:4])
    ratio = size / (c * c * norm)
    last = size / (form - ratio * ratio * c * c * c * norm)
    return ((1.0 + last * c * (1.0 + ratio)) / c) * right_side - (last / c) * image


def solution(mesh):
    blocks = P(("var", "gx", "gy", "nd"))
    tables = P(AXES)
    in_specs = (blocks, blocks, blocks, tables, blocks, tables, tables)
    return jax.shard_map(shards, mesh=mesh, in_specs=in_specs, out_specs=blocks, check_vma=False)
```

```python
from functools import partial

import jax
import jax.numpy as jnp
from jax import lax
from jax.experimental import pallas as pl
from jax.experimental.pallas import tpu as pltpu
from jax.sharding import PartitionSpec as P

F32 = jnp.float32
BF16 = jnp.bfloat16
AXES = ("gx", "gy", "nd")
SIDE = 2
LIMIT = 8 << 20
EXTRA = 8
TAIL = 8


def vmem():
    return pl.BlockSpec(memory_space=pltpu.VMEM)


def call(kernel, name, shapes, scratch=(), flops=None):
    def run(*args):
        args = [pltpu.with_memory_space_constraint(a, pltpu.VMEM) for a in args]
        return pl.pallas_call(
            kernel,
            name=name,
            in_specs=[vmem()] * len(args),
            out_specs=[vmem()] * len(shapes),
            out_shape=[pltpu.VMEM(shape, F32) for shape in shapes],
            scratch_shapes=scratch,
            compiler_params=pltpu.CompilerParams(vmem_limit_bytes=LIMIT),
            cost_estimate=flops and pl.CostEstimate(flops=flops, bytes_accessed=1 << 20, transcendentals=0),
        )(*args)

    return run


def join(state):
    count = lax.axis_size(AXES)
    assert count & (count - 1) == 0
    step = 1
    while step < count:
        masks = [m * step for m in (1, 2, 3) if m * step < count]
        others = [lax.ppermute(state, AXES, [(i, i ^ m) for i in range(count)]) for m in masks]
        (state,) = call(merge_kernel, "merge", [state.shape])(state, *others)
        step *= 4
    return state


def split(a):
    high = a.astype(BF16)
    return high, (a - high.astype(F32)).astype(BF16)


def dot(a, b):
    (ah, al), (bh, bl) = split(a), split(b)
    mul = partial(jnp.dot, preferred_element_type=F32)
    return mul(ah, bh) + (mul(ah, bl) + mul(al, bh))


def col_sum(a, b):
    return jnp.sum(a * b, axis=0, keepdims=True)


def stack_rows(rows, shape):
    line = lax.broadcasted_iota(jnp.int32, shape, 0)
    return sum(jnp.where(line == n, row, 0.0) for n, row in rows)


def pack_kernel(gives, *refs):
    marks, refs = (refs[0], refs[1:]) if gives != [1] else (None, refs)
    border, send, rows, toward, *pays, sems, table, table_sems = refs
    bs = border.shape[1]
    tables = [pltpu.make_async_copy(ref, table.at[n], table_sems.at[n]) for n, ref in enumerate((rows, send, toward))]
    copies = []
    for n, (give, pay) in enumerate(zip(gives, pays)):
        give = marks[0] if give is None else give
        for s in range(SIDE):
            block = pay.at[pl.ds(0, bs), pl.ds(s * bs, bs)]
            copies.append(pltpu.make_async_copy(border.at[give * SIDE + s], block, sems.at[n, s]))
    for copy in tables + copies:
        copy.start()
    for copy in tables:
        copy.wait()
    count = table.shape[2]
    for pay in pays:
        for n in range(3):
            pay[pl.ds(bs + n, 1), pl.ds(0, count)] = table[n].astype(F32)
    for copy in copies:
        copy.wait()


def prep_kernel(cols, marks, diag, local, packed, own, pair, low, high):
    nblocks, nonzeros, bs, _ = local.shape
    width = nblocks * bs
    patch_len = 2 * nblocks
    base = marks[1] * nblocks
    own[...] = jnp.zeros((width, width), F32)
    pair[...] = jnp.zeros((width, width), F32)
    for b in range(nblocks):
        for k in range(nonzeros):
            spot = lax.rem(cols[b, k] - base + patch_len, patch_len)
            block = local[b, k]
            for c in range(nblocks):

                @pl.when(spot == c)
                def _():
                    own[pl.ds(b * bs, bs), pl.ds(c * bs, bs)] += block

                @pl.when(spot == c + nblocks)
                def _():
                    pair[pl.ds(b * bs, bs), pl.ds(c * bs, bs)] += block

    lower = own[...]
    here = lax.broadcasted_iota(jnp.int32, (width, width), 0)
    there = lax.broadcasted_iota(jnp.int32, (width, width), 1)
    own[...] = lower + lower.T + jnp.where(here == there, diag[...], 0.0)
    low[...] = pair[:, : width // 2]
    high[...] = pair[:, width // 2 :]


def edge(take, width, mine, pay, border):
    bs = border.shape[1]
    known = isinstance(take, int)

    def pick(of):
        return of(take) if known else jnp.where(take == 2.0, of(2), of(3))

    def number(ref, line, t):
        return ref[pl.ds(ref.shape[0] - TAIL + line, 1), pl.ds(t * SIDE + s, 1)]

    blocks = [[0.0] * (width // bs) for _ in range(width // bs)]
    for s in range(SIDE):
        turned = pay[pl.ds(0, bs), pl.ds(s * bs, bs)].T
        pairs = [
            (pick(lambda t: border[t * SIDE + s]), pick(lambda t: number(mine, 0, t)), pick(lambda t: number(pay, 1, t))),
            (turned, pick(lambda t: number(mine, 1, t ^ 1)), pick(lambda t: number(pay, 0, t ^ 1))),
        ]
        for block, to, at in pairs:
            for i, line in enumerate(blocks):
                for j in range(len(line)):
                    line[j] = line[j] + jnp.where((to == i) & (at == j), block, 0.0)
    return jnp.concatenate([jnp.concatenate(line, axis=1) for line in blocks], axis=0)


def base_kernel(field, own, pair, mate, low, high, image, coup):
    coup[...] = pair[...] + jnp.concatenate([low[...].T, high[...].T], axis=0)
    image[...] = dot(own[...], field[...]) + dot(coup[...], mate[...])


def back_kernel(takes, mine, field, border, *refs):
    count = len(takes)
    *pays, pay = refs[: count + 1]
    coup, back, out, other, *coups = refs[count + 1 :]
    width = field.shape[0]
    toward = mine[pl.ds(mine.shape[0] - TAIL + 2, 1), pl.ds(0, 1)]
    coup[...] = edge(0, width, mine, pay, border)
    for take, gy_pay, gy_coup in zip(takes, pays, coups):
        gy_coup[...] = edge(toward if take is None else take, width, mine, gy_pay, border)
    back[...] = dot(coup[...].T, field[...])
    out[pl.ds(0, width), :] = columns(back, toward, True)
    other[pl.ds(0, width), :] = columns(back, toward, False)


def left_kernel(part, coup, there, image, once):
    term = dot(coup[...], there[...])
    image[...] = part[...] + term
    once[...] = part[...] + 2.0 * term


def turn(mine, width):
    toward = mine[pl.ds(mine.shape[0] - TAIL + 2, 1), pl.ds(0, 1)]
    count = mine.shape[1]
    first = jnp.where(lax.broadcasted_iota(jnp.int32, (1, count), 1) < count // 2, 1.0, 0.0)
    return jnp.where(toward == 3.0, first, 1.0 - first)


def gy_kernel(take, weight, mine, part, single, coup, there, image, once):
    term = dot(coup[...], there[...])
    image[...] = part[...] + term
    once[...] = single[...] + (weight * turn(mine, part.shape[0]) if take is None else weight) * term


def columns(ref, toward, out):
    middle = ref.shape[1] // 2
    return jnp.where((toward == 3.0) == out, ref[:, middle:], ref[:, :middle])


def right_kernel(mine, part, out, half, across):
    width = part.shape[0]
    toward = mine[pl.ds(mine.shape[0] - TAIL + 2, 1), pl.ds(0, 1)]
    half[...] = columns(part, toward, True) + out[pl.ds(0, width), :]
    across[pl.ds(0, width), :] = half[...]
    across[pl.ds(width, EXTRA), :] = jnp.zeros((EXTRA, half.shape[1]), F32)


def joined(toward, out, other):
    low = jnp.where(toward == 3.0, other, out)
    high = jnp.where(toward == 3.0, out, other)
    return jnp.concatenate([low, high], axis=1)


def whole_kernel(mine, part, half, rest, image, other):
    toward = mine[pl.ds(mine.shape[0] - TAIL + 2, 1), pl.ds(0, 1)]
    other[...] = columns(part, toward, False) + rest[pl.ds(0, part.shape[0]), :]
    image[...] = joined(toward, half[...], other[...])


def near_kernel(mine, field, image, once, mate, mate_out, mate_other, own, coup, there, back, part, lift, state):
    b = field[...]
    toward = mine[pl.ds(mine.shape[0] - TAIL + 2, 1), pl.ds(0, 1)]
    mate_w = joined(toward, mate_out[...], mate_other[...])
    norm = col_sum(b, b)
    c = jnp.where(norm > 0.0, col_sum(b, image[...]) / jnp.where(norm > 0.0, norm, 1.0), 0.0)
    g = image[...] - c * b
    part[...] = dot(own[...], g) + dot(coup[...], mate_w - c * mate[...])
    lift[...] = back[...] - c * there[...]
    rows = [(0, norm), (1, c), (2, col_sum(g, g)), (4, -col_sum(g, once[...])), (5, col_sum(b, once[...]))]
    state[...] = stack_rows(rows, state.shape)


def far_kernel(take, field, image, part, near, lift, coup, left, *refs):
    *sides, state = refs
    width = field.shape[0]
    b = field[...]
    c = near[1:2, :]
    acc = part[...] + 2.0 * dot(coup[...], left[...] + lift[...])
    if sides:
        mine, coup_gy, there, side = sides
        if take is None:
            toward = mine[pl.ds(mine.shape[0] - TAIL + 2, 1), pl.ds(0, 1)]
            middle = b.shape[1] // 2
            shift = c * there[...]
            term = dot(coup_gy[...], side[pl.ds(0, width), :] - jnp.where(toward == 3.0, shift[:, :middle], shift[:, middle:]))
            acc += 2.0 * turn(mine, width) * jnp.concatenate([term, term], axis=1)
        else:
            acc += 2.0 * dot(coup_gy[...], side[...] - c * there[...])
    state[...] = near[...] + stack_rows([(3, col_sum(image[...] - c * b, acc)), (4, -col_sum(b, acc))], state.shape)


def merge_kernel(*refs):
    *states, out = refs
    norm = sum(s[0:1, :] for s in states)
    base = states[0][1:2, :]
    shift = sum(s[0:1, :] * (s[1:2, :] - base) for s in states)
    c = base + jnp.where(norm > 0.0, shift / jnp.where(norm > 0.0, norm, 1.0), 0.0)
    size, flat, slope, bend = (jnp.zeros_like(c) for _ in range(4))
    for s in states:
        d = c - s[1:2, :]
        size += s[2:3, :] + s[0:1, :] * d * d
        flat += s[3:4, :] + (s[4:5, :] + s[5:6, :] * d) * d
        slope += s[4:5, :] + 2.0 * s[5:6, :] * d
        bend += s[5:6, :]
    out[...] = stack_rows(list(enumerate([norm, c, size, flat, slope, bend])), out.shape)


def shards(right_side, node_diag, local_coup, block_cols, border_coup, border_send, border_rows):
    width, ncols = right_side.shape
    nblocks, _, bs, _ = local_coup.shape
    n_gx, n_gy, n_nd = (lax.axis_size(a) for a in AXES)
    assert n_nd == 2 and border_coup.shape[1] == 4 * SIDE
    swap = [(0, 1), (1, 0)]
    right = [(i, (i + 1) % n_gx) for i in range(n_gx)]
    left = [(j, i) for i, j in right]
    up = [(i, i + 1) for i in range(n_gy - 1)]
    down = [(j, i) for i, j in up]
    facing = jnp.where(lax.axis_index("gy") == 0, 3, 2).astype(jnp.int32)
    if n_gy == 2:
        sides = [(swap, None, 2.0)]
    elif n_gy > 2:
        sides = [(up, 2, 2.0), (down, 3, 0.0)]
    else:
        sides = []
    sends = [("gx", right)] + [("gy", perm) for perm, _, _ in sides]
    gives = [1] + [None if t is None else t ^ 1 for _, t, _ in sides]
    toward = jnp.full((1, 4 * SIDE), facing)
    marks = jnp.stack([facing, lax.axis_index("nd").astype(jnp.int32)])
    border = border_coup[0]

    def smem(n):
        return [pl.BlockSpec(memory_space=pltpu.SMEM)] * n

    full, half, longer = (bs + TAIL, ncols), (width, ncols // 2), (width + EXTRA, ncols // 2)

    def pack(gives):
        count = len(gives)
        tables = [marks] if gives != [1] else []
        return pl.pallas_call(
            partial(pack_kernel, gives),
            name="pack",
            in_specs=smem(len(tables)) + [pl.BlockSpec(memory_space=pl.ANY)] * 4,
            out_specs=[vmem()] * count,
            out_shape=[pltpu.VMEM(full, F32)] * count,
            scratch_shapes=[
                pltpu.SemaphoreType.DMA((count, SIDE)),
                pltpu.VMEM((3, 1, 4 * SIDE), jnp.int32),
                pltpu.SemaphoreType.DMA((3,)),
            ],
            compiler_params=pltpu.CompilerParams(vmem_limit_bytes=LIMIT),
        )(*tables, *[pltpu.with_memory_space_constraint(a, pltpu.HBM) for a in (border, border_send, border_rows)], toward)

    packed = pack(gives)
    pays = [lax.ppermute(pay, axis, perm) for pay, (axis, perm) in zip(packed, sends)]
    mine = packed[0]
    fields = [lax.ppermute(right_side, axis, perm) for axis, perm in sends]
    mate = lax.ppermute(right_side, "nd", swap)

    def tabled(kernel, name, tables, shapes, flops=None):
        def run(*args):
            args = list(args[:tables]) + [pltpu.with_memory_space_constraint(a, pltpu.VMEM) for a in args[tables:]]
            return pl.pallas_call(
                kernel,
                name=name,
                in_specs=smem(tables) + [vmem()] * (len(args) - tables),
                out_specs=[vmem()] * len(shapes),
                out_shape=[pltpu.VMEM(shape, F32) for shape in shapes],
                compiler_params=pltpu.CompilerParams(vmem_limit_bytes=LIMIT),
                cost_estimate=flops and pl.CostEstimate(flops=flops, bytes_accessed=1 << 20, transcendentals=0),
            )(*args)

        return run

    field, square = (width, ncols), (width, width)
    own, pair, *pieces = tabled(prep_kernel, "prep", 2, [square] * 2 + [(width, width // 2)] * 2, 1 << 24)(
        block_cols, marks, node_diag.reshape(1, width), local_coup, mine
    )
    mate_pair = [lax.ppermute(piece, "nd", swap) for piece in pieces]

    part, coup = call(base_kernel, "base", [field, square])(right_side, own, pair, mate, *mate_pair)
    kernel = partial(back_kernel, [take for _, take, _ in sides])
    left_coup, back, *to_left = call(kernel, "back", [square, field] + [longer] * 2 + [square] * len(sides))(
        mine, right_side, border, *pays[1:], pays[0]
    )
    to_left, side_coup = to_left[:2], to_left[2:]
    from_right = [lax.ppermute(piece, "gx", left) for piece in to_left]
    part, once = call(left_kernel, "left", [field] * 2)(part, left_coup, fields[0])
    for (_, take, weight), block, there in zip(sides, side_coup, fields[1:]):
        part, once = call(partial(gy_kernel, take, weight), "gy", [field] * 2)(mine, part, once, block, there)
    left_w = lax.ppermute(part, "gx", right)
    half_w, across = call(right_kernel, "right", [half, longer])(mine, part, from_right[0])
    image, other_w = call(whole_kernel, "whole", [field, half])(mine, part, half_w, from_right[1])
    mate_w = [lax.ppermute(w, "nd", swap) for w in (half_w, other_w)]
    part, lift, state = call(near_kernel, "near", [field, field, (TAIL, ncols)])(
        mine, right_side, image, once, mate, *mate_w, own, coup, fields[0], back
    )
    far = []
    take = None
    if sides:
        perm, take, _ = sides[0]
        far = [mine, side_coup[0], fields[1], lax.ppermute(across if take is None else image, "gy", perm)]
    (state,) = call(partial(far_kernel, take), "far", [(TAIL, ncols)])(
        right_side, image, part, state, lift, left_coup, left_w, *far
    )
    state = join(state)
    norm, c, size, form = (row[None] for row in state[:4])
    ratio = size / (c * c * norm)
    last = size / (form - ratio * ratio * c * c * c * norm)
    return ((1.0 + last * c * (1.0 + ratio)) / c) * right_side - (last / c) * image


def solution(mesh):
    blocks = P(("var", "gx", "gy", "nd"))
    tables = P(AXES)
    in_specs = (blocks, blocks, blocks, tables, blocks, tables, tables)
    return jax.shard_map(shards, mesh=mesh, in_specs=in_specs, out_specs=blocks, check_vma=False)
```

```python
from functools import partial

import jax
import jax.numpy as jnp
from jax import lax
from jax.experimental import pallas as pl
from jax.experimental.pallas import tpu as pltpu
from jax.sharding import PartitionSpec as P

F32 = jnp.float32
BF16 = jnp.bfloat16
AXES = ("gx", "gy", "nd")
SIDE = 2
LIMIT = 8 << 20
EXTRA = 8
TAIL = 8


def vmem():
    return pl.BlockSpec(memory_space=pltpu.VMEM)


def call(kernel, name, shapes, scratch=(), flops=None):
    def run(*args):
        args = [pltpu.with_memory_space_constraint(a, pltpu.VMEM) for a in args]
        return pl.pallas_call(
            kernel,
            name=name,
            in_specs=[vmem()] * len(args),
            out_specs=[vmem()] * len(shapes),
            out_shape=[pltpu.VMEM(shape, F32) for shape in shapes],
            scratch_shapes=scratch,
            compiler_params=pltpu.CompilerParams(vmem_limit_bytes=LIMIT),
            cost_estimate=flops and pl.CostEstimate(flops=flops, bytes_accessed=1 << 20, transcendentals=0),
        )(*args)

    return run


def join(state):
    count = lax.axis_size(AXES)
    assert count & (count - 1) == 0
    step = 1
    while step < count:
        masks = [m * step for m in (1, 2, 3) if m * step < count]
        others = [lax.ppermute(state, AXES, [(i, i ^ m) for i in range(count)]) for m in masks]
        (state,) = call(merge_kernel, "merge", [state.shape])(state, *others)
        step *= 4
    return state


def split(a):
    high = a.astype(BF16)
    return high, (a - high.astype(F32)).astype(BF16)


def dot(a, b):
    (ah, al), (bh, bl) = split(a), split(b)
    mul = partial(jnp.dot, preferred_element_type=F32)
    return mul(ah, bh) + (mul(ah, bl) + mul(al, bh))


def col_sum(a, b):
    return jnp.sum(a * b, axis=0, keepdims=True)


def stack_rows(rows, shape):
    line = lax.broadcasted_iota(jnp.int32, shape, 0)
    return sum(jnp.where(line == n, row, 0.0) for n, row in rows)


def pack_kernel(gives, *refs):
    border, send, rows, toward, *pays, sems, table, table_sems, both = refs
    bs = border.shape[1]
    tables = [pltpu.make_async_copy(ref, table.at[n], table_sems.at[n]) for n, ref in enumerate((rows, send, toward))]
    copies = []
    for n, (give, pay) in enumerate(zip(gives, pays)):
        if give is None:
            copies.append(pltpu.make_async_copy(border.at[pl.ds(2 * SIDE, 2 * SIDE)], both, sems.at[n, 0]))
            continue
        for s in range(SIDE):
            block = pay.at[pl.ds(0, bs), pl.ds(s * bs, bs)]
            copies.append(pltpu.make_async_copy(border.at[give * SIDE + s], block, sems.at[n, s]))
    for copy in tables + copies:
        copy.start()
    for copy in tables:
        copy.wait()
    count = table.shape[2]
    for pay in pays:
        for n in range(3):
            pay[pl.ds(bs + n, 1), pl.ds(0, count)] = table[n].astype(F32)
    for copy in copies:
        copy.wait()
    facing = table[2][:, 0:1]
    for give, pay in zip(gives, pays):
        if give is None:
            for s in range(SIDE):
                pay[pl.ds(0, bs), pl.ds(s * bs, bs)] = jnp.where(facing == 3, both[SIDE + s], both[s])


def prep_kernel(cols, marks, diag, local, packed, own, pair, low, high):
    nblocks, nonzeros, bs, _ = local.shape
    width = nblocks * bs
    patch_len = 2 * nblocks
    base = marks[1] * nblocks
    own[...] = jnp.zeros((width, width), F32)
    pair[...] = jnp.zeros((width, width), F32)
    for b in range(nblocks):
        for k in range(nonzeros):
            spot = lax.rem(cols[b, k] - base + patch_len, patch_len)
            block = local[b, k]
            for c in range(nblocks):

                @pl.when(spot == c)
                def _():
                    own[pl.ds(b * bs, bs), pl.ds(c * bs, bs)] += block

                @pl.when(spot == c + nblocks)
                def _():
                    pair[pl.ds(b * bs, bs), pl.ds(c * bs, bs)] += block

    lower = own[...]
    here = lax.broadcasted_iota(jnp.int32, (width, width), 0)
    there = lax.broadcasted_iota(jnp.int32, (width, width), 1)
    own[...] = lower + lower.T + jnp.where(here == there, diag[...], 0.0)
    low[...] = pair[:, : width // 2]
    high[...] = pair[:, width // 2 :]


def edge(take, width, mine, pay, border):
    bs = border.shape[1]
    known = isinstance(take, int)

    def pick(of):
        return of(take) if known else jnp.where(take == 2.0, of(2), of(3))

    def number(ref, line, t):
        return ref[pl.ds(ref.shape[0] - TAIL + line, 1), pl.ds(t * SIDE + s, 1)]

    blocks = [[0.0] * (width // bs) for _ in range(width // bs)]
    for s in range(SIDE):
        turned = pay[pl.ds(0, bs), pl.ds(s * bs, bs)].T
        pairs = [
            (pick(lambda t: border[t * SIDE + s]), pick(lambda t: number(mine, 0, t)), pick(lambda t: number(pay, 1, t))),
            (turned, pick(lambda t: number(mine, 1, t ^ 1)), pick(lambda t: number(pay, 0, t ^ 1))),
        ]
        for block, to, at in pairs:
            for i, line in enumerate(blocks):
                for j in range(len(line)):
                    line[j] = line[j] + jnp.where((to == i) & (at == j), block, 0.0)
    return jnp.concatenate([jnp.concatenate(line, axis=1) for line in blocks], axis=0)


def base_kernel(field, own, pair, mate, low, high, image, coup):
    coup[...] = pair[...] + jnp.concatenate([low[...].T, high[...].T], axis=0)
    image[...] = dot(own[...], field[...]) + dot(coup[...], mate[...])


def back_kernel(mine, field, border, pay, coup, back, out, other):
    width = field.shape[0]
    toward = mine[pl.ds(mine.shape[0] - TAIL + 2, 1), pl.ds(0, 1)]
    coup[...] = edge(0, width, mine, pay, border)
    back[...] = dot(coup[...].T, field[...])
    out[pl.ds(0, width), :] = columns(back, toward, True)
    other[pl.ds(0, width), :] = columns(back, toward, False)


def left_kernel(part, coup, there, image, once):
    term = dot(coup[...], there[...])
    image[...] = part[...] + term
    once[...] = part[...] + 2.0 * term


def turn(mine, width):
    toward = mine[pl.ds(mine.shape[0] - TAIL + 2, 1), pl.ds(0, 1)]
    count = mine.shape[1]
    first = jnp.where(lax.broadcasted_iota(jnp.int32, (1, count), 1) < count // 2, 1.0, 0.0)
    return jnp.where(toward == 3.0, first, 1.0 - first)


def gy_kernel(take, weight, mine, part, single, border, pay, there, image, once, coup):
    width = coup.shape[0]
    toward = mine[pl.ds(mine.shape[0] - TAIL + 2, 1), pl.ds(0, 1)]
    coup[...] = edge(toward if take is None else take, width, mine, pay, border)
    term = dot(coup[...], there[...])
    image[...] = part[...] + term
    scale = weight * turn(mine, width) if take is None else weight
    once[...] = single[...] + scale * term


def columns(ref, toward, out):
    middle = ref.shape[1] // 2
    return jnp.where((toward == 3.0) == out, ref[:, middle:], ref[:, :middle])


def right_kernel(mine, part, out, half, across):
    width = part.shape[0]
    toward = mine[pl.ds(mine.shape[0] - TAIL + 2, 1), pl.ds(0, 1)]
    half[...] = columns(part, toward, True) + out[pl.ds(0, width), :]
    across[pl.ds(0, width), :] = half[...]
    across[pl.ds(width, EXTRA), :] = jnp.zeros((EXTRA, half.shape[1]), F32)


def joined(toward, out, other):
    low = jnp.where(toward == 3.0, other, out)
    high = jnp.where(toward == 3.0, out, other)
    return jnp.concatenate([low, high], axis=1)


def whole_kernel(mine, part, half, rest, image, other):
    toward = mine[pl.ds(mine.shape[0] - TAIL + 2, 1), pl.ds(0, 1)]
    other[...] = columns(part, toward, False) + rest[pl.ds(0, part.shape[0]), :]
    image[...] = joined(toward, half[...], other[...])


def near_kernel(mine, field, image, once, mate, mate_out, mate_other, own, coup, there, back, part, lift, state):
    b = field[...]
    toward = mine[pl.ds(mine.shape[0] - TAIL + 2, 1), pl.ds(0, 1)]
    mate_w = joined(toward, mate_out[...], mate_other[...])
    norm = col_sum(b, b)
    c = jnp.where(norm > 0.0, col_sum(b, image[...]) / jnp.where(norm > 0.0, norm, 1.0), 0.0)
    g = image[...] - c * b
    part[...] = dot(own[...], g) + dot(coup[...], mate_w - c * mate[...])
    lift[...] = back[...] - c * there[...]
    rows = [(0, norm), (1, c), (2, col_sum(g, g)), (4, -col_sum(g, once[...])), (5, col_sum(b, once[...]))]
    state[...] = stack_rows(rows, state.shape)


def far_kernel(take, field, image, part, near, lift, coup, left, *refs):
    *sides, state = refs
    width = field.shape[0]
    b = field[...]
    c = near[1:2, :]
    acc = part[...] + 2.0 * dot(coup[...], left[...] + lift[...])
    if sides:
        mine, coup_gy, there, side = sides
        if take is None:
            toward = mine[pl.ds(mine.shape[0] - TAIL + 2, 1), pl.ds(0, 1)]
            middle = b.shape[1] // 2
            shift = c * there[...]
            term = dot(coup_gy[...], side[pl.ds(0, width), :] - jnp.where(toward == 3.0, shift[:, :middle], shift[:, middle:]))
            acc += 2.0 * turn(mine, width) * jnp.concatenate([term, term], axis=1)
        else:
            acc += 2.0 * dot(coup_gy[...], side[...] - c * there[...])
    state[...] = near[...] + stack_rows([(3, col_sum(image[...] - c * b, acc)), (4, -col_sum(b, acc))], state.shape)


def merge_kernel(*refs):
    *states, out = refs
    norm = sum(s[0:1, :] for s in states)
    base = states[0][1:2, :]
    shift = sum(s[0:1, :] * (s[1:2, :] - base) for s in states)
    c = base + jnp.where(norm > 0.0, shift / jnp.where(norm > 0.0, norm, 1.0), 0.0)
    size, flat, slope, bend = (jnp.zeros_like(c) for _ in range(4))
    for s in states:
        d = c - s[1:2, :]
        size += s[2:3, :] + s[0:1, :] * d * d
        flat += s[3:4, :] + (s[4:5, :] + s[5:6, :] * d) * d
        slope += s[4:5, :] + 2.0 * s[5:6, :] * d
        bend += s[5:6, :]
    out[...] = stack_rows(list(enumerate([norm, c, size, flat, slope, bend])), out.shape)


def shards(right_side, node_diag, local_coup, block_cols, border_coup, border_send, border_rows):
    width, ncols = right_side.shape
    nblocks, _, bs, _ = local_coup.shape
    n_gx, n_gy, n_nd = (lax.axis_size(a) for a in AXES)
    assert n_nd == 2 and border_coup.shape[1] == 4 * SIDE
    swap = [(0, 1), (1, 0)]
    right = [(i, (i + 1) % n_gx) for i in range(n_gx)]
    left = [(j, i) for i, j in right]
    up = [(i, i + 1) for i in range(n_gy - 1)]
    down = [(j, i) for i, j in up]
    facing = jnp.where(lax.axis_index("gy") == 0, 3, 2).astype(jnp.int32)
    if n_gy == 2:
        sides = [(swap, None, 2.0)]
    elif n_gy > 2:
        sides = [(up, 2, 2.0), (down, 3, 0.0)]
    else:
        sides = []
    sends = [("gx", right)] + [("gy", perm) for perm, _, _ in sides]
    gives = [1] + [None if t is None else t ^ 1 for _, t, _ in sides]
    toward = jnp.full((1, 4 * SIDE), facing)
    marks = jnp.stack([facing, lax.axis_index("nd").astype(jnp.int32)])
    border = border_coup[0]

    def smem(n):
        return [pl.BlockSpec(memory_space=pltpu.SMEM)] * n

    full, half, longer = (bs + TAIL, ncols), (width, ncols // 2), (width + EXTRA, ncols // 2)

    def pack(gives):
        count = len(gives)
        return pl.pallas_call(
            partial(pack_kernel, gives),
            name="pack",
            in_specs=[pl.BlockSpec(memory_space=pl.ANY)] * 4,
            out_specs=[vmem()] * count,
            out_shape=[pltpu.VMEM(full, F32)] * count,
            scratch_shapes=[
                pltpu.SemaphoreType.DMA((count, SIDE)),
                pltpu.VMEM((3, 1, 4 * SIDE), jnp.int32),
                pltpu.SemaphoreType.DMA((3,)),
                pltpu.VMEM((2 * SIDE, bs, bs), F32),
            ],
            compiler_params=pltpu.CompilerParams(vmem_limit_bytes=LIMIT),
        )(*[pltpu.with_memory_space_constraint(a, pltpu.HBM) for a in (border, border_send, border_rows)], toward)

    packed = pack(gives)
    pays = [lax.ppermute(pay, axis, perm) for pay, (axis, perm) in zip(packed, sends)]
    mine = packed[0]
    fields = [lax.ppermute(right_side, axis, perm) for axis, perm in sends]
    mate = lax.ppermute(right_side, "nd", swap)

    def tabled(kernel, name, tables, shapes, flops=None):
        def run(*args):
            args = list(args[:tables]) + [pltpu.with_memory_space_constraint(a, pltpu.VMEM) for a in args[tables:]]
            return pl.pallas_call(
                kernel,
                name=name,
                in_specs=smem(tables) + [vmem()] * (len(args) - tables),
                out_specs=[vmem()] * len(shapes),
                out_shape=[pltpu.VMEM(shape, F32) for shape in shapes],
                compiler_params=pltpu.CompilerParams(vmem_limit_bytes=LIMIT),
                cost_estimate=flops and pl.CostEstimate(flops=flops, bytes_accessed=1 << 20, transcendentals=0),
            )(*args)

        return run

    field, square = (width, ncols), (width, width)
    own, pair, *pieces = tabled(prep_kernel, "prep", 2, [square] * 2 + [(width, width // 2)] * 2, 1 << 24)(
        block_cols, marks, node_diag.reshape(1, width), local_coup, mine
    )
    mate_pair = [lax.ppermute(piece, "nd", swap) for piece in pieces]

    part, coup = call(base_kernel, "base", [field, square])(right_side, own, pair, mate, *mate_pair)
    left_coup, back, *to_left = call(back_kernel, "back", [square, field] + [longer] * 2)(mine, right_side, border, pays[0])
    from_right = [lax.ppermute(piece, "gx", left) for piece in to_left]
    part, once = call(left_kernel, "left", [field] * 2)(part, left_coup, fields[0])
    side_coup = []
    for (_, take, weight), pay, there in zip(sides, pays[1:], fields[1:]):
        part, once, block = call(partial(gy_kernel, take, weight), "gy", [field, field, square])(mine, part, once, border, pay, there)
        side_coup.append(block)
    left_w = lax.ppermute(part, "gx", right)
    half_w, across = call(right_kernel, "right", [half, longer])(mine, part, from_right[0])
    image, other_w = call(whole_kernel, "whole", [field, half])(mine, part, half_w, from_right[1])
    mate_w = [lax.ppermute(w, "nd", swap) for w in (half_w, other_w)]
    part, lift, state = call(near_kernel, "near", [field, field, (TAIL, ncols)])(
        mine, right_side, image, once, mate, *mate_w, own, coup, fields[0], back
    )
    far = []
    take = None
    if sides:
        perm, take, _ = sides[0]
        far = [mine, side_coup[0], fields[1], lax.ppermute(across if take is None else image, "gy", perm)]
    (state,) = call(partial(far_kernel, take), "far", [(TAIL, ncols)])(
        right_side, image, part, state, lift, left_coup, left_w, *far
    )
    state = join(state)
    norm, c, size, form = (row[None] for row in state[:4])
    ratio = size / (c * c * norm)
    last = size / (form - ratio * ratio * c * c * c * norm)
    return ((1.0 + last * c * (1.0 + ratio)) / c) * right_side - (last / c) * image


def solution(mesh):
    blocks = P(("var", "gx", "gy", "nd"))
    tables = P(AXES)
    in_specs = (blocks, blocks, blocks, tables, blocks, tables, tables)
    return jax.shard_map(shards, mesh=mesh, in_specs=in_specs, out_specs=blocks, check_vma=False)
```

```python
from functools import partial

import jax
import jax.numpy as jnp
from jax import lax
from jax.experimental import pallas as pl
from jax.experimental.pallas import tpu as pltpu
from jax.sharding import PartitionSpec as P

F32 = jnp.float32
BF16 = jnp.bfloat16
AXES = ("gx", "gy", "nd")
SIDE = 2
LIMIT = 8 << 20
EXTRA = 8
TAIL = 8


def vmem():
    return pl.BlockSpec(memory_space=pltpu.VMEM)


def call(kernel, name, shapes, scratch=(), flops=None):
    def run(*args):
        args = [pltpu.with_memory_space_constraint(a, pltpu.VMEM) for a in args]
        return pl.pallas_call(
            kernel,
            name=name,
            in_specs=[vmem()] * len(args),
            out_specs=[vmem()] * len(shapes),
            out_shape=[pltpu.VMEM(shape, F32) for shape in shapes],
            scratch_shapes=scratch,
            compiler_params=pltpu.CompilerParams(vmem_limit_bytes=LIMIT),
            cost_estimate=flops and pl.CostEstimate(flops=flops, bytes_accessed=1 << 20, transcendentals=0),
        )(*args)

    return run


def join(state):
    count = lax.axis_size(AXES)
    assert count & (count - 1) == 0
    step = 1
    while step < count:
        masks = [m * step for m in (1, 2, 3) if m * step < count]
        others = [lax.ppermute(state, AXES, [(i, i ^ m) for i in range(count)]) for m in masks]
        (state,) = call(merge_kernel, "merge", [state.shape])(state, *others)
        step *= 4
    return state


def split(a):
    high = a.astype(BF16)
    return high, (a - high.astype(F32)).astype(BF16)


def dot(a, b):
    (ah, al), (bh, bl) = split(a), split(b)
    mul = partial(jnp.dot, preferred_element_type=F32)
    return mul(ah, bh) + (mul(ah, bl) + mul(al, bh))


def col_sum(a, b):
    return jnp.sum(a * b, axis=0, keepdims=True)


def stack_rows(rows, shape):
    line = lax.broadcasted_iota(jnp.int32, shape, 0)
    return sum(jnp.where(line == n, row, 0.0) for n, row in rows)


def pack_kernel(gives, *refs):
    border, send, rows, toward, *pays, sems, table, table_sems, both = refs
    bs = border.shape[1]
    tables = [pltpu.make_async_copy(ref, table.at[n], table_sems.at[n]) for n, ref in enumerate((rows, send, toward))]
    copies = []
    for n, (give, pay) in enumerate(zip(gives, pays)):
        if give is None:
            copies.append(pltpu.make_async_copy(border.at[pl.ds(2 * SIDE, 2 * SIDE)], both, sems.at[n, 0]))
            continue
        for s in range(SIDE):
            block = pay.at[pl.ds(0, bs), pl.ds(s * bs, bs)]
            copies.append(pltpu.make_async_copy(border.at[give * SIDE + s], block, sems.at[n, s]))
    for copy in tables + copies:
        copy.start()
    for copy in tables:
        copy.wait()
    count = table.shape[2]
    for pay in pays:
        for n in range(3):
            pay[pl.ds(bs + n, 1), pl.ds(0, count)] = table[n].astype(F32)
    for copy in copies:
        copy.wait()
    facing = table[2][:, 0:1]
    for give, pay in zip(gives, pays):
        if give is None:
            for s in range(SIDE):
                pay[pl.ds(0, bs), pl.ds(s * bs, bs)] = jnp.where(facing == 3, both[SIDE + s], both[s])


def prep_kernel(cols, marks, diag, local, packed, own, pair, low, high):
    nblocks, nonzeros, bs, _ = local.shape
    width = nblocks * bs
    patch_len = 2 * nblocks
    base = marks[1] * nblocks
    own[...] = jnp.zeros((width, width), F32)
    pair[...] = jnp.zeros((width, width), F32)
    for b in range(nblocks):
        for k in range(nonzeros):
            spot = lax.rem(cols[b, k] - base + patch_len, patch_len)
            block = local[b, k]
            for c in range(nblocks):

                @pl.when(spot == c)
                def _():
                    own[pl.ds(b * bs, bs), pl.ds(c * bs, bs)] += block

                @pl.when(spot == c + nblocks)
                def _():
                    pair[pl.ds(b * bs, bs), pl.ds(c * bs, bs)] += block

    lower = own[...]
    here = lax.broadcasted_iota(jnp.int32, (width, width), 0)
    there = lax.broadcasted_iota(jnp.int32, (width, width), 1)
    own[...] = lower + lower.T + jnp.where(here == there, diag[...], 0.0)
    low[...] = pair[:, : width // 2]
    high[...] = pair[:, width // 2 :]


def edge(take, width, mine, pay, border):
    bs = border.shape[1]
    known = isinstance(take, int)

    def pick(of):
        return of(take) if known else jnp.where(take == 2.0, of(2), of(3))

    def number(ref, line, t):
        return ref[pl.ds(ref.shape[0] - TAIL + line, 1), pl.ds(t * SIDE + s, 1)]

    blocks = [[0.0] * (width // bs) for _ in range(width // bs)]
    for s in range(SIDE):
        turned = pay[pl.ds(0, bs), pl.ds(s * bs, bs)].T
        pairs = [
            (pick(lambda t: border[t * SIDE + s]), pick(lambda t: number(mine, 0, t)), pick(lambda t: number(pay, 1, t))),
            (turned, pick(lambda t: number(mine, 1, t ^ 1)), pick(lambda t: number(pay, 0, t ^ 1))),
        ]
        for block, to, at in pairs:
            for i, line in enumerate(blocks):
                for j in range(len(line)):
                    line[j] = line[j] + jnp.where((to == i) & (at == j), block, 0.0)
    return jnp.concatenate([jnp.concatenate(line, axis=1) for line in blocks], axis=0)


def base_kernel(field, own, pair, mate, low, high, image, coup):
    coup[...] = pair[...] + jnp.concatenate([low[...].T, high[...].T], axis=0)
    image[...] = dot(own[...], field[...]) + dot(coup[...], mate[...])


def back_kernel(takes, mine, field, border, *refs):
    count = len(takes)
    *pays, pay = refs[: count + 1]
    coup, back, out, other, *coups = refs[count + 1 :]
    width = field.shape[0]
    toward = mine[pl.ds(mine.shape[0] - TAIL + 2, 1), pl.ds(0, 1)]
    coup[...] = edge(0, width, mine, pay, border)
    for take, gy_pay, gy_coup in zip(takes, pays, coups):
        gy_coup[...] = edge(toward if take is None else take, width, mine, gy_pay, border)
    back[...] = dot(coup[...].T, field[...])
    out[pl.ds(0, width), :] = columns(back, toward, True)
    other[pl.ds(0, width), :] = columns(back, toward, False)


def left_kernel(part, coup, there, image, once):
    term = dot(coup[...], there[...])
    image[...] = part[...] + term
    once[...] = part[...] + 2.0 * term


def turn(mine, width):
    toward = mine[pl.ds(mine.shape[0] - TAIL + 2, 1), pl.ds(0, 1)]
    count = mine.shape[1]
    first = jnp.where(lax.broadcasted_iota(jnp.int32, (1, count), 1) < count // 2, 1.0, 0.0)
    return jnp.where(toward == 3.0, first, 1.0 - first)


def gy_kernel(take, weight, mine, part, single, coup, there, image, once):
    term = dot(coup[...], there[...])
    image[...] = part[...] + term
    once[...] = single[...] + (weight * turn(mine, part.shape[0]) if take is None else weight) * term


def columns(ref, toward, out):
    middle = ref.shape[1] // 2
    return jnp.where((toward == 3.0) == out, ref[:, middle:], ref[:, :middle])


def right_kernel(mine, part, out, half, across):
    width = part.shape[0]
    toward = mine[pl.ds(mine.shape[0] - TAIL + 2, 1), pl.ds(0, 1)]
    half[...] = columns(part, toward, True) + out[pl.ds(0, width), :]
    across[pl.ds(0, width), :] = half[...]
    across[pl.ds(width, EXTRA), :] = jnp.zeros((EXTRA, half.shape[1]), F32)


def joined(toward, out, other):
    low = jnp.where(toward == 3.0, other, out)
    high = jnp.where(toward == 3.0, out, other)
    return jnp.concatenate([low, high], axis=1)


def whole_kernel(mine, part, half, rest, image, other):
    toward = mine[pl.ds(mine.shape[0] - TAIL + 2, 1), pl.ds(0, 1)]
    other[...] = columns(part, toward, False) + rest[pl.ds(0, part.shape[0]), :]
    image[...] = joined(toward, half[...], other[...])


def near_kernel(mine, field, image, once, mate, mate_out, mate_other, own, coup, there, back, part, lift, state):
    b = field[...]
    toward = mine[pl.ds(mine.shape[0] - TAIL + 2, 1), pl.ds(0, 1)]
    mate_w = joined(toward, mate_out[...], mate_other[...])
    norm = col_sum(b, b)
    c = jnp.where(norm > 0.0, col_sum(b, image[...]) / jnp.where(norm > 0.0, norm, 1.0), 0.0)
    g = image[...] - c * b
    part[...] = dot(own[...], g) + dot(coup[...], mate_w - c * mate[...])
    lift[...] = back[...] - c * there[...]
    rows = [(0, norm), (1, c), (2, col_sum(g, g)), (4, -col_sum(g, once[...])), (5, col_sum(b, once[...]))]
    state[...] = stack_rows(rows, state.shape)


def far_kernel(take, field, image, part, near, lift, coup, left, *refs):
    *sides, state = refs
    width = field.shape[0]
    b = field[...]
    c = near[1:2, :]
    acc = part[...] + 2.0 * dot(coup[...], left[...] + lift[...])
    if sides:
        mine, coup_gy, there, side = sides
        if take is None:
            toward = mine[pl.ds(mine.shape[0] - TAIL + 2, 1), pl.ds(0, 1)]
            middle = b.shape[1] // 2
            shift = c * there[...]
            term = dot(coup_gy[...], side[pl.ds(0, width), :] - jnp.where(toward == 3.0, shift[:, :middle], shift[:, middle:]))
            acc += 2.0 * turn(mine, width) * jnp.concatenate([term, term], axis=1)
        else:
            acc += 2.0 * dot(coup_gy[...], side[...] - c * there[...])
    state[...] = near[...] + stack_rows([(3, col_sum(image[...] - c * b, acc)), (4, -col_sum(b, acc))], state.shape)


def merge_kernel(*refs):
    *states, out = refs
    norm = sum(s[0:1, :] for s in states)
    base = states[0][1:2, :]
    shift = sum(s[0:1, :] * (s[1:2, :] - base) for s in states)
    c = base + jnp.where(norm > 0.0, shift / jnp.where(norm > 0.0, norm, 1.0), 0.0)
    size, flat, slope, bend = (jnp.zeros_like(c) for _ in range(4))
    for s in states:
        d = c - s[1:2, :]
        size += s[2:3, :] + s[0:1, :] * d * d
        flat += s[3:4, :] + (s[4:5, :] + s[5:6, :] * d) * d
        slope += s[4:5, :] + 2.0 * s[5:6, :] * d
        bend += s[5:6, :]
    out[...] = stack_rows(list(enumerate([norm, c, size, flat, slope, bend])), out.shape)


def shards(right_side, node_diag, local_coup, block_cols, border_coup, border_send, border_rows):
    width, ncols = right_side.shape
    nblocks, _, bs, _ = local_coup.shape
    n_gx, n_gy, n_nd = (lax.axis_size(a) for a in AXES)
    assert n_nd == 2 and border_coup.shape[1] == 4 * SIDE
    swap = [(0, 1), (1, 0)]
    right = [(i, (i + 1) % n_gx) for i in range(n_gx)]
    left = [(j, i) for i, j in right]
    up = [(i, i + 1) for i in range(n_gy - 1)]
    down = [(j, i) for i, j in up]
    facing = jnp.where(lax.axis_index("gy") == 0, 3, 2).astype(jnp.int32)
    if n_gy == 2:
        sides = [(swap, None, 2.0)]
    elif n_gy > 2:
        sides = [(up, 2, 2.0), (down, 3, 0.0)]
    else:
        sides = []
    sends = [("gx", right)] + [("gy", perm) for perm, _, _ in sides]
    gives = [1] + [None if t is None else t ^ 1 for _, t, _ in sides]
    toward = jnp.full((1, 4 * SIDE), facing)
    marks = jnp.stack([facing, lax.axis_index("nd").astype(jnp.int32)])
    border = border_coup[0]

    def smem(n):
        return [pl.BlockSpec(memory_space=pltpu.SMEM)] * n

    full, half, longer = (bs + TAIL, ncols), (width, ncols // 2), (width + EXTRA, ncols // 2)

    def pack(gives):
        count = len(gives)
        return pl.pallas_call(
            partial(pack_kernel, gives),
            name="pack",
            in_specs=[pl.BlockSpec(memory_space=pl.ANY)] * 4,
            out_specs=[vmem()] * count,
            out_shape=[pltpu.VMEM(full, F32)] * count,
            scratch_shapes=[
                pltpu.SemaphoreType.DMA((count, SIDE)),
                pltpu.VMEM((3, 1, 4 * SIDE), jnp.int32),
                pltpu.SemaphoreType.DMA((3,)),
                pltpu.VMEM((2 * SIDE, bs, bs), F32),
            ],
            compiler_params=pltpu.CompilerParams(vmem_limit_bytes=LIMIT),
        )(*[pltpu.with_memory_space_constraint(a, pltpu.HBM) for a in (border, border_send, border_rows)], toward)

    packed = pack(gives)
    pays = [lax.ppermute(pay, axis, perm) for pay, (axis, perm) in zip(packed, sends)]
    mine = packed[0]
    fields = [lax.ppermute(right_side, axis, perm) for axis, perm in sends]
    mate = lax.ppermute(right_side, "nd", swap)

    def tabled(kernel, name, tables, shapes, flops=None):
        def run(*args):
            args = list(args[:tables]) + [pltpu.with_memory_space_constraint(a, pltpu.VMEM) for a in args[tables:]]
            return pl.pallas_call(
                kernel,
                name=name,
                in_specs=smem(tables) + [vmem()] * (len(args) - tables),
                out_specs=[vmem()] * len(shapes),
                out_shape=[pltpu.VMEM(shape, F32) for shape in shapes],
                compiler_params=pltpu.CompilerParams(vmem_limit_bytes=LIMIT),
                cost_estimate=flops and pl.CostEstimate(flops=flops, bytes_accessed=1 << 20, transcendentals=0),
            )(*args)

        return run

    field, square = (width, ncols), (width, width)
    own, pair, *pieces = tabled(prep_kernel, "prep", 2, [square] * 2 + [(width, width // 2)] * 2, 1 << 24)(
        block_cols, marks, node_diag.reshape(1, width), local_coup, mine
    )
    mate_pair = [lax.ppermute(piece, "nd", swap) for piece in pieces]

    part, coup = call(base_kernel, "base", [field, square])(right_side, own, pair, mate, *mate_pair)
    kernel = partial(back_kernel, [take for _, take, _ in sides])
    left_coup, back, *to_left = call(kernel, "back", [square, field] + [longer] * 2 + [square] * len(sides))(
        mine, right_side, border, *pays[1:], pays[0]
    )
    to_left, side_coup = to_left[:2], to_left[2:]
    from_right = [lax.ppermute(piece, "gx", left) for piece in to_left]
    part, once = call(left_kernel, "left", [field] * 2)(part, left_coup, fields[0])
    for (_, take, weight), block, there in zip(sides, side_coup, fields[1:]):
        part, once = call(partial(gy_kernel, take, weight), "gy", [field] * 2)(mine, part, once, block, there)
    left_w = lax.ppermute(part, "gx", right)
    half_w, across = call(right_kernel, "right", [half, longer])(mine, part, from_right[0])
    image, other_w = call(whole_kernel, "whole", [field, half])(mine, part, half_w, from_right[1])
    mate_w = [lax.ppermute(w, "nd", swap) for w in (half_w, other_w)]
    part, lift, state = call(near_kernel, "near", [field, field, (TAIL, ncols)])(
        mine, right_side, image, once, mate, *mate_w, own, coup, fields[0], back
    )
    far = []
    take = None
    if sides:
        perm, take, _ = sides[0]
        far = [mine, side_coup[0], fields[1], lax.ppermute(across if take is None else image, "gy", perm)]
    (state,) = call(partial(far_kernel, take), "far", [(TAIL, ncols)])(
        right_side, image, part, state, lift, left_coup, left_w, *far
    )
    state = join(state)
    norm, c, size, form = (row[None] for row in state[:4])
    ratio = size / (c * c * norm)
    last = size / (form - ratio * ratio * c * c * c * norm)
    return ((1.0 + last * c * (1.0 + ratio)) / c) * right_side - (last / c) * image


def solution(mesh):
    blocks = P(("var", "gx", "gy", "nd"))
    tables = P(AXES)
    in_specs = (blocks, blocks, blocks, tables, blocks, tables, tables)
    return jax.shard_map(shards, mesh=mesh, in_specs=in_specs, out_specs=blocks, check_vma=False)
```

```python
from functools import partial

import jax
import jax.numpy as jnp
from jax import lax
from jax.experimental import pallas as pl
from jax.experimental.pallas import tpu as pltpu
from jax.sharding import PartitionSpec as P

F32 = jnp.float32
BF16 = jnp.bfloat16
AXES = ("gx", "gy", "nd")
SIDE = 2
LIMIT = 8 << 20
EXTRA = 8
TAIL = 8


def vmem():
    return pl.BlockSpec(memory_space=pltpu.VMEM)


def call(kernel, name, shapes, scratch=(), flops=None):
    def run(*args):
        args = [pltpu.with_memory_space_constraint(a, pltpu.VMEM) for a in args]
        return pl.pallas_call(
            kernel,
            name=name,
            in_specs=[vmem()] * len(args),
            out_specs=[vmem()] * len(shapes),
            out_shape=[pltpu.VMEM(shape, F32) for shape in shapes],
            scratch_shapes=scratch,
            compiler_params=pltpu.CompilerParams(vmem_limit_bytes=LIMIT),
            cost_estimate=flops and pl.CostEstimate(flops=flops, bytes_accessed=1 << 20, transcendentals=0),
        )(*args)

    return run


def join(state):
    count = lax.axis_size(AXES)
    assert count & (count - 1) == 0
    step = 1
    while step < count:
        masks = [m * step for m in (1, 2, 3) if m * step < count]
        others = [lax.ppermute(state, AXES, [(i, i ^ m) for i in range(count)]) for m in masks]
        (state,) = call(merge_kernel, "merge", [state.shape])(state, *others)
        step *= 4
    return state


def split(a):
    high = a.astype(BF16)
    return high, (a - high.astype(F32)).astype(BF16)


def dot(a, b):
    (ah, al), (bh, bl) = split(a), split(b)
    mul = partial(jnp.dot, preferred_element_type=F32)
    return mul(ah, bh) + (mul(ah, bl) + mul(al, bh))


def col_sum(a, b):
    return jnp.sum(a * b, axis=0, keepdims=True)


def stack_rows(rows, shape):
    line = lax.broadcasted_iota(jnp.int32, shape, 0)
    return sum(jnp.where(line == n, row, 0.0) for n, row in rows)


def pack_kernel(gives, *refs):
    marks, refs = (refs[0], refs[1:]) if gives != [1] else (None, refs)
    border, send, rows, toward, *pays, sems, table, table_sems = refs
    bs = border.shape[1]
    tables = [pltpu.make_async_copy(ref, table.at[n], table_sems.at[n]) for n, ref in enumerate((rows, send, toward))]
    copies = []
    for n, (give, pay) in enumerate(zip(gives, pays)):
        give = marks[0] if give is None else give
        for s in range(SIDE):
            block = pay.at[pl.ds(0, bs), pl.ds(s * bs, bs)]
            copies.append(pltpu.make_async_copy(border.at[give * SIDE + s], block, sems.at[n, s]))
    for copy in tables + copies:
        copy.start()
    for copy in tables:
        copy.wait()
    count = table.shape[2]
    for pay in pays:
        for n in range(3):
            pay[pl.ds(bs + n, 1), pl.ds(0, count)] = table[n].astype(F32)
    for copy in copies:
        copy.wait()


def prep_kernel(cols, marks, diag, local, packed, own, pair):
    nblocks, nonzeros, bs, _ = local.shape
    width = nblocks * bs
    patch_len = 2 * nblocks
    base = marks[1] * nblocks
    own[...] = jnp.zeros((width, width), F32)
    pair[...] = jnp.zeros((width, width), F32)
    for b in range(nblocks):
        for k in range(nonzeros):
            spot = lax.rem(cols[b, k] - base + patch_len, patch_len)
            block = local[b, k]
            for c in range(nblocks):

                @pl.when(spot == c)
                def _():
                    own[pl.ds(b * bs, bs), pl.ds(c * bs, bs)] += block

                @pl.when(spot == c + nblocks)
                def _():
                    pair[pl.ds(b * bs, bs), pl.ds(c * bs, bs)] += block

    lower = own[...]
    here = lax.broadcasted_iota(jnp.int32, (width, width), 0)
    there = lax.broadcasted_iota(jnp.int32, (width, width), 1)
    own[...] = lower + lower.T + jnp.where(here == there, diag[...], 0.0)


def edge(take, width, mine, pay, border):
    bs = border.shape[1]
    known = isinstance(take, int)

    def pick(of):
        return of(take) if known else jnp.where(take == 2.0, of(2), of(3))

    def number(ref, line, t):
        return ref[pl.ds(ref.shape[0] - TAIL + line, 1), pl.ds(t * SIDE + s, 1)]

    blocks = [[0.0] * (width // bs) for _ in range(width // bs)]
    for s in range(SIDE):
        turned = pay[pl.ds(0, bs), pl.ds(s * bs, bs)].T
        pairs = [
            (pick(lambda t: border[t * SIDE + s]), pick(lambda t: number(mine, 0, t)), pick(lambda t: number(pay, 1, t))),
            (turned, pick(lambda t: number(mine, 1, t ^ 1)), pick(lambda t: number(pay, 0, t ^ 1))),
        ]
        for block, to, at in pairs:
            for i, line in enumerate(blocks):
                for j in range(len(line)):
                    line[j] = line[j] + jnp.where((to == i) & (at == j), block, 0.0)
    return jnp.concatenate([jnp.concatenate(line, axis=1) for line in blocks], axis=0)


def base_kernel(field, own, pair, mate, mate_pair, image, coup):
    coup[...] = pair[...] + mate_pair[...].T
    image[...] = dot(own[...], field[...]) + dot(coup[...], mate[...])


def back_kernel(mine, field, border, pay, coup, back, out, other):
    width = field.shape[0]
    toward = mine[pl.ds(mine.shape[0] - TAIL + 2, 1), pl.ds(0, 1)]
    coup[...] = edge(0, width, mine, pay, border)
    back[...] = dot(coup[...].T, field[...])
    out[pl.ds(0, width), :] = columns(back, toward, True)
    other[pl.ds(0, width), :] = columns(back, toward, False)


def left_kernel(part, coup, there, image, once):
    term = dot(coup[...], there[...])
    image[...] = part[...] + term
    once[...] = part[...] + 2.0 * term


def turn(mine, width):
    toward = mine[pl.ds(mine.shape[0] - TAIL + 2, 1), pl.ds(0, 1)]
    count = mine.shape[1]
    first = jnp.where(lax.broadcasted_iota(jnp.int32, (1, count), 1) < count // 2, 1.0, 0.0)
    return jnp.where(toward == 3.0, first, 1.0 - first)


def gy_kernel(take, weight, mine, part, single, border, pay, there, image, once, coup):
    width = coup.shape[0]
    toward = mine[pl.ds(mine.shape[0] - TAIL + 2, 1), pl.ds(0, 1)]
    coup[...] = edge(toward if take is None else take, width, mine, pay, border)
    term = dot(coup[...], there[...])
    image[...] = part[...] + term
    scale = weight * turn(mine, width) if take is None else weight
    once[...] = single[...] + scale * term


def columns(ref, toward, out):
    middle = ref.shape[1] // 2
    return jnp.where((toward == 3.0) == out, ref[:, middle:], ref[:, :middle])


def right_kernel(mine, part, out, half, across):
    width = part.shape[0]
    toward = mine[pl.ds(mine.shape[0] - TAIL + 2, 1), pl.ds(0, 1)]
    half[...] = columns(part, toward, True) + out[pl.ds(0, width), :]
    across[pl.ds(0, width), :] = half[...]
    across[pl.ds(width, EXTRA), :] = jnp.zeros((EXTRA, half.shape[1]), F32)


def joined(toward, out, other):
    low = jnp.where(toward == 3.0, other, out)
    high = jnp.where(toward == 3.0, out, other)
    return jnp.concatenate([low, high], axis=1)


def whole_kernel(mine, part, half, rest, image, other):
    toward = mine[pl.ds(mine.shape[0] - TAIL + 2, 1), pl.ds(0, 1)]
    other[...] = columns(part, toward, False) + rest[pl.ds(0, part.shape[0]), :]
    image[...] = joined(toward, half[...], other[...])


def near_kernel(mine, field, image, once, mate, mate_out, mate_other, own, coup, there, back, part, lift, state):
    b = field[...]
    toward = mine[pl.ds(mine.shape[0] - TAIL + 2, 1), pl.ds(0, 1)]
    mate_w = joined(toward, mate_out[...], mate_other[...])
    norm = col_sum(b, b)
    c = jnp.where(norm > 0.0, col_sum(b, image[...]) / jnp.where(norm > 0.0, norm, 1.0), 0.0)
    g = image[...] - c * b
    part[...] = dot(own[...], g) + dot(coup[...], mate_w - c * mate[...])
    lift[...] = back[...] - c * there[...]
    rows = [(0, norm), (1, c), (2, col_sum(g, g)), (4, -col_sum(g, once[...])), (5, col_sum(b, once[...]))]
    state[...] = stack_rows(rows, state.shape)


def far_kernel(take, field, image, part, near, lift, coup, left, *refs):
    *sides, state = refs
    width = field.shape[0]
    b = field[...]
    c = near[1:2, :]
    acc = part[...] + 2.0 * dot(coup[...], left[...] + lift[...])
    if sides:
        mine, coup_gy, there, side = sides
        if take is None:
            toward = mine[pl.ds(mine.shape[0] - TAIL + 2, 1), pl.ds(0, 1)]
            middle = b.shape[1] // 2
            shift = c * there[...]
            term = dot(coup_gy[...], side[pl.ds(0, width), :] - jnp.where(toward == 3.0, shift[:, :middle], shift[:, middle:]))
            acc += 2.0 * turn(mine, width) * jnp.concatenate([term, term], axis=1)
        else:
            acc += 2.0 * dot(coup_gy[...], side[...] - c * there[...])
    state[...] = near[...] + stack_rows([(3, col_sum(image[...] - c * b, acc)), (4, -col_sum(b, acc))], state.shape)


def merge_kernel(*refs):
    *states, out = refs
    norm = sum(s[0:1, :] for s in states)
    base = states[0][1:2, :]
    shift = sum(s[0:1, :] * (s[1:2, :] - base) for s in states)
    c = base + jnp.where(norm > 0.0, shift / jnp.where(norm > 0.0, norm, 1.0), 0.0)
    size, flat, slope, bend = (jnp.zeros_like(c) for _ in range(4))
    for s in states:
        d = c - s[1:2, :]
        size += s[2:3, :] + s[0:1, :] * d * d
        flat += s[3:4, :] + (s[4:5, :] + s[5:6, :] * d) * d
        slope += s[4:5, :] + 2.0 * s[5:6, :] * d
        bend += s[5:6, :]
    out[...] = stack_rows(list(enumerate([norm, c, size, flat, slope, bend])), out.shape)


def shards(right_side, node_diag, local_coup, block_cols, border_coup, border_send, border_rows):
    width, ncols = right_side.shape
    nblocks, _, bs, _ = local_coup.shape
    n_gx, n_gy, n_nd = (lax.axis_size(a) for a in AXES)
    assert n_nd == 2 and border_coup.shape[1] == 4 * SIDE
    swap = [(0, 1), (1, 0)]
    right = [(i, (i + 1) % n_gx) for i in range(n_gx)]
    left = [(j, i) for i, j in right]
    up = [(i, i + 1) for i in range(n_gy - 1)]
    down = [(j, i) for i, j in up]
    facing = jnp.where(lax.axis_index("gy") == 0, 3, 2).astype(jnp.int32)
    if n_gy == 2:
        sides = [(swap, None, 2.0)]
    elif n_gy > 2:
        sides = [(up, 2, 2.0), (down, 3, 0.0)]
    else:
        sides = []
    sends = [("gx", right)] + [("gy", perm) for perm, _, _ in sides]
    gives = [1] + [None if t is None else t ^ 1 for _, t, _ in sides]
    toward = jnp.full((1, 4 * SIDE), facing)
    marks = jnp.stack([facing, lax.axis_index("nd").astype(jnp.int32)])
    border = border_coup[0]

    def smem(n):
        return [pl.BlockSpec(memory_space=pltpu.SMEM)] * n

    full, half, longer = (bs + TAIL, ncols), (width, ncols // 2), (width + EXTRA, ncols // 2)

    def pack(gives):
        count = len(gives)
        tables = [marks] if gives != [1] else []
        return pl.pallas_call(
            partial(pack_kernel, gives),
            name="pack",
            in_specs=smem(len(tables)) + [pl.BlockSpec(memory_space=pl.ANY)] * 4,
            out_specs=[vmem()] * count,
            out_shape=[pltpu.VMEM(full, F32)] * count,
            scratch_shapes=[
                pltpu.SemaphoreType.DMA((count, SIDE)),
                pltpu.VMEM((3, 1, 4 * SIDE), jnp.int32),
                pltpu.SemaphoreType.DMA((3,)),
            ],
            compiler_params=pltpu.CompilerParams(vmem_limit_bytes=LIMIT),
        )(*tables, *[pltpu.with_memory_space_constraint(a, pltpu.HBM) for a in (border, border_send, border_rows)], toward)

    packed = pack(gives)
    pays = [lax.ppermute(pay, axis, perm) for pay, (axis, perm) in zip(packed, sends)]
    mine = packed[0]
    fields = [lax.ppermute(right_side, axis, perm) for axis, perm in sends]
    mate = lax.ppermute(right_side, "nd", swap)

    def tabled(kernel, name, tables, shapes, flops=None):
        def run(*args):
            args = list(args[:tables]) + [pltpu.with_memory_space_constraint(a, pltpu.VMEM) for a in args[tables:]]
            return pl.pallas_call(
                kernel,
                name=name,
                in_specs=smem(tables) + [vmem()] * (len(args) - tables),
                out_specs=[vmem()] * len(shapes),
                out_shape=[pltpu.VMEM(shape, F32) for shape in shapes],
                compiler_params=pltpu.CompilerParams(vmem_limit_bytes=LIMIT),
                cost_estimate=flops and pl.CostEstimate(flops=flops, bytes_accessed=1 << 20, transcendentals=0),
            )(*args)

        return run

    field, square = (width, ncols), (width, width)
    own, pair = tabled(prep_kernel, "prep", 2, [square] * 2, 1 << 24)(
        block_cols, marks, node_diag.reshape(1, width), local_coup, mine
    )
    mate_pair = lax.ppermute(pair, "nd", swap)

    part, coup = call(base_kernel, "base", [field, square])(right_side, own, pair, mate, mate_pair)
    left_coup, back, *to_left = call(back_kernel, "back", [square, field] + [longer] * 2)(mine, right_side, border, pays[0])
    from_right = [lax.ppermute(piece, "gx", left) for piece in to_left]
    part, once = call(left_kernel, "left", [field] * 2)(part, left_coup, fields[0])
    side_coup = []
    for (_, take, weight), pay, there in zip(sides, pays[1:], fields[1:]):
        part, once, block = call(partial(gy_kernel, take, weight), "gy", [field, field, square])(mine, part, once, border, pay, there)
        side_coup.append(block)
    left_w = lax.ppermute(part, "gx", right)
    half_w, across = call(right_kernel, "right", [half, longer])(mine, part, from_right[0])
    image, other_w = call(whole_kernel, "whole", [field, half])(mine, part, half_w, from_right[1])
    mate_w = [lax.ppermute(w, "nd", swap) for w in (half_w, other_w)]
    part, lift, state = call(near_kernel, "near", [field, field, (TAIL, ncols)])(
        mine, right_side, image, once, mate, *mate_w, own, coup, fields[0], back
    )
    far = []
    take = None
    if sides:
        perm, take, _ = sides[0]
        far = [mine, side_coup[0], fields[1], lax.ppermute(across if take is None else image, "gy", perm)]
    (state,) = call(partial(far_kernel, take), "far", [(TAIL, ncols)])(
        right_side, image, part, state, lift, left_coup, left_w, *far
    )
    state = join(state)
    norm, c, size, form = (row[None] for row in state[:4])
    ratio = size / (c * c * norm)
    last = size / (form - ratio * ratio * c * c * c * norm)
    return ((1.0 + last * c * (1.0 + ratio)) / c) * right_side - (last / c) * image


def solution(mesh):
    blocks = P(("var", "gx", "gy", "nd"))
    tables = P(AXES)
    in_specs = (blocks, blocks, blocks, tables, blocks, tables, tables)
    return jax.shard_map(shards, mesh=mesh, in_specs=in_specs, out_specs=blocks, check_vma=False)
```
